32 devices in a mesh: gx: 8 (over z, y), gy: 4 (over x, core).
Axes of the slice: x: 2, y: 2, z: 4, core: 2. Of those that a mesh axis runs over, the one named last changes fastest.
Arguments:
- state_in: float32 [5, 16, 32, 32, 128], P(None, None, 'gx', 'gy'), may hold values from -6 to 6
- sponge: float32 [32, 32, 128], P('gx', 'gy'), may hold values from 0.05 to 0.5
- mean_velocity: float32 [3], replicated, may hold values from -0.6 to 0.6
- wall_vector: float32 [5], replicated, may hold values from -3 to 3
- mode_shapes: float32 [16, 8192], P(None, ('gx', 'gy')), may hold values from -6 to 6
- wall_nodes: int32 [4, 32, 128], P(None, 'gx'), may hold values from 0 to 8191
- wall_weights: float32 [4, 32, 128], P(None, 'gx'), may hold values from 0.1 to 1
- wall_count: int32 [32], P('gx'), may hold values from 32 to 128
Outputs:
- state_out: float32 [5, 16, 32, 32, 128], P(None, None, 'gx', 'gy')
- r_factor: float32 [32, 32], replicated
The draws below stay inside these ranges and needn't reach their ends.
All inputs are finite; a program needn't handle non-finite values.
Results may differ from the reference program's by a relative error of at most 0.00013.
Values sent between devices are 32-bit elements; how exact they have to be, the bound alone decides.
No kernel may reach another device: no remote copies, remote signals or barrier semaphores. Data moves between devices by JAX's collectives and lax.ppermute only.
A program may use at most 192 MiB of HBM per device.

```python
import math
import jax
import jax.numpy as jnp
import numpy as np
from jax import lax

MODES = 16
STEPS = 2
NODES_PER_CELL = 4
NZ = 128
NX = 32
NY = 32
NODES = 8192


def plant(drawn, own_key, least, top_value):
    longest = drawn.shape.index(max(drawn.shape))
    spots = []
    for shift in (0, 1):
        where = [jax.random.randint(jax.random.fold_in(own_key, axis), (), 0, length) for axis, length in enumerate(drawn.shape)]
        where[longest] = (where[longest] + shift) % drawn.shape[longest]
        spots.append(tuple(where))
    return drawn.at[spots[0]].set(least).at[spots[1]].set(top_value)


def shard_levels(stream_key, shape, shards, low, top_value):
    gain = 1.0
    for position, parts in shards:
        draws = jax.random.uniform(jax.random.fold_in(jax.random.fold_in(stream_key, 6), position), (parts,), jnp.float32, low / len(shards), top_value / len(shards))
        gain = gain * jnp.repeat(jnp.exp(draws), shape[position] // parts).reshape((-1,) + (1,) * (len(shape) - 1 - position))
    return gain


def noise(key, extent, spread, limit, pieces=(), kind=jnp.bfloat16):
    entries = spread * jax.random.normal(key, extent, jnp.float32)
    if pieces:
        entries = entries * shard_levels(key, extent, pieces, -0.22, 0.18)
    return jnp.clip(entries, -limit, limit).astype(kind)


def setup_inputs(seed: int = 0) -> dict:
    streams_of = jax.random.split(jax.random.key(seed), 9)
    state_in = noise(streams_of[0], (5, MODES, NX, NY, NZ), 1.0, 6.0, ((2, 8), (3, 4)), jnp.float32)
    sponge = jnp.clip(jnp.exp(math.log(0.5) - 2.3025851 * jax.random.uniform(streams_of[1], (NX, NY, NZ), jnp.float32) ** shard_levels(streams_of[1], (NX, NY, NZ), ((0, 8), (1, 4)), -0.2, 0.2)), 0.05, 0.5)
    mean_velocity = jnp.clip(jax.random.uniform(streams_of[2], (3,), jnp.float32, -0.6, 0.6), -0.6, 0.6)
    wall_vector = noise(streams_of[3], (5,), 1.0, 3.0, (), jnp.float32)
    mode_shapes = noise(streams_of[4], (MODES, NODES), 1.0, 6.0, ((1, 32),), jnp.float32)
    wall_nodes = plant(jax.random.randint(streams_of[5], (NODES_PER_CELL, NX, NZ), 0, NODES), jax.random.fold_in(streams_of[5], 1), 0, NODES - 1).astype(jnp.int32)
    wall_weights = jnp.clip(0.1 + 0.9 * jax.random.uniform(streams_of[6], (NODES_PER_CELL, NX, NZ), jnp.float32) ** shard_levels(streams_of[6], (NODES_PER_CELL, NX, NZ), ((1, 8),), -0.2, 0.2), 0.1, 1.0)
    wall_count = plant(jax.random.randint(streams_of[7], (NX,), NZ // 4, NZ + 1), jax.random.fold_in(streams_of[7], 1), NZ // 4, NZ).astype(jnp.int32)
    return {"state_in": state_in, "sponge": sponge, "mean_velocity": mean_velocity, "wall_vector": wall_vector, "mode_shapes": mode_shapes, "wall_nodes": wall_nodes, "wall_weights": wall_weights, "wall_count": wall_count}


C_SOUND = 1.0
NU_DAMP = 0.25
DT_STEP = 0.4
PULSE_MID = 0.8
PULSE_WIDTH = 0.5

def pulse(time_now):
    return math.exp(-((time_now - PULSE_MID) / PULSE_WIDTH) ** 2)

def jacobians(velocity):
    identity = jnp.eye(5, dtype=velocity.dtype)
    matrices = []
    for dimension in range(3):
        coupling = np.zeros((5, 5))
        coupling[0, 1 + dimension] = 1.0
        coupling[1 + dimension, 4] = 1.0
        coupling[4, 1 + dimension] = C_SOUND * C_SOUND
        matrices.append(velocity[dimension] * identity + jnp.asarray(coupling, velocity.dtype))
    return jnp.stack(matrices)

def rates(padded, jacobian, sponge, wall_rows, wall_line):
    highest = lax.Precision.HIGHEST
    center = padded[:, 1:-1, 1:-1, :]
    east_side = padded[:, 2:, 1:-1, :]
    west_side = padded[:, :-2, 1:-1, :]
    north_side = padded[:, 1:-1, 2:, :]
    south_side = padded[:, 1:-1, :-2, :]
    zero_plane = jnp.zeros_like(center[..., :1])
    upper_side = jnp.concatenate([center[..., 1:], zero_plane], axis=3)
    lower_side = jnp.concatenate([zero_plane, center[..., :-1]], axis=3)
    flux_sum = jnp.einsum('fg,gxyz->fxyz', jacobian[0], east_side - west_side, precision=highest) + jnp.einsum('fg,gxyz->fxyz', jacobian[1], north_side - south_side, precision=highest) + jnp.einsum('fg,gxyz->fxyz', jacobian[2], upper_side - lower_side, precision=highest)
    source = wall_rows[:, :, None, :] * wall_line[None, None, :, None]
    neighbours = east_side + west_side + north_side + south_side + upper_side + lower_side
    return -0.5 * flux_sum + NU_DAMP * (neighbours - 6.0 * center) - sponge[None] * center + source

def respond(state, forcing_mode, jacobian, sponge, wall_vector):
    wall_rows = wall_vector[:, None, None] * forcing_mode[None]
    wall_base = (jnp.arange(NY) == 0).astype(state.dtype)

    def section_rate(field_state, time_now):
        padded = jnp.pad(field_state, ((0, 0), (1, 1), (1, 1), (0, 0)))
        return rates(padded, jacobian, sponge, wall_rows, wall_base * pulse(time_now))
    snapshots = []
    for step in range(STEPS):
        time_now = step * DT_STEP
        rate_one = section_rate(state, time_now)
        rate_two = section_rate(state + 0.5 * DT_STEP * rate_one, time_now + 0.5 * DT_STEP)
        rate_three = section_rate(state + 0.5 * DT_STEP * rate_two, time_now + 0.5 * DT_STEP)
        rate_four = section_rate(state + DT_STEP * rate_three, time_now + DT_STEP)
        state = state + DT_STEP / 6.0 * (rate_one + 2.0 * rate_two + 2.0 * rate_three + rate_four)
        snapshots.append(state)
    return (state, jnp.stack(snapshots))

def reference(state_in, sponge, mean_velocity, wall_vector, mode_shapes, wall_nodes, wall_weights, wall_count):
    jacobian = jacobians(mean_velocity)
    values_taken = mode_shapes[:, wall_nodes]
    forcing = jnp.sum(wall_weights[None] * values_taken, axis=1)
    wall_mask = (jnp.arange(NZ)[None, :] < wall_count[:, None]).astype(forcing.dtype)
    forcing = forcing * wall_mask[None]

    def one_mode(inputs):
        return respond(inputs[0], inputs[1], jacobian, sponge, wall_vector)
    finals, snapshots = lax.map(one_mode, (jnp.transpose(state_in, (1, 0, 2, 3, 4)), forcing))
    state_out = jnp.transpose(finals, (1, 0, 2, 3, 4))
    columns = jnp.transpose(snapshots, (1, 0, 2, 3, 4, 5)).reshape(STEPS * MODES, -1)
    gram_matrix = jnp.dot(columns.astype(jnp.float32), columns.T.astype(jnp.float32), precision=lax.Precision.HIGHEST, preferred_element_type=jnp.float32) / (5.0 * NX * NY * NZ)
    return (state_out, jnp.linalg.cholesky(gram_matrix).T)
```

```python
import functools
import math

import jax
import jax.numpy as jnp
from jax import lax
from jax.experimental import pallas as pl
from jax.experimental.pallas import tpu as pltpu
from jax.sharding import PartitionSpec as P

STEPS = 2
NU_DAMP = 0.25
DT_STEP = 0.4
PULSE_MID = 0.8
PULSE_WIDTH = 0.5

AXES = ("gx", "gy")
FIELDS = 5
DEEP = 4
MEMBERS = 8
ROWS = 8
LANES = 128
TABLE = FIELDS * 2 * DEEP
F32 = jnp.float32

VMEM = pl.BlockSpec(memory_space=pltpu.VMEM)
SMEM = pl.BlockSpec(memory_space=pltpu.SMEM)
PARAMS = pltpu.CompilerParams(vmem_limit_bytes=48 * 1024 * 1024)


def pulse(time_now):
    return math.exp(-(((time_now - PULSE_MID) / PULSE_WIDTH) ** 2))


def step_scales(step):
    start = step * DT_STEP
    p0, ph, p1 = pulse(start), pulse(start + 0.5 * DT_STEP), pulse(start + DT_STEP)
    return (
        (DT_STEP / 4.0, p0),
        (DT_STEP / 3.0, (p0 + ph) / 2.0),
        (DT_STEP / 2.0, (p0 + 2.0 * ph) / 3.0),
        (DT_STEP, (p0 + 4.0 * ph + p1) / 6.0),
    )


def position():
    along_x = lax.axis_index("gx")
    return along_x // 2, (along_x % 2) * 4 + lax.axis_index("gy")


def pack_kernel(state_ref, sponge_ref, nodes_ref, weights_ref, count_ref, *pieces):
    _, member = position()
    row = member % 4
    lane = lax.broadcasted_iota(jnp.int32, (1, LANES), 1)
    table = [nodes_ref[row].astype(F32)]
    for x in range(DEEP):
        kept = jnp.where(lane < count_ref[x], 1.0, 0.0)
        table.append(weights_ref[row, pl.ds(x, 1), :] * kept)
    table = jnp.concatenate(table, axis=0)
    for d, piece in enumerate(pieces):
        other = member ^ d
        for f in range(FIELDS):
            for j in range(2):
                for x in range(DEEP):
                    piece[(f * 2 + j) * DEEP + x] = state_ref[f, 2 * other + j, x]
        piece[TABLE] = table
        for x in range(DEEP):
            piece[TABLE + 1 + x] = sponge_ref[x]


def pack(state_in, sponge, nodes, weights, count):
    shape = jax.ShapeDtypeStruct((TABLE + 1 + DEEP, ROWS, LANES), F32)
    return pl.pallas_call(
        pack_kernel,
        out_shape=[shape] * MEMBERS,
        in_specs=[VMEM, VMEM, VMEM, VMEM, SMEM],
        out_specs=[VMEM] * MEMBERS,
        compiler_params=PARAMS,
        name="pack",
    )(state_in, sponge, nodes, weights, count)


def shifted_rows(tiles, sub):
    ahead = [pltpu.roll(t, ROWS - 1, 0) for t in tiles]
    behind = [pltpu.roll(t, 1, 0) for t in tiles]
    zero = jnp.zeros_like(tiles[0])
    last, first = sub == ROWS - 1, sub == 0
    count = len(tiles)
    north = [jnp.where(last, ahead[t + 1] if t + 1 < count else zero, ahead[t]) for t in range(count)]
    south = [jnp.where(first, behind[t - 1] if t > 0 else zero, behind[t]) for t in range(count)]
    return north, south


def run_stage(src, base, dst, shift, sponge_ref, wall_ref, vel, wall_vec, h, scale, low, high):
    lane = lax.broadcasted_iota(jnp.int32, (ROWS, LANES), 1)
    sub = lax.broadcasted_iota(jnp.int32, (ROWS, LANES), 0)
    plus = [h * (NU_DAMP - 0.5 * v) for v in vel]
    minus = [h * (NU_DAMP + 0.5 * v) for v in vel]
    not_top, not_low = lane < LANES - 1, lane > 0
    plus_z = jnp.where(not_top, plus[2], 0.0)
    minus_z = jnp.where(not_low, minus[2], 0.0)
    flux = -0.5 * h
    flux_up = jnp.where(not_top, flux, 0.0)
    flux_low = jnp.where(not_low, flux, 0.0)
    tiles = range(4)

    def plane(i, carry):
        damp = [-h * (6.0 * NU_DAMP + sponge_ref[i, pl.ds(ROWS * t, ROWS), :]) for t in tiles]
        for j in range(2):
            def load(ref, f, at):
                return [ref[f, j, at, pl.ds(ROWS * t, ROWS), :] for t in tiles]

            new, d1, d2, d3, d4 = [], None, None, None, None
            for f in range(FIELDS):
                center = load(src, f, i)
                east, west = load(src, f, i + 1), load(src, f, i - 1)
                north, south = shifted_rows(center, sub)
                upper = [pltpu.roll(c, LANES - 1, 1) for c in center]
                lower = [pltpu.roll(c, 1, 1) for c in center]
                old = load(base, f, i)
                out = []
                for t in tiles:
                    acc = old[t] + damp[t] * center[t]
                    acc += plus[0] * east[t] + minus[0] * west[t]
                    acc += plus[1] * north[t] + minus[1] * south[t]
                    acc += plus_z * upper[t] + minus_z * lower[t]
                    if t == 0:
                        acc += (h * scale * wall_vec[f]) * wall_ref[j, i]
                    out.append(acc)
                new.append(out)
                if f == 1:
                    d1 = [flux * (east[t] - west[t]) for t in tiles]
                elif f == 2:
                    d2 = [flux * (north[t] - south[t]) for t in tiles]
                elif f == 3:
                    d3 = [flux_up * upper[t] - flux_low * lower[t] for t in tiles]
                elif f == 4:
                    d4 = [
                        (
                            flux * (east[t] - west[t]),
                            flux * (north[t] - south[t]),
                            flux_up * upper[t] - flux_low * lower[t],
                        )
                        for t in tiles
                    ]
            for t in tiles:
                spread = d1[t] + d2[t] + d3[t]
                new[0][t] += spread
                new[4][t] += spread
                for d in range(3):
                    new[1 + d][t] += d4[t][d]
            for f in range(FIELDS):
                for t in tiles:
                    dst[f, j, i - shift, pl.ds(ROWS * t, ROWS), :] = new[f][t]
        return carry

    lax.fori_loop(low, high, plane, 0)


def run_step(step, base, va, vb, q_low, q_high, sponge_ref, wall_ref, vel, wall_vec, has_low, has_high):
    zero = jnp.zeros((ROWS, LANES), F32)
    for buffer in (va, vb):
        for f in range(FIELDS):
            for j in range(2):
                for t in range(4):
                    buffer[f, j, DEEP - 1, pl.ds(ROWS * t, ROWS), :] = zero
                    buffer[f, j, 3 * DEEP, pl.ds(ROWS * t, ROWS), :] = zero
    scales = step_scales(step)
    src = base
    for k in range(4):
        h, scale = scales[k]
        args = (sponge_ref, wall_ref, vel, wall_vec, h, scale)
        if k < 3:
            dst = va if k % 2 == 0 else vb
            low = jnp.where(has_low, k + 1, DEEP)
            high = jnp.where(has_high, 4 * DEEP - 1 - k, 3 * DEEP)
            run_stage(src, base, dst, 0, *args, low, high)
            src = dst
        else:
            run_stage(src, base, q_low, DEEP, *args, DEEP, 2 * DEEP)
            run_stage(src, base, q_high, 2 * DEEP, *args, 2 * DEEP, 3 * DEEP)


def write_pieces(q_low, q_high, pieces, member):
    for d, piece in enumerate(pieces):
        other = member ^ d
        row = pl.multiple_of((other % 4) * ROWS, ROWS)

        def copy(source):
            for f in range(FIELDS):
                for j in range(2):
                    for x in range(DEEP):
                        piece[j, f, x] = source[f, j, x, pl.ds(row, ROWS), :]

        @pl.when(other < 4)
        def _():
            copy(q_low)

        @pl.when(other >= 4)
        def _():
            copy(q_high)


def gather_forcing(tables, shapes_ref, wall_ref):
    low_part, high_part, weights = [], [], []
    for table in tables:
        low_part.append(table[0] & (LANES - 1))
        high_part.append(table[0] // LANES)
        weights.append(table[1])
    count = len(tables)
    rows = shapes_ref.shape[1]

    def body(r, taken):
        out = [list(taken[j]) for j in range(2)]
        for j in range(2):
            line = jnp.broadcast_to(shapes_ref[j, pl.ds(r, 1), :], (ROWS, LANES))
            for b in range(count):
                value = jnp.take_along_axis(line, low_part[b], axis=1)
                out[j][b] = jnp.where(high_part[b] == r, value, taken[j][b])
        return tuple(tuple(o) for o in out)

    zero = jnp.zeros((ROWS, LANES), F32)
    taken = lax.fori_loop(0, rows, body, tuple(tuple(zero for _ in range(count)) for _ in range(2)))
    return [[taken[j][b] * weights[b] for b in range(count)] for j in range(2)]


def first_kernel(groups, vel_ref, vec_ref, shapes_ref, *refs):
    own, halo = refs[:MEMBERS], refs[MEMBERS : 2 * MEMBERS]
    q_low, q_high, wall_ref, sponge_ref = refs[2 * MEMBERS : 2 * MEMBERS + 4]
    pieces = refs[2 * MEMBERS + 4 : 3 * MEMBERS + 4]
    base, va, vb, tab = refs[3 * MEMBERS + 4 :]
    group, member = position()
    for d in range(MEMBERS):
        other = member ^ d
        row = pl.multiple_of((other % 4) * ROWS, ROWS)
        upper = other // 4
        for piece, start in ((own[d], DEEP + DEEP * upper), (halo[d], 3 * DEEP * (1 - upper))):
            for f in range(FIELDS):
                for j in range(2):
                    for x in range(DEEP):
                        base[f, j, start + x, pl.ds(row, ROWS), :] = piece[(f * 2 + j) * DEEP + x]
            for x in range(DEEP):
                sponge_ref[start + x, pl.ds(row, ROWS), :] = piece[TABLE + 1 + x]
            tab[other % 4, start // DEEP] = piece[TABLE]
    tables = []
    for block in range(4):
        for half in range(2):
            two = [tab[2 * half + n, block] for n in range(2)]
            index = jnp.concatenate([two[0][:DEEP], two[1][:DEEP]], axis=0).astype(jnp.int32)
            weight = jnp.concatenate([two[0][DEEP:], two[1][DEEP:]], axis=0)
            tables.append((index, weight))
    forced = gather_forcing(tables, shapes_ref, wall_ref)
    sub = lax.broadcasted_iota(jnp.int32, (ROWS, LANES), 0)
    for j in range(2):
        for block in range(4):
            total = forced[j][2 * block] + forced[j][2 * block + 1]
            total = total[:DEEP] + total[DEEP:]
            for x in range(DEEP):
                line = jnp.broadcast_to(total[x : x + 1], (ROWS, LANES))
                wall_ref[j, DEEP * block + x] = jnp.where(sub == 0, line, 0.0)
    vel = [vel_ref[d] for d in range(3)]
    vec = [vec_ref[f] for f in range(FIELDS)]
    run_step(0, base, va, vb, q_low, q_high, sponge_ref, wall_ref, vel, vec, group > 0, group < groups - 1)
    write_pieces(q_low, q_high, pieces, member)


def second_kernel(groups, vel_ref, vec_ref, sponge_ref, wall_ref, below, q_low, q_high, above, *refs):
    pieces = refs[:MEMBERS]
    r_low, r_high, base, va, vb = refs[MEMBERS:]
    group, member = position()
    for n, source in enumerate((below, q_low, q_high, above)):
        for f in range(FIELDS):
            for j in range(2):
                for x in range(DEEP):
                    for t in range(4):
                        rows = pl.ds(ROWS * t, ROWS)
                        base[f, j, DEEP * n + x, rows, :] = source[f, j, x, rows, :]
    vel = [vel_ref[d] for d in range(3)]
    vec = [vec_ref[f] for f in range(FIELDS)]
    run_step(1, base, va, vb, r_low, r_high, sponge_ref, wall_ref, vel, vec, group > 0, group < groups - 1)
    write_pieces(r_low, r_high, pieces, member)


def gram_kernel(total, *refs):
    parts = (refs[:MEMBERS], refs[MEMBERS : 2 * MEMBERS])
    state_ref, gram_ref, columns = refs[2 * MEMBERS :]
    _, member = position()
    tiles = FIELDS * DEEP
    for d in range(MEMBERS):
        other = member ^ d
        for n in range(STEPS):
            for j in range(2):
                for f in range(FIELDS):
                    for x in range(DEEP):
                        value = parts[n][d][j, f, x]
                        start = pl.multiple_of(
                            (n * 2 * MEMBERS + 2 * other + j) * tiles * ROWS, ROWS
                        ) + (f * DEEP + x) * ROWS
                        columns[pl.ds(pl.multiple_of(start, ROWS), ROWS), :] = value
                        if n == STEPS - 1:
                            state_ref[f, 2 * other + j, x] = value
    size = STEPS * 2 * MEMBERS
    stride = tiles * ROWS

    def body(r, acc):
        a = jnp.concatenate(
            [columns[pl.ds(4 * r + n, size, stride=stride), :] for n in range(4)], axis=1
        )
        return acc + lax.dot_general(
            a, a, (((1,), (1,)), ((), ())),
            precision=lax.Precision.HIGHEST, preferred_element_type=F32,
        )

    gram = lax.fori_loop(0, stride // 4, body, jnp.zeros((size, size), F32), unroll=4)
    tile = jnp.concatenate([gram[ROWS * n : ROWS * n + ROWS] for n in range(4)], axis=1)
    for n in range(gram_ref.shape[0]):
        gram_ref[n] = tile


def sum_kernel(total, parts_ref, gram_ref):
    acc = parts_ref[0]
    for n in range(1, parts_ref.shape[0]):
        acc = acc + parts_ref[n]
    acc = acc / total
    for n in range(4):
        gram_ref[pl.ds(ROWS * n, ROWS), :] = acc[:, 32 * n : 32 * n + 32]


def local(state_in, sponge, mean_velocity, wall_vector, mode_shapes, wall_nodes, wall_weights, wall_count):
    gx_size, gy_size = lax.axis_size("gx"), lax.axis_size("gy")
    groups = gx_size // 2
    devices = gx_size * gy_size
    cells_x, cells_y, cells_z = state_in.shape[2:]
    def inside(d):
        return [(i, i ^ d) for i in range(devices)]

    def across(d):
        moves = []
        for i in range(devices):
            g, m = divmod(i, MEMBERS)
            target = g + 1 if m >= 4 else g - 1
            if 0 <= target < groups:
                moves.append((i, target * MEMBERS + (m ^ d)))
        return moves

    up = [(i, i + MEMBERS) for i in range(devices - MEMBERS)]
    down = [(j, i) for i, j in up]

    pieces = pack(state_in, sponge, wall_nodes, wall_weights, wall_count)
    own = [pieces[0]] + [lax.ppermute(pieces[d], AXES, inside(d)) for d in range(1, MEMBERS)]
    halo = [lax.ppermute(pieces[d], AXES, across(d)) for d in range(MEMBERS)]

    nodes_here = mode_shapes.shape[1]
    sent = jnp.tile(mode_shapes.reshape(MEMBERS, 2 * nodes_here // LANES, LANES), (groups, 1, 1))
    got = lax.all_to_all(sent, AXES, 0, 0)
    shapes = got.reshape(devices, 2, nodes_here // LANES, LANES).transpose(1, 0, 2, 3)
    shapes = shapes.reshape(2, devices * nodes_here // LANES, LANES)

    border = jax.ShapeDtypeStruct((FIELDS, 2, DEEP, 4 * ROWS, LANES), F32)
    piece = jax.ShapeDtypeStruct((2, FIELDS, DEEP, ROWS, LANES), F32)
    wall = jax.ShapeDtypeStruct((2, 4 * DEEP, ROWS, LANES), F32)
    field = pltpu.VMEM((FIELDS, 2, 4 * DEEP, 4 * ROWS, LANES), F32)
    damping = jax.ShapeDtypeStruct((4 * DEEP, 4 * ROWS, LANES), F32)
    q_low, q_high, wall_rows, sponge_ext, *first = pl.pallas_call(
        functools.partial(first_kernel, groups),
        out_shape=[border, border, wall, damping] + [piece] * MEMBERS,
        in_specs=[SMEM, SMEM, VMEM] + [VMEM] * (2 * MEMBERS),
        out_specs=[VMEM] * (4 + MEMBERS),
        scratch_shapes=[field, field, field, pltpu.VMEM((4, 4, ROWS, LANES), F32)],
        compiler_params=PARAMS,
        name="first_step",
    )(mean_velocity, wall_vector, shapes, *own, *halo)

    below = lax.ppermute(q_high, AXES, up)
    above = lax.ppermute(q_low, AXES, down)
    first = [first[0]] + [lax.ppermute(first[d], AXES, inside(d)) for d in range(1, MEMBERS)]

    half = pltpu.VMEM((FIELDS, 2, DEEP, 4 * ROWS, LANES), F32)
    second = pl.pallas_call(
        functools.partial(second_kernel, groups),
        out_shape=[piece] * MEMBERS,
        in_specs=[SMEM, SMEM] + [VMEM] * 6,
        out_specs=[VMEM] * MEMBERS,
        scratch_shapes=[half, half, field, field, field],
        compiler_params=PARAMS,
        name="second_step",
    )(mean_velocity, wall_vector, sponge_ext, wall_rows, below, q_low, q_high, above)
    second = [second[0]] + [lax.ppermute(second[d], AXES, inside(d)) for d in range(1, MEMBERS)]

    rows_total = float(FIELDS * cells_x * gx_size * cells_y * gy_size * cells_z)
    snap_count = STEPS * 2 * MEMBERS
    state_out, grams = pl.pallas_call(
        functools.partial(gram_kernel, rows_total),
        out_shape=[
            jax.ShapeDtypeStruct(state_in.shape, F32),
            jax.ShapeDtypeStruct((devices, ROWS, LANES), F32),
        ],
        in_specs=[VMEM] * (2 * MEMBERS),
        out_specs=[VMEM, VMEM],
        scratch_shapes=[pltpu.VMEM((snap_count * FIELDS * DEEP * ROWS, LANES), F32)],
        compiler_params=PARAMS,
        name="gram",
    )(*first, *second)
    grams = lax.all_to_all(grams, AXES, 0, 0)
    gram_matrix = pl.pallas_call(
        functools.partial(sum_kernel, rows_total),
        out_shape=jax.ShapeDtypeStruct((snap_count, snap_count), F32),
        in_specs=[VMEM],
        out_specs=VMEM,
        compiler_params=PARAMS,
        name="gram_sum",
    )(grams)
    return state_out, jnp.linalg.cholesky(gram_matrix).T


def solution(mesh):
    placed = (
        P(None, None, "gx", "gy", None),
        P("gx", "gy", None),
        P(),
        P(),
        P(None, ("gx", "gy")),
        P(None, "gx", None),
        P(None, "gx", None),
        P("gx"),
    )
    return jax.shard_map(
        local,
        mesh=mesh,
        in_specs=placed,
        out_specs=(P(None, None, "gx", "gy", None), P()),
        check_vma=False,
    )
```

```python
import functools
import math

import jax
import jax.numpy as jnp
from jax import lax
from jax.experimental import pallas as pl
from jax.experimental.pallas import tpu as pltpu
from jax.sharding import PartitionSpec as P

STEPS = 2
NU_DAMP = 0.25
DT_STEP = 0.4
PULSE_MID = 0.8
PULSE_WIDTH = 0.5

AXES = ("gx", "gy")
FIELDS = 5
DEEP = 4
MEMBERS = 8
ROWS = 8
LANES = 128
STATE = FIELDS * DEEP
SPONGE = 2 * STATE
PIECE = SPONGE + DEEP
F32 = jnp.float32

VMEM = pl.BlockSpec(memory_space=pltpu.VMEM)
SMEM = pl.BlockSpec(memory_space=pltpu.SMEM)
HBM = pl.BlockSpec(memory_space=pltpu.HBM)
PARAMS = pltpu.CompilerParams(vmem_limit_bytes=48 * 1024 * 1024)


def cost(micros):
    return pl.CostEstimate(flops=0, transcendentals=0, bytes_accessed=int(3.0e6 * micros))


def pulse(time_now):
    return math.exp(-(((time_now - PULSE_MID) / PULSE_WIDTH) ** 2))


def step_scales(step):
    start = step * DT_STEP
    p0, ph, p1 = pulse(start), pulse(start + 0.5 * DT_STEP), pulse(start + DT_STEP)
    return (
        (DT_STEP / 4.0, p0),
        (DT_STEP / 3.0, (p0 + ph) / 2.0),
        (DT_STEP / 2.0, (p0 + 2.0 * ph) / 3.0),
        (DT_STEP, (p0 + 4.0 * ph + p1) / 6.0),
    )


def position():
    along_x = lax.axis_index("gx")
    return along_x // 2, (along_x % 2) * 4 + lax.axis_index("gy")


def pack_kernel(groups, state_hbm, sponge_hbm, nodes_hbm, weights_hbm, count_hbm, shapes_hbm, *refs):
    pieces, wall = refs[:MEMBERS], refs[MEMBERS]
    sponge_ref, nodes_ref, weights_ref, count_ref, shapes_ref, sems = refs[MEMBERS + 1 :]
    _, member = position()
    row = member % 4
    small = [
        pltpu.make_async_copy(count_hbm, count_ref, sems.at[0]),
        pltpu.make_async_copy(nodes_hbm.at[row], nodes_ref, sems.at[1]),
        pltpu.make_async_copy(weights_hbm.at[row], weights_ref, sems.at[2]),
        pltpu.make_async_copy(sponge_hbm, sponge_ref, sems.at[3]),
        pltpu.make_async_copy(shapes_hbm, shapes_ref, sems.at[4]),
    ]
    large = []
    for d, piece in enumerate(pieces):
        for f in range(FIELDS):
            large.append(
                pltpu.make_async_copy(
                    state_hbm.at[f, pl.ds(2 * DEEP * (member ^ d), 2 * DEEP)],
                    piece.at[pl.ds(2 * DEEP * f, 2 * DEEP)],
                    sems.at[5 + d * FIELDS + f],
                )
            )
    for copy in small + large:
        copy.start()
    for copy in small:
        copy.wait()
    lane = lax.broadcasted_iota(jnp.int32, (1, LANES), 1)
    table = [nodes_ref[...].astype(F32)]
    for x in range(DEEP):
        kept = jnp.where(lane < count_ref[x], 1.0, 0.0)
        table.append(weights_ref[pl.ds(x, 1), :] * kept)
    table = jnp.concatenate(table, axis=0)
    for piece in pieces:
        for x in range(DEEP):
            piece[SPONGE + x] = sponge_ref[x]
    for m in range(MEMBERS):
        two = shapes_ref[2 * m : 2 * m + 2, :]
        lines = jnp.concatenate([two[:, :LANES], two[:, LANES:]] * 2, axis=0)
        for g in range(groups):
            wall[g * MEMBERS + m, 0] = lines
            wall[g * MEMBERS + m, 1] = table
    for copy in large:
        copy.wait()


def pack(groups, state_in, sponge, nodes, weights, count, shapes):
    inputs = (
        state_in.reshape(FIELDS, 2 * MEMBERS * DEEP, ROWS, LANES),
        sponge, nodes, weights, count, shapes,
    )
    return pl.pallas_call(
        functools.partial(pack_kernel, groups),
        out_shape=[jax.ShapeDtypeStruct((PIECE, ROWS, LANES), F32)] * MEMBERS
        + [jax.ShapeDtypeStruct((groups * MEMBERS, 2, ROWS, LANES), F32)],
        in_specs=[HBM] * 6,
        out_specs=[VMEM] * (MEMBERS + 1),
        scratch_shapes=[
            pltpu.VMEM(sponge.shape, F32),
            pltpu.VMEM(nodes.shape[1:], jnp.int32),
            pltpu.VMEM(weights.shape[1:], F32),
            pltpu.SMEM(count.shape, jnp.int32),
            pltpu.VMEM(shapes.shape, F32),
            pltpu.SemaphoreType.DMA((5 + MEMBERS * FIELDS,)),
        ],
        compiler_params=PARAMS,
        cost_estimate=cost(2),
        name="pack",
    )(*[pltpu.with_memory_space_constraint(x, pltpu.HBM) for x in inputs])


def assemble_kernel(*refs):
    pieces, targets = refs[:MEMBERS], refs[MEMBERS:]
    group, member = position()
    even = group % 2 == 0
    for d, piece in enumerate(pieces):
        other = member ^ d
        is_first = (other >= 4) == even

        def copy(modes):
            for f in range(FIELDS):
                for j in range(2):
                    for x in range(DEEP):
                        modes[j][other % 4, f * DEEP + x] = piece[(f * 2 + j) * DEEP + x]
            for x in range(DEEP):
                modes[0][other % 4, STATE + x] = piece[SPONGE + x]

        @pl.when(is_first)
        def _():
            copy(targets[0::2])

        @pl.when(jnp.logical_not(is_first))
        def _():
            copy(targets[1::2])


def shifted_rows(tiles, sub):
    ahead = [pltpu.roll(t, ROWS - 1, 0) for t in tiles]
    behind = [pltpu.roll(t, 1, 0) for t in tiles]
    zero = jnp.zeros_like(tiles[0])
    last, first = sub == ROWS - 1, sub == 0
    count = len(tiles)
    north = [jnp.where(last, ahead[t + 1] if t + 1 < count else zero, ahead[t]) for t in range(count)]
    south = [jnp.where(first, behind[t - 1] if t > 0 else zero, behind[t]) for t in range(count)]
    return north, south


def run_stage(src, base, dst, sponge_ref, wall_ref, vel, wall_vec, h, scale, low, high):
    lane = lax.broadcasted_iota(jnp.int32, (ROWS, LANES), 1)
    sub = lax.broadcasted_iota(jnp.int32, (ROWS, LANES), 0)
    plus = [h * (NU_DAMP - 0.5 * v) for v in vel]
    minus = [h * (NU_DAMP + 0.5 * v) for v in vel]
    not_top, not_low = lane < LANES - 1, lane > 0
    plus_z = jnp.where(not_top, plus[2], 0.0)
    minus_z = jnp.where(not_low, minus[2], 0.0)
    flux = -0.5 * h
    flux_up = jnp.where(not_top, flux, 0.0)
    flux_low = jnp.where(not_low, flux, 0.0)
    tiles = range(4)

    def plane(i, carry):
        def load(ref, f, at):
            return [ref[f, at, pl.ds(ROWS * t, ROWS), :] for t in tiles]

        damp = [-h * (6.0 * NU_DAMP + sponge_ref[i, pl.ds(ROWS * t, ROWS), :]) for t in tiles]
        new = []
        for f in range(FIELDS):
            center = load(src, f, i)
            east, west = load(src, f, i + 1), load(src, f, i - 1)
            north, south = shifted_rows(center, sub)
            upper = [pltpu.roll(c, LANES - 1, 1) for c in center]
            lower = [pltpu.roll(c, 1, 1) for c in center]
            old = load(base, f, i)
            out = []
            for t in tiles:
                acc = old[t] + damp[t] * center[t]
                acc += plus[0] * east[t] + minus[0] * west[t]
                acc += plus[1] * north[t] + minus[1] * south[t]
                acc += plus_z * upper[t] + minus_z * lower[t]
                if t == 0:
                    acc += (h * scale * wall_vec[f]) * wall_ref[i]
                out.append(acc)
            new.append(out)
            if f == 1:
                d1 = [east[t] - west[t] for t in tiles]
            elif f == 2:
                d2 = [north[t] - south[t] for t in tiles]
            elif f == 3:
                d3 = [flux_up * upper[t] - flux_low * lower[t] for t in tiles]
            elif f == 4:
                for t in tiles:
                    new[1][t] += flux * (east[t] - west[t])
                    new[2][t] += flux * (north[t] - south[t])
                    new[3][t] += flux_up * upper[t] - flux_low * lower[t]
        for t in tiles:
            spread = flux * (d1[t] + d2[t]) + d3[t]
            new[0][t] += spread
            new[4][t] += spread
        for f in range(FIELDS):
            for t in tiles:
                dst[f, i, pl.ds(ROWS * t, ROWS), :] = new[f][t]
        return carry

    def two_planes(n, carry):
        plane(low + 2 * n, carry)
        return plane(low + 2 * n + 1, carry)

    lax.fori_loop(0, (high - low) // 2, two_planes, 0)


def run_step(step, base, va, vb, sponge_ref, wall_ref, vel, wall_vec, has_low, has_high):
    zero = jnp.zeros((ROWS, LANES), F32)
    src = base
    for k, (h, scale) in enumerate(step_scales(step)):
        dst = va if k % 2 == 0 else vb
        low, high = k + 1, 4 * DEEP - 1 - k
        run_stage(src, base, dst, sponge_ref, wall_ref, vel, wall_vec, h, scale, low, high)
        if k < 3:
            for there, at in ((has_low, DEEP - 1), (has_high, 3 * DEEP)):

                @pl.when(jnp.logical_not(there))
                def _():
                    for f in range(FIELDS):
                        for t in range(4):
                            dst[f, at, pl.ds(ROWS * t, ROWS), :] = zero

        src = dst


def write_pieces(sources, pieces):
    for m in range(MEMBERS):
        row = ROWS * (m % 4)
        for j, (ref, starts) in enumerate(sources):
            for f in range(FIELDS):
                for x in range(DEEP):
                    pieces[m, j, f, x] = ref[f, starts[m // 4] + x, row : row + ROWS, :]


def block_starts(group):
    even = group % 2 == 0
    return (
        jnp.where(even, 2 * DEEP, DEEP),
        jnp.where(even, DEEP, 2 * DEEP),
        jnp.where(even, 3 * DEEP, 0),
        jnp.where(even, 0, 3 * DEEP),
    )


def forcing_kernel(groups, parts, *walls):
    group, member = position()
    last = groups - 1
    tab = []
    for block in range(4):
        side = jnp.clip(group + (-1, 0, 0, 1)[block], 0, last)
        there = (group > 0, True, True, group < last)[block]
        for half in range(2):
            two = [parts[side * MEMBERS + (4, 0, 4, 0)[block] + 2 * half + n, 1] for n in range(2)]
            tab.append((two, there))
    zero = jnp.zeros((ROWS, LANES), F32)
    low_part, high_part, weights = [], [], []
    for two, there in tab:
        index = jnp.concatenate([two[0][:DEEP], two[1][:DEEP]], axis=0).astype(jnp.int32)
        weight = jnp.concatenate([two[0][DEEP:], two[1][DEEP:]], axis=0)
        weights.append(weight if there is True else jnp.where(there, weight, 0.0))
        low_part.append(index & (LANES - 1))
        high_part.append(index // LANES)
    count = len(weights)

    def body(q, taken):
        taken = [list(taken[j]) for j in range(2)]
        tile = parts[q, 0]
        for s in range(2):
            for j in range(2):
                line = jnp.broadcast_to(tile[2 * s + j : 2 * s + j + 1], (ROWS, LANES))
                for b in range(count):
                    value = jnp.take_along_axis(line, low_part[b], axis=1)
                    taken[j][b] = jnp.where(high_part[b] == 2 * q + s, value, taken[j][b])
        return tuple(tuple(t) for t in taken)

    start = tuple(tuple(zero for _ in range(count)) for _ in range(2))
    taken = lax.fori_loop(0, groups * MEMBERS, body, start)
    sub = lax.broadcasted_iota(jnp.int32, (ROWS, LANES), 0)
    for j in range(2):
        for block in range(4):
            total = sum(taken[j][2 * block + n] * weights[2 * block + n] for n in range(2))
            total = total[:DEEP] + total[DEEP:]
            for x in range(DEEP):
                line = jnp.broadcast_to(total[x : x + 1], (ROWS, LANES))
                walls[j][DEEP * block + x] = jnp.where(sub == 0, line, 0.0)


def first_kernel(groups, mode, vel_ref, vec_ref, wall_ref, *refs):
    blocks, refs = refs[:4], refs[4:]
    if mode == 0:
        a_ref, b_ref, sponge_ref, base, va, vb = refs
    else:
        sponge_ref, a_other, b_other, a_ref, b_ref = refs[:5]
        pieces, base, va, vb = refs[5:]
    group, member = position()
    starts = block_starts(group)
    for source, start in zip(blocks, starts):
        for y in range(4):
            rows = pl.ds(ROWS * y, ROWS)
            for f in range(FIELDS):
                for x in range(DEEP):
                    base[f, start + x, rows, :] = source[y, f * DEEP + x]
            if mode == 0:
                for x in range(DEEP):
                    sponge_ref[start + x, rows, :] = source[y, STATE + x]
    vel = [vel_ref[d] for d in range(3)]
    vec = [vec_ref[f] for f in range(FIELDS)]
    run_step(0, base, va, vb, sponge_ref, wall_ref, vel, vec, group > 0, group < groups - 1)
    for target, start in zip((a_ref, b_ref), starts):
        for f in range(FIELDS):
            for x in range(DEEP):
                target[f, x] = vb[f, start + x]
    if mode == 1:
        for f in range(FIELDS):
            for x in range(DEEP):
                va[f, starts[0] + x] = a_other[f, x]
                va[f, starts[1] + x] = b_other[f, x]
        write_pieces([(va, (DEEP, 2 * DEEP)), (vb, (DEEP, 2 * DEEP))], pieces)


def second_kernel(groups, mode, vel_ref, vec_ref, wall_ref, *refs):
    blocks, refs = refs[:4], refs[4:]
    if mode == 0:
        sponge_ref, target, base, va, vb = refs
    else:
        sponge_ref, other = refs[:2]
        pieces = refs[2 : 2 + MEMBERS]
        base, va, vb = refs[2 + MEMBERS :]
    group, member = position()
    for source, start in zip(blocks, block_starts(group)):
        for f in range(FIELDS):
            for x in range(DEEP):
                base[f, start + x] = source[f, x]
    vel = [vel_ref[d] for d in range(3)]
    vec = [vec_ref[f] for f in range(FIELDS)]
    run_step(1, base, va, vb, sponge_ref, wall_ref, vel, vec, group > 0, group < groups - 1)
    if mode == 0:
        for f in range(FIELDS):
            for x in range(2 * DEEP):
                target[f, x] = vb[f, DEEP + x]
    else:
        for d in range(MEMBERS):
            to = member ^ d
            row = pl.multiple_of((to % 4) * ROWS, ROWS)
            start = DEEP * (to // 4)
            for f in range(FIELDS):
                for x in range(DEEP):
                    pieces[d][0, f, x] = other[f, start + x, pl.ds(row, ROWS), :]
                    pieces[d][1, f, x] = vb[f, DEEP + start + x, pl.ds(row, ROWS), :]


def gram_kernel(total, *refs):
    first, second = refs[0], refs[1 : 1 + MEMBERS]
    state_ref, gram_ref, columns = refs[1 + MEMBERS :]
    _, member = position()
    tiles = FIELDS * DEEP
    for d in range(MEMBERS):
        other = member ^ d
        for j in range(2):
            here = (2 * d + j) * tiles * ROWS
            there = pl.multiple_of((2 * MEMBERS + 2 * other + j) * tiles * ROWS, ROWS)
            for f in range(FIELDS):
                for x in range(DEEP):
                    n = (f * DEEP + x) * ROWS
                    columns[here + n : here + n + ROWS, :] = first[d, j, f, x]
                    value = second[d][j, f, x]
                    columns[pl.ds(pl.multiple_of(there + n, ROWS), ROWS), :] = value
                    state_ref[f, 2 * other + j, x] = value
    size = STEPS * 2 * MEMBERS
    stride = tiles * ROWS

    def body(r, acc):
        a = jnp.concatenate(
            [columns[pl.ds(4 * r + n, size, stride=stride), :] for n in range(4)], axis=1
        )
        return acc + lax.dot_general(
            a, a, (((1,), (1,)), ((), ())),
            precision=lax.Precision.HIGHEST, preferred_element_type=F32,
        )

    gram = lax.fori_loop(0, stride // 4, body, jnp.zeros((size, size), F32), unroll=4)
    tile = jnp.concatenate([gram[ROWS * n : ROWS * n + ROWS] for n in range(4)], axis=1)
    for n in range(gram_ref.shape[0]):
        gram_ref[n] = tile


def factor_kernel(total, parts_ref, factor_ref):
    acc = parts_ref[0]
    for n in range(1, parts_ref.shape[0]):
        acc = acc + parts_ref[n]
    acc = acc / total
    size = factor_ref.shape[0]
    a = jnp.concatenate([acc[:, size * n : size * n + size] for n in range(4)], axis=0)
    lines = []
    for k in range(size):
        inverse = 1.0 / jnp.sqrt(a[k : k + 1, k : k + 1])
        line = a[k : k + 1, :] * inverse
        lines.append(line)
        if k < size - 1:
            a = a - (a[:, k : k + 1] * inverse) * line
    factor = jnp.concatenate(lines, axis=0)
    row = lax.broadcasted_iota(jnp.int32, (size, size), 0)
    col = lax.broadcasted_iota(jnp.int32, (size, size), 1)
    factor_ref[...] = jnp.where(col >= row, factor, 0.0)


def local(state_in, sponge, mean_velocity, wall_vector, mode_shapes, wall_nodes, wall_weights, wall_count):
    gx_size, gy_size = lax.axis_size("gx"), lax.axis_size("gy")
    groups = gx_size // 2
    devices = gx_size * gy_size
    cells_x, cells_y, cells_z = state_in.shape[2:]
    def inside(d):
        return [(i, i ^ d) for i in range(devices)]

    def swap(first):
        moves = []
        for i in range(devices):
            g = i // MEMBERS
            target = g + 1 if (g % 2 == 0) == first else g - 1
            if 0 <= target < groups:
                moves.append((i, i + (target - g) * MEMBERS))
        return moves

    def exchange(a, b):
        return a, b, lax.ppermute(a, AXES, swap(True)), lax.ppermute(b, AXES, swap(False))

    def spread(pieces):
        got = {0: pieces[0]}
        for d in (4, 2, 5, 3, 6, 7, 1):
            got[d] = lax.ppermute(pieces[d], AXES, inside(d))
        return [got[d] for d in range(MEMBERS)]

    def call(kernel, name, micros, out_shape, inputs, scratch=(), scalars=0):
        return pl.pallas_call(
            kernel,
            out_shape=out_shape,
            in_specs=[SMEM] * scalars + [VMEM] * (len(inputs) - scalars),
            out_specs=[VMEM] * len(out_shape),
            scratch_shapes=scratch,
            compiler_params=PARAMS,
            cost_estimate=cost(micros),
            name=name,
        )(*inputs)

    def shape(*sizes):
        return jax.ShapeDtypeStruct(sizes, F32)

    *pieces, wall = pack(groups, state_in, sponge, wall_nodes, wall_weights, wall_count, mode_shapes)
    pieces = spread(pieces)
    wall, pieces[1] = lax.optimization_barrier((wall, pieces[1]))
    wall = lax.all_to_all(wall, AXES, 0, 0)
    messages = call(
        assemble_kernel,
        "assemble",
        1,
        [shape(4, STATE + DEEP, ROWS, LANES)] * 2 + [shape(4, STATE, ROWS, LANES)] * 2,
        pieces,
    )
    blocks = [exchange(*messages[:2]), exchange(*messages[2:])]
    walls = call(
        functools.partial(forcing_kernel, groups),
        "forcing",
        5.0,
        [shape(4 * DEEP, ROWS, LANES)] * 2,
        [wall],
    )
    field = [pltpu.VMEM((FIELDS, 4 * DEEP, 4 * ROWS, LANES), F32)] * 3
    border = shape(FIELDS, DEEP, 4 * ROWS, LANES)
    piece = shape(2, FIELDS, DEEP, ROWS, LANES)
    constants = (mean_velocity, wall_vector)
    a0, b0, sponge_ext = call(
        functools.partial(first_kernel, groups, 0),
        "first_step_0",
        5.0,
        [border, border, shape(4 * DEEP, 4 * ROWS, LANES)],
        (*constants, walls[0], *blocks[0]),
        field,
        2,
    )
    next_blocks = [exchange(a0, b0)]
    a1, b1, first = call(
        functools.partial(first_kernel, groups, 1),
        "first_step_1",
        5.0,
        [border, border, shape(MEMBERS, 2, FIELDS, DEEP, ROWS, LANES)],
        (*constants, walls[1], *blocks[1], sponge_ext, a0, b0),
        field,
        2,
    )
    next_blocks.append(exchange(a1, b1))
    members = [[g * MEMBERS + m for m in range(MEMBERS)] for g in range(groups)]
    first = lax.all_to_all(first, AXES, 0, 0, axis_index_groups=members)
    (second_0,) = call(
        functools.partial(second_kernel, groups, 0),
        "second_step_0",
        5.0,
        [shape(FIELDS, 2 * DEEP, 4 * ROWS, LANES)],
        (*constants, walls[0], *next_blocks[0], sponge_ext),
        field,
        2,
    )
    second = call(
        functools.partial(second_kernel, groups, 1),
        "second_step_1",
        5.0,
        [piece] * MEMBERS,
        (*constants, walls[1], *next_blocks[1], sponge_ext, second_0),
        field,
        2,
    )
    second = spread(second)

    rows_total = float(FIELDS * cells_x * gx_size * cells_y * gy_size * cells_z)
    snap_count = STEPS * 2 * MEMBERS
    state_out, grams = pl.pallas_call(
        functools.partial(gram_kernel, rows_total),
        out_shape=[
            jax.ShapeDtypeStruct(state_in.shape, F32),
            jax.ShapeDtypeStruct((devices, ROWS, LANES), F32),
        ],
        in_specs=[VMEM] * (1 + MEMBERS),
        out_specs=[VMEM, VMEM],
        scratch_shapes=[pltpu.VMEM((snap_count * FIELDS * DEEP * ROWS, LANES), F32)],
        compiler_params=PARAMS,
        name="gram",
    )(first, *second)
    grams = lax.all_to_all(grams, AXES, 0, 0)
    factor = pl.pallas_call(
        functools.partial(factor_kernel, rows_total),
        out_shape=jax.ShapeDtypeStruct((snap_count, snap_count), F32),
        in_specs=[VMEM],
        out_specs=VMEM,
        compiler_params=PARAMS,
        name="factor",
    )(grams)
    return state_out, factor


def solution(mesh):
    placed = (
        P(None, None, "gx", "gy", None),
        P("gx", "gy", None),
        P(),
        P(),
        P(None, ("gx", "gy")),
        P(None, "gx", None),
        P(None, "gx", None),
        P("gx"),
    )
    return jax.shard_map(
        local,
        mesh=mesh,
        in_specs=placed,
        out_specs=(P(None, None, "gx", "gy", None), P()),
        check_vma=False,
    )
```

```python
import functools
import math

import jax
import jax.numpy as jnp
from jax import lax
from jax.experimental import pallas as pl
from jax.experimental.pallas import tpu as pltpu
from jax.sharding import PartitionSpec as P

STEPS = 2
NU_DAMP = 0.25
DT_STEP = 0.4
PULSE_MID = 0.8
PULSE_WIDTH = 0.5

AXES = ("gx", "gy")
FIELDS = 5
DEEP = 4
MEMBERS = 8
ROWS = 8
LANES = 128
STATE = FIELDS * DEEP
SPONGE = 2 * STATE
PIECE = SPONGE + DEEP
F32 = jnp.float32
TURNS = (0, 1, 4, 2, 5, 3, 6, 7)

VMEM = pl.BlockSpec(memory_space=pltpu.VMEM)
SMEM = pl.BlockSpec(memory_space=pltpu.SMEM)
HBM = pl.BlockSpec(memory_space=pltpu.HBM)
PARAMS = pltpu.CompilerParams(vmem_limit_bytes=24 * 1024 * 1024)


def cost(micros):
    return pl.CostEstimate(flops=0, transcendentals=0, bytes_accessed=int(3.0e6 * micros))


def pulse(time_now):
    return math.exp(-(((time_now - PULSE_MID) / PULSE_WIDTH) ** 2))


def step_scales(step):
    start = step * DT_STEP
    p0, ph, p1 = pulse(start), pulse(start + 0.5 * DT_STEP), pulse(start + DT_STEP)
    return (
        (DT_STEP / 4.0, p0),
        (DT_STEP / 3.0, (p0 + ph) / 2.0),
        (DT_STEP / 2.0, (p0 + 2.0 * ph) / 3.0),
        (DT_STEP, (p0 + 4.0 * ph + p1) / 6.0),
    )


def position():
    along_x = lax.axis_index("gx")
    return along_x // 2, (along_x % 2) * 4 + lax.axis_index("gy")


def pack_kernel(groups, state_hbm, sponge_hbm, nodes_hbm, weights_hbm, count_hbm, shapes_hbm, *refs):
    pieces, wall = refs[:MEMBERS], refs[MEMBERS]
    sponge_ref, nodes_ref, weights_ref, count_ref, shapes_ref, sems = refs[MEMBERS + 1 :]
    _, member = position()
    row = member % 4
    small = [
        pltpu.make_async_copy(count_hbm, count_ref, sems.at[0]),
        pltpu.make_async_copy(nodes_hbm.at[row], nodes_ref, sems.at[1]),
        pltpu.make_async_copy(weights_hbm.at[row], weights_ref, sems.at[2]),
        pltpu.make_async_copy(sponge_hbm, sponge_ref, sems.at[3]),
        pltpu.make_async_copy(shapes_hbm, shapes_ref, sems.at[4]),
    ]
    large = []
    for n, piece in enumerate(pieces):
        for f in range(FIELDS):
            large.append(
                pltpu.make_async_copy(
                    state_hbm.at[f, pl.ds(2 * DEEP * (member ^ TURNS[n]), 2 * DEEP)],
                    piece.at[pl.ds(2 * DEEP * f, 2 * DEEP)],
                    sems.at[5 + n * FIELDS + f],
                )
            )
    for copy in small + large:
        copy.start()
    for copy in small:
        copy.wait()
    lane = lax.broadcasted_iota(jnp.int32, (1, LANES), 1)
    table = [nodes_ref[...].astype(F32)]
    for x in range(DEEP):
        kept = jnp.where(lane < count_ref[x], 1.0, 0.0)
        table.append(weights_ref[pl.ds(x, 1), :] * kept)
    table = jnp.concatenate(table, axis=0)
    for piece in pieces:
        for x in range(DEEP):
            piece[SPONGE + x] = sponge_ref[x]
    for m in range(MEMBERS):
        two = shapes_ref[2 * m : 2 * m + 2, :]
        lines = jnp.concatenate([two[:, :LANES], two[:, LANES:]] * 2, axis=0)
        for g in range(groups):
            wall[g * MEMBERS + m, 0] = lines
            wall[g * MEMBERS + m, 1] = table
    for copy in large:
        copy.wait()


def pack(groups, state_in, sponge, nodes, weights, count, shapes):
    inputs = (
        state_in.reshape(FIELDS, 2 * MEMBERS * DEEP, ROWS, LANES),
        sponge, nodes, weights, count, shapes,
    )
    return pl.pallas_call(
        functools.partial(pack_kernel, groups),
        out_shape=[jax.ShapeDtypeStruct((PIECE, ROWS, LANES), F32)] * MEMBERS
        + [jax.ShapeDtypeStruct((groups * MEMBERS, 2, ROWS, LANES), F32)],
        in_specs=[HBM] * 6,
        out_specs=[VMEM] * (MEMBERS + 1),
        scratch_shapes=[
            pltpu.VMEM(sponge.shape, F32),
            pltpu.VMEM(nodes.shape[1:], jnp.int32),
            pltpu.VMEM(weights.shape[1:], F32),
            pltpu.SMEM(count.shape, jnp.int32),
            pltpu.VMEM(shapes.shape, F32),
            pltpu.SemaphoreType.DMA((5 + MEMBERS * FIELDS,)),
        ],
        compiler_params=PARAMS,
        cost_estimate=cost(2),
        name="pack",
    )(*[pltpu.with_memory_space_constraint(x, pltpu.HBM) for x in inputs])


def assemble_kernel(*refs):
    pieces, targets = refs[:MEMBERS], refs[MEMBERS:]
    group, member = position()
    even = group % 2 == 0
    for d, piece in zip(TURNS, pieces):
        other = member ^ d
        is_first = (other >= 4) == even

        def copy(modes):
            for f in range(FIELDS):
                for j in range(2):
                    for x in range(DEEP):
                        modes[j][other % 4, f * DEEP + x] = piece[(f * 2 + j) * DEEP + x]
            for x in range(DEEP):
                modes[0][other % 4, STATE + x] = piece[SPONGE + x]

        @pl.when(is_first)
        def _():
            copy(targets[0::2])

        @pl.when(jnp.logical_not(is_first))
        def _():
            copy(targets[1::2])


def shifted_rows(tiles, sub):
    ahead = [pltpu.roll(t, ROWS - 1, 0) for t in tiles]
    behind = [pltpu.roll(t, 1, 0) for t in tiles]
    zero = jnp.zeros_like(tiles[0])
    last, first = sub == ROWS - 1, sub == 0
    count = len(tiles)
    north = [jnp.where(last, ahead[t + 1] if t + 1 < count else zero, ahead[t]) for t in range(count)]
    south = [jnp.where(first, behind[t - 1] if t > 0 else zero, behind[t]) for t in range(count)]
    return north, south


def run_stage(src, base, dst, sponge_ref, wall_ref, vel, wall_vec, h, scale, low, high):
    lane = lax.broadcasted_iota(jnp.int32, (ROWS, LANES), 1)
    sub = lax.broadcasted_iota(jnp.int32, (ROWS, LANES), 0)
    plus = [h * (NU_DAMP - 0.5 * v) for v in vel]
    minus = [h * (NU_DAMP + 0.5 * v) for v in vel]
    not_top, not_low = lane < LANES - 1, lane > 0
    plus_z = jnp.where(not_top, plus[2], 0.0)
    minus_z = jnp.where(not_low, minus[2], 0.0)
    flux = -0.5 * h
    flux_up = jnp.where(not_top, flux, 0.0)
    flux_low = jnp.where(not_low, flux, 0.0)
    tiles = range(4)

    def plane(i, carry):
        def load(ref, f, at):
            return [ref[f, at, pl.ds(ROWS * t, ROWS), :] for t in tiles]

        damp = [-h * (6.0 * NU_DAMP + sponge_ref[i, pl.ds(ROWS * t, ROWS), :]) for t in tiles]
        new = []
        for f in range(FIELDS):
            center = load(src, f, i)
            east, west = load(src, f, i + 1), load(src, f, i - 1)
            north, south = shifted_rows(center, sub)
            upper = [pltpu.roll(c, LANES - 1, 1) for c in center]
            lower = [pltpu.roll(c, 1, 1) for c in center]
            old = load(base, f, i)
            out = []
            for t in tiles:
                acc = old[t] + damp[t] * center[t]
                acc += plus[0] * east[t] + minus[0] * west[t]
                acc += plus[1] * north[t] + minus[1] * south[t]
                acc += plus_z * upper[t] + minus_z * lower[t]
                if t == 0:
                    acc += (h * scale * wall_vec[f]) * wall_ref[i]
                out.append(acc)
            new.append(out)
            if f == 1:
                d1 = [east[t] - west[t] for t in tiles]
            elif f == 2:
                d2 = [north[t] - south[t] for t in tiles]
            elif f == 3:
                d3 = [flux_up * upper[t] - flux_low * lower[t] for t in tiles]
            elif f == 4:
                for t in tiles:
                    new[1][t] += flux * (east[t] - west[t])
                    new[2][t] += flux * (north[t] - south[t])
                    new[3][t] += flux_up * upper[t] - flux_low * lower[t]
        for t in tiles:
            spread = flux * (d1[t] + d2[t]) + d3[t]
            new[0][t] += spread
            new[4][t] += spread
        for f in range(FIELDS):
            for t in tiles:
                dst[f, i, pl.ds(ROWS * t, ROWS), :] = new[f][t]
        return carry

    def two_planes(n, carry):
        plane(low + 2 * n, carry)
        return plane(low + 2 * n + 1, carry)

    lax.fori_loop(0, (high - low) // 2, two_planes, 0)


def run_step(step, base, va, vb, sponge_ref, wall_ref, vel, wall_vec, has_low, has_high):
    zero = jnp.zeros((ROWS, LANES), F32)
    src = base
    for k, (h, scale) in enumerate(step_scales(step)):
        dst = va if k % 2 == 0 else vb
        low, high = k + 1, 4 * DEEP - 1 - k
        run_stage(src, base, dst, sponge_ref, wall_ref, vel, wall_vec, h, scale, low, high)
        if k < 3:
            for there, at in ((has_low, DEEP - 1), (has_high, 3 * DEEP)):

                @pl.when(jnp.logical_not(there))
                def _():
                    for f in range(FIELDS):
                        for t in range(4):
                            dst[f, at, pl.ds(ROWS * t, ROWS), :] = zero

        src = dst


def write_pieces(sources, pieces):
    for m in range(MEMBERS):
        row = ROWS * (m % 4)
        for j, (ref, starts) in enumerate(sources):
            for f in range(FIELDS):
                for x in range(DEEP):
                    pieces[m, j, f, x] = ref[f, starts[m // 4] + x, row : row + ROWS, :]


def block_starts(group):
    even = group % 2 == 0
    return (
        jnp.where(even, 2 * DEEP, DEEP),
        jnp.where(even, DEEP, 2 * DEEP),
        jnp.where(even, 3 * DEEP, 0),
        jnp.where(even, 0, 3 * DEEP),
    )


def forcing_kernel(groups, parts, *walls):
    group, member = position()
    last = groups - 1
    tab = []
    for block in range(4):
        side = jnp.clip(group + (-1, 0, 0, 1)[block], 0, last)
        there = (group > 0, True, True, group < last)[block]
        for half in range(2):
            two = [parts[side * MEMBERS + (4, 0, 4, 0)[block] + 2 * half + n, 1] for n in range(2)]
            tab.append((two, there))
    zero = jnp.zeros((ROWS, LANES), F32)
    low_part, high_part, weights = [], [], []
    for two, there in tab:
        index = jnp.concatenate([two[0][:DEEP], two[1][:DEEP]], axis=0).astype(jnp.int32)
        weight = jnp.concatenate([two[0][DEEP:], two[1][DEEP:]], axis=0)
        weights.append(weight if there is True else jnp.where(there, weight, 0.0))
        low_part.append(index & (LANES - 1))
        high_part.append(index // LANES)
    count = len(weights)

    def body(q, taken):
        taken = [list(taken[j]) for j in range(2)]
        tile = parts[q, 0]
        for s in range(2):
            for j in range(2):
                line = jnp.broadcast_to(tile[2 * s + j : 2 * s + j + 1], (ROWS, LANES))
                for b in range(count):
                    value = jnp.take_along_axis(line, low_part[b], axis=1)
                    taken[j][b] = jnp.where(high_part[b] == 2 * q + s, value, taken[j][b])
        return tuple(tuple(t) for t in taken)

    start = tuple(tuple(zero for _ in range(count)) for _ in range(2))
    taken = lax.fori_loop(0, groups * MEMBERS, body, start)
    sub = lax.broadcasted_iota(jnp.int32, (ROWS, LANES), 0)
    for j in range(2):
        for block in range(4):
            total = sum(taken[j][2 * block + n] * weights[2 * block + n] for n in range(2))
            total = total[:DEEP] + total[DEEP:]
            for x in range(DEEP):
                line = jnp.broadcast_to(total[x : x + 1], (ROWS, LANES))
                walls[j][DEEP * block + x] = jnp.where(sub == 0, line, 0.0)


def first_kernel(groups, mode, vel_ref, vec_ref, wall_ref, *refs):
    blocks, refs = refs[:4], refs[4:]
    if mode == 0:
        a_ref, b_ref, sponge_ref, base, va, vb = refs
    else:
        sponge_ref, a_other, b_other, a_ref, b_ref = refs[:5]
        pieces, base, va, vb = refs[5:]
    group, member = position()
    starts = block_starts(group)
    for source, start in zip(blocks, starts):
        for y in range(4):
            rows = pl.ds(ROWS * y, ROWS)
            for f in range(FIELDS):
                for x in range(DEEP):
                    base[f, start + x, rows, :] = source[y, f * DEEP + x]
            if mode == 0:
                for x in range(DEEP):
                    sponge_ref[start + x, rows, :] = source[y, STATE + x]
    vel = [vel_ref[d] for d in range(3)]
    vec = [vec_ref[f] for f in range(FIELDS)]
    run_step(0, base, va, vb, sponge_ref, wall_ref, vel, vec, group > 0, group < groups - 1)
    for target, start in zip((a_ref, b_ref), starts):
        for f in range(FIELDS):
            for x in range(DEEP):
                target[f, x] = vb[f, start + x]
    if mode == 1:
        for f in range(FIELDS):
            for x in range(DEEP):
                va[f, starts[0] + x] = a_other[f, x]
                va[f, starts[1] + x] = b_other[f, x]
        write_pieces([(va, (DEEP, 2 * DEEP)), (vb, (DEEP, 2 * DEEP))], pieces)


def second_kernel(groups, mode, vel_ref, vec_ref, wall_ref, *refs):
    blocks, refs = refs[:4], refs[4:]
    if mode == 0:
        sponge_ref, target, base, va, vb = refs
    else:
        sponge_ref, other = refs[:2]
        pieces = refs[2 : 2 + MEMBERS]
        base, va, vb = refs[2 + MEMBERS :]
    group, member = position()
    for source, start in zip(blocks, block_starts(group)):
        for f in range(FIELDS):
            for x in range(DEEP):
                base[f, start + x] = source[f, x]
    vel = [vel_ref[d] for d in range(3)]
    vec = [vec_ref[f] for f in range(FIELDS)]
    run_step(1, base, va, vb, sponge_ref, wall_ref, vel, vec, group > 0, group < groups - 1)
    if mode == 0:
        for f in range(FIELDS):
            for x in range(2 * DEEP):
                target[f, x] = vb[f, DEEP + x]
    else:
        for d in range(MEMBERS):
            to = member ^ TURNS[d]
            row = pl.multiple_of((to % 4) * ROWS, ROWS)
            start = DEEP * (to // 4)
            for f in range(FIELDS):
                for x in range(DEEP):
                    pieces[d][0, f, x] = other[f, start + x, pl.ds(row, ROWS), :]
                    pieces[d][1, f, x] = vb[f, DEEP + start + x, pl.ds(row, ROWS), :]


def gram_kernel(total, *refs):
    first, second = refs[0], refs[1 : 1 + MEMBERS]
    state_ref, gram_ref, columns = refs[1 + MEMBERS :]
    _, member = position()
    tiles = FIELDS * DEEP
    for d in range(MEMBERS):
        other = member ^ TURNS[d]
        for j in range(2):
            here = (2 * d + j) * tiles * ROWS
            there = pl.multiple_of((2 * MEMBERS + 2 * other + j) * tiles * ROWS, ROWS)
            for f in range(FIELDS):
                for x in range(DEEP):
                    n = (f * DEEP + x) * ROWS
                    columns[here + n : here + n + ROWS, :] = first[d, j, f, x]
                    value = second[d][j, f, x]
                    columns[pl.ds(pl.multiple_of(there + n, ROWS), ROWS), :] = value
                    state_ref[f, 2 * other + j, x] = value
    size = STEPS * 2 * MEMBERS
    stride = tiles * ROWS

    def body(r, acc):
        a = jnp.concatenate(
            [columns[pl.ds(4 * r + n, size, stride=stride), :] for n in range(4)], axis=1
        )
        return acc + lax.dot_general(
            a, a, (((1,), (1,)), ((), ())),
            precision=lax.Precision.HIGHEST, preferred_element_type=F32,
        )

    gram = lax.fori_loop(0, stride // 4, body, jnp.zeros((size, size), F32), unroll=4)
    tile = jnp.concatenate([gram[ROWS * n : ROWS * n + ROWS] for n in range(4)], axis=1)
    for n in range(gram_ref.shape[0]):
        gram_ref[n] = tile


def factor_kernel(total, parts_ref, factor_ref):
    acc = parts_ref[0]
    for n in range(1, parts_ref.shape[0]):
        acc = acc + parts_ref[n]
    acc = acc / total
    size = factor_ref.shape[0]
    a = jnp.concatenate([acc[:, size * n : size * n + size] for n in range(4)], axis=0)
    lines, pivots = [], []
    for k in range(0, size, 2):
        row0, row1 = a[k : k + 1, :], a[k + 1 : k + 2, :]
        pivot0, side, corner = row0[:, k : k + 1], row0[:, k + 1 : k + 2], row1[:, k + 1 : k + 2]
        ratio = side / pivot0
        pivot1 = corner - side * ratio
        row1 = row1 - ratio * row0
        lines += [row0, row1]
        pivots += [pivot0, pivot1]
        if k < size - 2:
            col0, col1 = a[:, k : k + 1], a[:, k + 1 : k + 2]
            a = a - col0 * (row0 / pivot0) - (col1 - ratio * col0) * (row1 / pivot1)
    factor = jnp.concatenate(lines, axis=0) / jnp.sqrt(jnp.concatenate(pivots, axis=0))
    row = lax.broadcasted_iota(jnp.int32, (size, size), 0)
    col = lax.broadcasted_iota(jnp.int32, (size, size), 1)
    factor_ref[...] = jnp.where(col >= row, factor, 0.0)


def local(state_in, sponge, mean_velocity, wall_vector, mode_shapes, wall_nodes, wall_weights, wall_count):
    gx_size, gy_size = lax.axis_size("gx"), lax.axis_size("gy")
    groups = gx_size // 2
    devices = gx_size * gy_size
    cells_x, cells_y, cells_z = state_in.shape[2:]
    def inside(d):
        return [(i, i ^ d) for i in range(devices)]

    def swap(first):
        moves = []
        for i in range(devices):
            g = i // MEMBERS
            target = g + 1 if (g % 2 == 0) == first else g - 1
            if 0 <= target < groups:
                moves.append((i, i + (target - g) * MEMBERS))
        return moves

    def exchange(a, b):
        return a, b, lax.ppermute(a, AXES, swap(True)), lax.ppermute(b, AXES, swap(False))

    def spread(pieces):
        sent = zip(pieces[1:], TURNS[1:])
        return [pieces[0]] + [lax.ppermute(piece, AXES, inside(d)) for piece, d in sent]

    def call(kernel, name, micros, out_shape, inputs, scratch=(), scalars=0):
        return pl.pallas_call(
            kernel,
            out_shape=out_shape,
            in_specs=[SMEM] * scalars + [VMEM] * (len(inputs) - scalars),
            out_specs=[VMEM] * len(out_shape),
            scratch_shapes=scratch,
            compiler_params=PARAMS,
            cost_estimate=cost(micros),
            name=name,
        )(*inputs)

    def shape(*sizes):
        return jax.ShapeDtypeStruct(sizes, F32)

    *pieces, wall = pack(groups, state_in, sponge, wall_nodes, wall_weights, wall_count, mode_shapes)
    pieces = spread(pieces)
    wall, pieces[1] = lax.optimization_barrier((wall, pieces[1]))
    wall = lax.all_to_all(wall, AXES, 0, 0)
    messages = call(
        assemble_kernel,
        "assemble",
        1,
        [shape(4, STATE + DEEP, ROWS, LANES)] * 2 + [shape(4, STATE, ROWS, LANES)] * 2,
        pieces,
    )
    blocks = [exchange(*messages[:2]), exchange(*messages[2:])]
    walls = call(
        functools.partial(forcing_kernel, groups),
        "forcing",
        5.0,
        [shape(4 * DEEP, ROWS, LANES)] * 2,
        [wall],
    )
    field = [pltpu.VMEM((FIELDS, 4 * DEEP, 4 * ROWS, LANES), F32)] * 3
    border = shape(FIELDS, DEEP, 4 * ROWS, LANES)
    piece = shape(2, FIELDS, DEEP, ROWS, LANES)
    constants = (mean_velocity, wall_vector)
    a0, b0, sponge_ext = call(
        functools.partial(first_kernel, groups, 0),
        "first_step_0",
        5.0,
        [border, border, shape(4 * DEEP, 4 * ROWS, LANES)],
        (*constants, walls[0], *blocks[0]),
        field,
        2,
    )
    next_blocks = [exchange(a0, b0)]
    a1, b1, first = call(
        functools.partial(first_kernel, groups, 1),
        "first_step_1",
        5.0,
        [border, border, shape(MEMBERS, 2, FIELDS, DEEP, ROWS, LANES)],
        (*constants, walls[1], *blocks[1], sponge_ext, a0, b0),
        field,
        2,
    )
    next_blocks.append(exchange(a1, b1))
    members = [[g * MEMBERS + m for m in range(MEMBERS)] for g in range(groups)]
    first, _ = lax.optimization_barrier((first, next_blocks[0]))
    first = lax.all_to_all(first, AXES, 0, 0, axis_index_groups=members)
    (second_0,) = call(
        functools.partial(second_kernel, groups, 0),
        "second_step_0",
        5.0,
        [shape(FIELDS, 2 * DEEP, 4 * ROWS, LANES)],
        (*constants, walls[0], *next_blocks[0], sponge_ext),
        field,
        2,
    )
    second = call(
        functools.partial(second_kernel, groups, 1),
        "second_step_1",
        5.0,
        [piece] * MEMBERS,
        (*constants, walls[1], *next_blocks[1], sponge_ext, second_0),
        field,
        2,
    )
    second = spread(second)

    rows_total = float(FIELDS * cells_x * gx_size * cells_y * gy_size * cells_z)
    snap_count = STEPS * 2 * MEMBERS
    state_out, grams = pl.pallas_call(
        functools.partial(gram_kernel, rows_total),
        out_shape=[
            jax.ShapeDtypeStruct(state_in.shape, F32),
            jax.ShapeDtypeStruct((devices, ROWS, LANES), F32),
        ],
        in_specs=[VMEM] * (1 + MEMBERS),
        out_specs=[VMEM, VMEM],
        scratch_shapes=[pltpu.VMEM((snap_count * FIELDS * DEEP * ROWS, LANES), F32)],
        compiler_params=PARAMS,
        name="gram",
    )(first, *second)
    grams = lax.all_to_all(grams, AXES, 0, 0)
    factor = pl.pallas_call(
        functools.partial(factor_kernel, rows_total),
        out_shape=jax.ShapeDtypeStruct((snap_count, snap_count), F32),
        in_specs=[VMEM],
        out_specs=VMEM,
        compiler_params=PARAMS,
        name="factor",
    )(grams)
    return state_out, factor


def solution(mesh):
    placed = (
        P(None, None, "gx", "gy", None),
        P("gx", "gy", None),
        P(),
        P(),
        P(None, ("gx", "gy")),
        P(None, "gx", None),
        P(None, "gx", None),
        P("gx"),
    )
    return jax.shard_map(
        local,
        mesh=mesh,
        in_specs=placed,
        out_specs=(P(None, None, "gx", "gy", None), P()),
        check_vma=False,
    )
```

```python
import functools
import math

import jax
import jax.numpy as jnp
from jax import lax
from jax.experimental import pallas as pl
from jax.experimental.pallas import tpu as pltpu
from jax.sharding import PartitionSpec as P

STEPS = 2
NU_DAMP = 0.25
DT_STEP = 0.4
PULSE_MID = 0.8
PULSE_WIDTH = 0.5

AXES = ("gx", "gy")
FIELDS = 5
DEEP = 4
MEMBERS = 8
ROWS = 8
LANES = 128
STATE = FIELDS * DEEP
SPONGE = 2 * STATE
PIECE = SPONGE + DEEP
CHUNK = 4
F32 = jnp.float32
TURNS = (0, 1, 4, 2, 5, 3, 6, 7)

VMEM = pl.BlockSpec(memory_space=pltpu.VMEM)
SMEM = pl.BlockSpec(memory_space=pltpu.SMEM)
HBM = pl.BlockSpec(memory_space=pltpu.HBM)
PARAMS = pltpu.CompilerParams(vmem_limit_bytes=24 * 1024 * 1024)


def cost(micros):
    return pl.CostEstimate(flops=0, transcendentals=0, bytes_accessed=int(3.0e6 * micros))


def pulse(time_now):
    return math.exp(-(((time_now - PULSE_MID) / PULSE_WIDTH) ** 2))


def step_scales(step):
    start = step * DT_STEP
    p0, ph, p1 = pulse(start), pulse(start + 0.5 * DT_STEP), pulse(start + DT_STEP)
    return (
        (DT_STEP / 4.0, p0),
        (DT_STEP / 3.0, (p0 + ph) / 2.0),
        (DT_STEP / 2.0, (p0 + 2.0 * ph) / 3.0),
        (DT_STEP, (p0 + 4.0 * ph + p1) / 6.0),
    )


def position():
    along_x = lax.axis_index("gx")
    return along_x // 2, (along_x % 2) * 4 + lax.axis_index("gy")


def pack_kernel(groups, state_hbm, sponge_hbm, nodes_hbm, weights_hbm, count_hbm, shapes_hbm, *refs):
    pieces, wall = refs[:MEMBERS], refs[MEMBERS]
    sponge_ref, nodes_ref, weights_ref, count_ref, shapes_ref, sems = refs[MEMBERS + 1 :]
    _, member = position()
    row = member % 4
    small = [
        pltpu.make_async_copy(count_hbm, count_ref, sems.at[0]),
        pltpu.make_async_copy(nodes_hbm.at[row], nodes_ref, sems.at[1]),
        pltpu.make_async_copy(weights_hbm.at[row], weights_ref, sems.at[2]),
        pltpu.make_async_copy(sponge_hbm, sponge_ref, sems.at[3]),
        pltpu.make_async_copy(shapes_hbm, shapes_ref, sems.at[4]),
    ]
    large = []
    for n, piece in enumerate(pieces):
        for f in range(FIELDS):
            large.append(
                pltpu.make_async_copy(
                    state_hbm.at[f, pl.ds(2 * DEEP * (member ^ TURNS[n]), 2 * DEEP)],
                    piece.at[pl.ds(2 * DEEP * f, 2 * DEEP)],
                    sems.at[5 + n * FIELDS + f],
                )
            )
    for copy in small + large:
        copy.start()
    for copy in small:
        copy.wait()
    lane = lax.broadcasted_iota(jnp.int32, (1, LANES), 1)
    table = [nodes_ref[...].astype(F32)]
    for x in range(DEEP):
        kept = jnp.where(lane < count_ref[x], 1.0, 0.0)
        table.append(weights_ref[pl.ds(x, 1), :] * kept)
    table = jnp.concatenate(table, axis=0)
    for piece in pieces:
        for x in range(DEEP):
            piece[SPONGE + x] = sponge_ref[x]
    for m in range(MEMBERS):
        two = shapes_ref[2 * m : 2 * m + 2, :]
        lines = jnp.concatenate([two[:, :LANES], two[:, LANES:]] * 2, axis=0)
        for g in range(groups):
            wall[g * MEMBERS + m, 0] = lines
            wall[g * MEMBERS + m, 1] = table
    for copy in large:
        copy.wait()


def pack(groups, state_in, sponge, nodes, weights, count, shapes):
    inputs = (
        state_in.reshape(FIELDS, 2 * MEMBERS * DEEP, ROWS, LANES),
        sponge, nodes, weights, count, shapes,
    )
    return pl.pallas_call(
        functools.partial(pack_kernel, groups),
        out_shape=[jax.ShapeDtypeStruct((PIECE, ROWS, LANES), F32)] * MEMBERS
        + [jax.ShapeDtypeStruct((groups * MEMBERS, 2, ROWS, LANES), F32)],
        in_specs=[HBM] * 6,
        out_specs=[VMEM] * (MEMBERS + 1),
        scratch_shapes=[
            pltpu.VMEM(sponge.shape, F32),
            pltpu.VMEM(nodes.shape[1:], jnp.int32),
            pltpu.VMEM(weights.shape[1:], F32),
            pltpu.SMEM(count.shape, jnp.int32),
            pltpu.VMEM(shapes.shape, F32),
            pltpu.SemaphoreType.DMA((5 + MEMBERS * FIELDS,)),
        ],
        compiler_params=PARAMS,
        cost_estimate=cost(2),
        name="pack",
    )(*[pltpu.with_memory_space_constraint(x, pltpu.HBM) for x in inputs])


def assemble_kernel(*refs):
    pieces, targets = refs[:MEMBERS], refs[MEMBERS:]
    group, member = position()
    even = group % 2 == 0
    for d, piece in zip(TURNS, pieces):
        other = member ^ d
        is_first = (other >= 4) == even

        def copy(modes):
            for f in range(FIELDS):
                for j in range(2):
                    for x in range(DEEP):
                        modes[j][other % 4, f * DEEP + x] = piece[(f * 2 + j) * DEEP + x]
            for x in range(DEEP):
                modes[0][other % 4, STATE + x] = piece[SPONGE + x]

        @pl.when(is_first)
        def _():
            copy(targets[0::2])

        @pl.when(jnp.logical_not(is_first))
        def _():
            copy(targets[1::2])


def shifted_rows(tiles, sub):
    ahead = [pltpu.roll(t, ROWS - 1, 0) for t in tiles]
    behind = [pltpu.roll(t, 1, 0) for t in tiles]
    zero = jnp.zeros_like(tiles[0])
    last, first = sub == ROWS - 1, sub == 0
    count = len(tiles)
    north = [jnp.where(last, ahead[t + 1] if t + 1 < count else zero, ahead[t]) for t in range(count)]
    south = [jnp.where(first, behind[t - 1] if t > 0 else zero, behind[t]) for t in range(count)]
    return north, south


def run_stage(src, base, dst, sponge_ref, wall_ref, vel, wall_vec, h, scale, low, high):
    lane = lax.broadcasted_iota(jnp.int32, (ROWS, LANES), 1)
    sub = lax.broadcasted_iota(jnp.int32, (ROWS, LANES), 0)
    plus = [h * (NU_DAMP - 0.5 * v) for v in vel]
    minus = [h * (NU_DAMP + 0.5 * v) for v in vel]
    not_top, not_low = lane < LANES - 1, lane > 0
    plus_z = jnp.where(not_top, plus[2], 0.0)
    minus_z = jnp.where(not_low, minus[2], 0.0)
    flux = -0.5 * h
    flux_up = jnp.where(not_top, flux, 0.0)
    flux_low = jnp.where(not_low, flux, 0.0)
    tiles = range(4)

    def plane(i, carry):
        def load(ref, f, at):
            return [ref[f, at, pl.ds(ROWS * t, ROWS), :] for t in tiles]

        damp = [-h * (6.0 * NU_DAMP + sponge_ref[i, pl.ds(ROWS * t, ROWS), :]) for t in tiles]
        new = []
        for f in range(FIELDS):
            center = load(src, f, i)
            east, west = load(src, f, i + 1), load(src, f, i - 1)
            north, south = shifted_rows(center, sub)
            upper = [pltpu.roll(c, LANES - 1, 1) for c in center]
            lower = [pltpu.roll(c, 1, 1) for c in center]
            old = load(base, f, i)
            out = []
            for t in tiles:
                acc = old[t] + damp[t] * center[t]
                acc += plus[0] * east[t] + minus[0] * west[t]
                acc += plus[1] * north[t] + minus[1] * south[t]
                acc += plus_z * upper[t] + minus_z * lower[t]
                if t == 0:
                    acc += (h * scale * wall_vec[f]) * wall_ref[i]
                out.append(acc)
            new.append(out)
            if f == 1:
                d1 = [east[t] - west[t] for t in tiles]
            elif f == 2:
                d2 = [north[t] - south[t] for t in tiles]
            elif f == 3:
                d3 = [flux_up * upper[t] - flux_low * lower[t] for t in tiles]
            elif f == 4:
                for t in tiles:
                    new[1][t] += flux * (east[t] - west[t])
                    new[2][t] += flux * (north[t] - south[t])
                    new[3][t] += flux_up * upper[t] - flux_low * lower[t]
        for t in tiles:
            spread = flux * (d1[t] + d2[t]) + d3[t]
            new[0][t] += spread
            new[4][t] += spread
        for f in range(FIELDS):
            for t in tiles:
                dst[f, i, pl.ds(ROWS * t, ROWS), :] = new[f][t]
        return carry

    def two_planes(n, carry):
        plane(low + 2 * n, carry)
        return plane(low + 2 * n + 1, carry)

    lax.fori_loop(0, (high - low) // 2, two_planes, 0)


def run_step(step, base, va, vb, sponge_ref, wall_ref, vel, wall_vec, has_low, has_high):
    zero = jnp.zeros((ROWS, LANES), F32)
    src = base
    for k, (h, scale) in enumerate(step_scales(step)):
        dst = va if k % 2 == 0 else vb
        low, high = k + 1, 4 * DEEP - 1 - k
        run_stage(src, base, dst, sponge_ref, wall_ref, vel, wall_vec, h, scale, low, high)
        if k < 3:
            for there, at in ((has_low, DEEP - 1), (has_high, 3 * DEEP)):

                @pl.when(jnp.logical_not(there))
                def _():
                    for f in range(FIELDS):
                        for t in range(4):
                            dst[f, at, pl.ds(ROWS * t, ROWS), :] = zero

        src = dst


def write_pieces(sources, pieces):
    for m in range(MEMBERS):
        row = ROWS * (m % 4)
        for j, (ref, starts) in enumerate(sources):
            for f in range(FIELDS):
                for x in range(DEEP):
                    pieces[m, j, f, x] = ref[f, starts[m // 4] + x, row : row + ROWS, :]


def block_starts(group):
    even = group % 2 == 0
    return (
        jnp.where(even, 2 * DEEP, DEEP),
        jnp.where(even, DEEP, 2 * DEEP),
        jnp.where(even, 3 * DEEP, 0),
        jnp.where(even, 0, 3 * DEEP),
    )


def forcing_kernel(groups, parts, *walls):
    group, member = position()
    last = groups - 1
    tab = []
    for block in range(4):
        side = jnp.clip(group + (-1, 0, 0, 1)[block], 0, last)
        there = (group > 0, True, True, group < last)[block]
        for half in range(2):
            two = [parts[side * MEMBERS + (4, 0, 4, 0)[block] + 2 * half + n, 1] for n in range(2)]
            tab.append((two, there))
    zero = jnp.zeros((ROWS, LANES), F32)
    low_part, high_part, weights = [], [], []
    for two, there in tab:
        index = jnp.concatenate([two[0][:DEEP], two[1][:DEEP]], axis=0).astype(jnp.int32)
        weight = jnp.concatenate([two[0][DEEP:], two[1][DEEP:]], axis=0)
        weights.append(weight if there is True else jnp.where(there, weight, 0.0))
        low_part.append(index & (LANES - 1))
        high_part.append(index // LANES)
    count = len(weights)

    def body(q, taken):
        taken = [list(taken[j]) for j in range(2)]
        tile = parts[q, 0]
        for s in range(2):
            for j in range(2):
                line = jnp.broadcast_to(tile[2 * s + j : 2 * s + j + 1], (ROWS, LANES))
                for b in range(count):
                    value = jnp.take_along_axis(line, low_part[b], axis=1)
                    taken[j][b] = jnp.where(high_part[b] == 2 * q + s, value, taken[j][b])
        return tuple(tuple(t) for t in taken)

    start = tuple(tuple(zero for _ in range(count)) for _ in range(2))
    taken = lax.fori_loop(0, groups * MEMBERS, body, start)
    sub = lax.broadcasted_iota(jnp.int32, (ROWS, LANES), 0)
    for j in range(2):
        for block in range(4):
            total = sum(taken[j][2 * block + n] * weights[2 * block + n] for n in range(2))
            total = total[:DEEP] + total[DEEP:]
            for x in range(DEEP):
                line = jnp.broadcast_to(total[x : x + 1], (ROWS, LANES))
                walls[j][DEEP * block + x] = jnp.where(sub == 0, line, 0.0)


def first_kernel(groups, mode, vel_ref, vec_ref, wall_ref, *refs):
    blocks, refs = refs[:4], refs[4:]
    if mode == 0:
        a_ref, b_ref, sponge_ref, base, va, vb = refs
    else:
        sponge_ref, a_other, b_other, a_ref, b_ref = refs[:5]
        pieces, base, va, vb = refs[5:]
    group, member = position()
    starts = block_starts(group)
    for source, start in zip(blocks, starts):
        for y in range(4):
            rows = pl.ds(ROWS * y, ROWS)
            for f in range(FIELDS):
                for x in range(DEEP):
                    base[f, start + x, rows, :] = source[y, f * DEEP + x]
            if mode == 0:
                for x in range(DEEP):
                    sponge_ref[start + x, rows, :] = source[y, STATE + x]
    vel = [vel_ref[d] for d in range(3)]
    vec = [vec_ref[f] for f in range(FIELDS)]
    run_step(0, base, va, vb, sponge_ref, wall_ref, vel, vec, group > 0, group < groups - 1)
    for target, start in zip((a_ref, b_ref), starts):
        for f in range(FIELDS):
            for x in range(DEEP):
                target[f, x] = vb[f, start + x]
    if mode == 1:
        for f in range(FIELDS):
            for x in range(DEEP):
                va[f, starts[0] + x] = a_other[f, x]
                va[f, starts[1] + x] = b_other[f, x]
        write_pieces([(va, (DEEP, 2 * DEEP)), (vb, (DEEP, 2 * DEEP))], pieces)


def second_kernel(groups, mode, vel_ref, vec_ref, wall_ref, *refs):
    blocks, refs = refs[:4], refs[4:]
    if mode == 0:
        sponge_ref, target, base, va, vb = refs
    else:
        sponge_ref, other = refs[:2]
        pieces = refs[2 : 2 + MEMBERS]
        base, va, vb = refs[2 + MEMBERS :]
    group, member = position()
    for source, start in zip(blocks, block_starts(group)):
        for f in range(FIELDS):
            for x in range(DEEP):
                base[f, start + x] = source[f, x]
    vel = [vel_ref[d] for d in range(3)]
    vec = [vec_ref[f] for f in range(FIELDS)]
    run_step(1, base, va, vb, sponge_ref, wall_ref, vel, vec, group > 0, group < groups - 1)
    if mode == 0:
        for f in range(FIELDS):
            for x in range(2 * DEEP):
                target[f, x] = vb[f, DEEP + x]
    else:
        for d in range(MEMBERS):
            to = member ^ TURNS[d]
            row = pl.multiple_of((to % 4) * ROWS, ROWS)
            start = DEEP * (to // 4)
            for f in range(FIELDS):
                for x in range(DEEP):
                    pieces[d][0, f, x] = other[f, start + x, pl.ds(row, ROWS), :]
                    pieces[d][1, f, x] = vb[f, DEEP + start + x, pl.ds(row, ROWS), :]


def three_parts(a):
    high = a.astype(jnp.bfloat16)
    rest = a - high.astype(F32)
    middle = rest.astype(jnp.bfloat16)
    low = (rest - middle.astype(F32)).astype(jnp.bfloat16)
    return jnp.concatenate([high, middle, low], axis=0)


def chunk_of(ref, r):
    stride = FIELDS * DEEP * ROWS
    rows = [ref[pl.ds(CHUNK * r + n, 2 * MEMBERS, stride=stride), :] for n in range(CHUNK)]
    return jnp.concatenate(rows, axis=1)


def split_kernel(first, parts_ref):
    def body(r, carry):
        parts_ref[r] = three_parts(chunk_of(first, r))
        return carry

    lax.fori_loop(0, parts_ref.shape[0], body, 0, unroll=4)


def gram_kernel(first_parts, *refs):
    second, (state_ref, gram_ref, columns) = refs[:MEMBERS], refs[MEMBERS:]
    _, member = position()
    tiles = FIELDS * DEEP
    for d in range(MEMBERS):
        other = member ^ TURNS[d]
        for j in range(2):
            start = (2 * other + j) * tiles * ROWS
            for f in range(FIELDS):
                for x in range(DEEP):
                    value = second[d][j, f, x]
                    at = pl.multiple_of(start + (f * DEEP + x) * ROWS, ROWS)
                    columns[pl.ds(at, ROWS), :] = value
                    state_ref[f, 2 * other + j, x] = value
    modes = 2 * MEMBERS

    def body(r, acc):
        parts = jnp.concatenate([first_parts[r], three_parts(chunk_of(columns, r))], axis=0)
        return acc + lax.dot_general(
            parts, parts, (((1,), (1,)), ((), ())), preferred_element_type=F32
        )

    acc = jnp.zeros((6 * modes, 6 * modes), F32)
    acc = lax.fori_loop(0, first_parts.shape[0], body, acc, unroll=4)

    def block(n, m):
        part = [modes * (3 * n + i) for i in range(3)], [modes * (3 * m + i) for i in range(3)]
        return sum(acc[r : r + modes, c : c + modes] for r in part[0] for c in part[1])

    rows = [jnp.concatenate([block(n, m) for m in range(STEPS)], axis=1) for n in range(STEPS)]
    tile = jnp.concatenate([line[ROWS * n : ROWS * n + ROWS] for line in rows for n in range(2)], axis=1)
    for n in range(gram_ref.shape[0]):
        gram_ref[n] = tile


def factor_kernel(total, parts_ref, factor_ref):
    acc = parts_ref[0]
    for n in range(1, parts_ref.shape[0]):
        acc = acc + parts_ref[n]
    acc = acc / total
    size = factor_ref.shape[0]
    a = jnp.concatenate([acc[:, size * n : size * n + size] for n in range(4)], axis=0)
    lines, pivots = [], []
    for k in range(0, size, 2):
        row0, row1 = a[k : k + 1, :], a[k + 1 : k + 2, :]
        pivot0, side, corner = row0[:, k : k + 1], row0[:, k + 1 : k + 2], row1[:, k + 1 : k + 2]
        ratio = side / pivot0
        pivot1 = corner - side * ratio
        row1 = row1 - ratio * row0
        lines += [row0, row1]
        pivots += [pivot0, pivot1]
        if k < size - 2:
            col0, col1 = a[:, k : k + 1], a[:, k + 1 : k + 2]
            a = a - col0 * (row0 / pivot0) - (col1 - ratio * col0) * (row1 / pivot1)
    factor = jnp.concatenate(lines, axis=0) / jnp.sqrt(jnp.concatenate(pivots, axis=0))
    row = lax.broadcasted_iota(jnp.int32, (size, size), 0)
    col = lax.broadcasted_iota(jnp.int32, (size, size), 1)
    factor_ref[...] = jnp.where(col >= row, factor, 0.0)


def local(state_in, sponge, mean_velocity, wall_vector, mode_shapes, wall_nodes, wall_weights, wall_count):
    gx_size, gy_size = lax.axis_size("gx"), lax.axis_size("gy")
    groups = gx_size // 2
    devices = gx_size * gy_size
    cells_x, cells_y, cells_z = state_in.shape[2:]
    def inside(d):
        return [(i, i ^ d) for i in range(devices)]

    def swap(first):
        moves = []
        for i in range(devices):
            g = i // MEMBERS
            target = g + 1 if (g % 2 == 0) == first else g - 1
            if 0 <= target < groups:
                moves.append((i, i + (target - g) * MEMBERS))
        return moves

    def exchange(a, b):
        return a, b, lax.ppermute(a, AXES, swap(True)), lax.ppermute(b, AXES, swap(False))

    def spread(pieces):
        sent = zip(pieces[1:], TURNS[1:])
        return [pieces[0]] + [lax.ppermute(piece, AXES, inside(d)) for piece, d in sent]

    def call(kernel, name, micros, out_shape, inputs, scratch=(), scalars=0):
        return pl.pallas_call(
            kernel,
            out_shape=out_shape,
            in_specs=[SMEM] * scalars + [VMEM] * (len(inputs) - scalars),
            out_specs=[VMEM] * len(out_shape),
            scratch_shapes=scratch,
            compiler_params=PARAMS,
            cost_estimate=cost(micros),
            name=name,
        )(*inputs)

    def shape(*sizes):
        return jax.ShapeDtypeStruct(sizes, F32)

    *pieces, wall = pack(groups, state_in, sponge, wall_nodes, wall_weights, wall_count, mode_shapes)
    pieces = spread(pieces)
    wall, pieces[1] = lax.optimization_barrier((wall, pieces[1]))
    wall = lax.all_to_all(wall, AXES, 0, 0)
    messages = call(
        assemble_kernel,
        "assemble",
        1,
        [shape(4, STATE + DEEP, ROWS, LANES)] * 2 + [shape(4, STATE, ROWS, LANES)] * 2,
        pieces,
    )
    blocks = [exchange(*messages[:2]), exchange(*messages[2:])]
    walls = call(
        functools.partial(forcing_kernel, groups),
        "forcing",
        5.0,
        [shape(4 * DEEP, ROWS, LANES)] * 2,
        [wall],
    )
    field = [pltpu.VMEM((FIELDS, 4 * DEEP, 4 * ROWS, LANES), F32)] * 3
    border = shape(FIELDS, DEEP, 4 * ROWS, LANES)
    piece = shape(2, FIELDS, DEEP, ROWS, LANES)
    constants = (mean_velocity, wall_vector)
    a0, b0, sponge_ext = call(
        functools.partial(first_kernel, groups, 0),
        "first_step_0",
        5.0,
        [border, border, shape(4 * DEEP, 4 * ROWS, LANES)],
        (*constants, walls[0], *blocks[0]),
        field,
        2,
    )
    next_blocks = [exchange(a0, b0)]
    a1, b1, first = call(
        functools.partial(first_kernel, groups, 1),
        "first_step_1",
        5.0,
        [border, border, shape(MEMBERS, 2, FIELDS, DEEP, ROWS, LANES)],
        (*constants, walls[1], *blocks[1], sponge_ext, a0, b0),
        field,
        2,
    )
    next_blocks.append(exchange(a1, b1))
    members = [[g * MEMBERS + m for m in range(MEMBERS)] for g in range(groups)]
    first, _ = lax.optimization_barrier((first, next_blocks[0]))
    first = lax.all_to_all(first, AXES, 0, 0, axis_index_groups=members)
    (second_0,) = call(
        functools.partial(second_kernel, groups, 0),
        "second_step_0",
        5.0,
        [shape(FIELDS, 2 * DEEP, 4 * ROWS, LANES)],
        (*constants, walls[0], *next_blocks[0], sponge_ext),
        field,
        2,
    )
    second = call(
        functools.partial(second_kernel, groups, 1),
        "second_step_1",
        5.0,
        [piece] * MEMBERS,
        (*constants, walls[1], *next_blocks[1], sponge_ext, second_0),
        field,
        2,
    )
    second = spread(second)

    row_count = FIELDS * DEEP * ROWS
    (parts,) = call(
        split_kernel,
        "split",
        2,
        [jax.ShapeDtypeStruct((row_count // CHUNK, 6 * MEMBERS, CHUNK * LANES), jnp.bfloat16)],
        [first.reshape(2 * MEMBERS * row_count, LANES)],
    )
    rows_total = float(FIELDS * cells_x * gx_size * cells_y * gy_size * cells_z)
    snap_count = STEPS * 2 * MEMBERS
    state_out, grams = pl.pallas_call(
        gram_kernel,
        out_shape=[
            jax.ShapeDtypeStruct(state_in.shape, F32),
            jax.ShapeDtypeStruct((devices, ROWS, LANES), F32),
        ],
        in_specs=[VMEM] * (1 + MEMBERS),
        out_specs=[VMEM, VMEM],
        scratch_shapes=[pltpu.VMEM((2 * MEMBERS * row_count, LANES), F32)],
        compiler_params=PARAMS,
        name="gram",
    )(parts, *second)
    grams = lax.all_to_all(grams, AXES, 0, 0)
    factor = pl.pallas_call(
        functools.partial(factor_kernel, rows_total),
        out_shape=jax.ShapeDtypeStruct((snap_count, snap_count), F32),
        in_specs=[VMEM],
        out_specs=VMEM,
        compiler_params=PARAMS,
        name="factor",
    )(grams)
    return state_out, factor


def solution(mesh):
    placed = (
        P(None, None, "gx", "gy", None),
        P("gx", "gy", None),
        P(),
        P(),
        P(None, ("gx", "gy")),
        P(None, "gx", None),
        P(None, "gx", None),
        P("gx"),
    )
    return jax.shard_map(
        local,
        mesh=mesh,
        in_specs=placed,
        out_specs=(P(None, None, "gx", "gy", None), P()),
        check_vma=False,
    )
```

```python
import functools
import math

import jax
import jax.numpy as jnp
from jax import lax
from jax.experimental import pallas as pl
from jax.experimental.pallas import tpu as pltpu
from jax.sharding import PartitionSpec as P

STEPS = 2
NU_DAMP = 0.25
DT_STEP = 0.4
PULSE_MID = 0.8
PULSE_WIDTH = 0.5

AXES = ("gx", "gy")
FIELDS = 5
DEEP = 4
MEMBERS = 8
ROWS = 8
LANES = 128
STATE = FIELDS * DEEP
SPONGE = 2 * STATE
PIECE = SPONGE + DEEP
CHUNK = 4
F32 = jnp.float32
TURNS = (0, 1, 4, 2, 5, 3, 6, 7)

VMEM = pl.BlockSpec(memory_space=pltpu.VMEM)
SMEM = pl.BlockSpec(memory_space=pltpu.SMEM)
HBM = pl.BlockSpec(memory_space=pltpu.HBM)
PARAMS = pltpu.CompilerParams(vmem_limit_bytes=24 * 1024 * 1024)


def cost(micros):
    return pl.CostEstimate(flops=0, transcendentals=0, bytes_accessed=int(3.0e6 * micros))


def pulse(time_now):
    return math.exp(-(((time_now - PULSE_MID) / PULSE_WIDTH) ** 2))


def step_scales(step):
    start = step * DT_STEP
    p0, ph, p1 = pulse(start), pulse(start + 0.5 * DT_STEP), pulse(start + DT_STEP)
    return (
        (DT_STEP / 4.0, p0),
        (DT_STEP / 3.0, (p0 + ph) / 2.0),
        (DT_STEP / 2.0, (p0 + 2.0 * ph) / 3.0),
        (DT_STEP, (p0 + 4.0 * ph + p1) / 6.0),
    )


def position():
    along_x = lax.axis_index("gx")
    return along_x // 2, (along_x % 2) * 4 + lax.axis_index("gy")


def pack_kernel(groups, state_hbm, sponge_hbm, nodes_hbm, weights_hbm, count_hbm, shapes_hbm, *refs):
    pieces, wall = refs[:MEMBERS], refs[MEMBERS]
    sponge_ref, nodes_ref, weights_ref, count_ref, shapes_ref, sems = refs[MEMBERS + 1 :]
    _, member = position()
    row = member % 4
    small = [
        pltpu.make_async_copy(count_hbm, count_ref, sems.at[0]),
        pltpu.make_async_copy(nodes_hbm.at[row], nodes_ref, sems.at[1]),
        pltpu.make_async_copy(weights_hbm.at[row], weights_ref, sems.at[2]),
        pltpu.make_async_copy(sponge_hbm, sponge_ref, sems.at[3]),
        pltpu.make_async_copy(shapes_hbm, shapes_ref, sems.at[4]),
    ]
    large = []
    for n, piece in enumerate(pieces):
        for f in range(FIELDS):
            large.append(
                pltpu.make_async_copy(
                    state_hbm.at[f, pl.ds(2 * DEEP * (member ^ TURNS[n]), 2 * DEEP)],
                    piece.at[pl.ds(2 * DEEP * f, 2 * DEEP)],
                    sems.at[5 + n * FIELDS + f],
                )
            )
    for copy in small + large:
        copy.start()
    for copy in small:
        copy.wait()
    lane = lax.broadcasted_iota(jnp.int32, (1, LANES), 1)
    table = [nodes_ref[...].astype(F32)]
    for x in range(DEEP):
        kept = jnp.where(lane < count_ref[x], 1.0, 0.0)
        table.append(weights_ref[pl.ds(x, 1), :] * kept)
    table = jnp.concatenate(table, axis=0)
    for piece in pieces:
        for x in range(DEEP):
            piece[SPONGE + x] = sponge_ref[x]
    for m in range(MEMBERS):
        two = shapes_ref[2 * m : 2 * m + 2, :]
        lines = jnp.concatenate([two[:, :LANES], two[:, LANES:]] * 2, axis=0)
        for g in range(groups):
            wall[g * MEMBERS + m, 0] = lines
            wall[g * MEMBERS + m, 1] = table
    for copy in large:
        copy.wait()


def pack(groups, state_in, sponge, nodes, weights, count, shapes):
    inputs = (
        state_in.reshape(FIELDS, 2 * MEMBERS * DEEP, ROWS, LANES),
        sponge, nodes, weights, count, shapes,
    )
    return pl.pallas_call(
        functools.partial(pack_kernel, groups),
        out_shape=[jax.ShapeDtypeStruct((PIECE, ROWS, LANES), F32)] * MEMBERS
        + [jax.ShapeDtypeStruct((groups * MEMBERS, 2, ROWS, LANES), F32)],
        in_specs=[HBM] * 6,
        out_specs=[VMEM] * (MEMBERS + 1),
        scratch_shapes=[
            pltpu.VMEM(sponge.shape, F32),
            pltpu.VMEM(nodes.shape[1:], jnp.int32),
            pltpu.VMEM(weights.shape[1:], F32),
            pltpu.SMEM(count.shape, jnp.int32),
            pltpu.VMEM(shapes.shape, F32),
            pltpu.SemaphoreType.DMA((5 + MEMBERS * FIELDS,)),
        ],
        compiler_params=PARAMS,
        cost_estimate=cost(2),
        name="pack",
    )(*[pltpu.with_memory_space_constraint(x, pltpu.HBM) for x in inputs])


def assemble_kernel(*refs):
    pieces, targets = refs[:MEMBERS], refs[MEMBERS:]
    group, member = position()
    even = group % 2 == 0
    for d, piece in zip(TURNS, pieces):
        other = member ^ d
        is_first = (other >= 4) == even

        def copy(modes):
            for f in range(FIELDS):
                for j in range(2):
                    for x in range(DEEP):
                        modes[j][other % 4, f * DEEP + x] = piece[(f * 2 + j) * DEEP + x]
            for x in range(DEEP):
                modes[0][other % 4, STATE + x] = piece[SPONGE + x]

        @pl.when(is_first)
        def _():
            copy(targets[0::2])

        @pl.when(jnp.logical_not(is_first))
        def _():
            copy(targets[1::2])


def shifted_rows(tiles, sub):
    ahead = [pltpu.roll(t, ROWS - 1, 0) for t in tiles]
    behind = [pltpu.roll(t, 1, 0) for t in tiles]
    zero = jnp.zeros_like(tiles[0])
    last, first = sub == ROWS - 1, sub == 0
    count = len(tiles)
    north = [jnp.where(last, ahead[t + 1] if t + 1 < count else zero, ahead[t]) for t in range(count)]
    south = [jnp.where(first, behind[t - 1] if t > 0 else zero, behind[t]) for t in range(count)]
    return north, south


def run_stage(src, base, dst, sponge_ref, wall_ref, vel, wall_vec, h, scale, low, high):
    lane = lax.broadcasted_iota(jnp.int32, (ROWS, LANES), 1)
    sub = lax.broadcasted_iota(jnp.int32, (ROWS, LANES), 0)
    plus = [h * (NU_DAMP - 0.5 * v) for v in vel]
    minus = [h * (NU_DAMP + 0.5 * v) for v in vel]
    not_top, not_low = lane < LANES - 1, lane > 0
    plus_z = jnp.where(not_top, plus[2], 0.0)
    minus_z = jnp.where(not_low, minus[2], 0.0)
    flux = -0.5 * h
    flux_up = jnp.where(not_top, flux, 0.0)
    flux_low = jnp.where(not_low, flux, 0.0)
    tiles = range(4)

    def plane(i, carry):
        def load(ref, f, at):
            return [ref[f, at, pl.ds(ROWS * t, ROWS), :] for t in tiles]

        damp = [-h * (6.0 * NU_DAMP + sponge_ref[i, pl.ds(ROWS * t, ROWS), :]) for t in tiles]
        new = []
        for f in range(FIELDS):
            center = load(src, f, i)
            east, west = load(src, f, i + 1), load(src, f, i - 1)
            north, south = shifted_rows(center, sub)
            upper = [pltpu.roll(c, LANES - 1, 1) for c in center]
            lower = [pltpu.roll(c, 1, 1) for c in center]
            old = load(base, f, i)
            out = []
            for t in tiles:
                acc = old[t] + damp[t] * center[t]
                acc += plus[0] * east[t] + minus[0] * west[t]
                acc += plus[1] * north[t] + minus[1] * south[t]
                acc += plus_z * upper[t] + minus_z * lower[t]
                if t == 0:
                    acc += (h * scale * wall_vec[f]) * wall_ref[i]
                out.append(acc)
            new.append(out)
            if f == 1:
                d1 = [east[t] - west[t] for t in tiles]
            elif f == 2:
                d2 = [north[t] - south[t] for t in tiles]
            elif f == 3:
                d3 = [flux_up * upper[t] - flux_low * lower[t] for t in tiles]
            elif f == 4:
                for t in tiles:
                    new[1][t] += flux * (east[t] - west[t])
                    new[2][t] += flux * (north[t] - south[t])
                    new[3][t] += flux_up * upper[t] - flux_low * lower[t]
        for t in tiles:
            spread = flux * (d1[t] + d2[t]) + d3[t]
            new[0][t] += spread
            new[4][t] += spread
        for f in range(FIELDS):
            for t in tiles:
                dst[f, i, pl.ds(ROWS * t, ROWS), :] = new[f][t]
        return carry

    def two_planes(n, carry):
        plane(low + 2 * n, carry)
        return plane(low + 2 * n + 1, carry)

    lax.fori_loop(0, (high - low) // 2, two_planes, 0)


def run_step(step, base, va, vb, sponge_ref, wall_ref, vel, wall_vec, has_low, has_high):
    zero = jnp.zeros((ROWS, LANES), F32)
    src = base
    for k, (h, scale) in enumerate(step_scales(step)):
        dst = va if k % 2 == 0 else vb
        low, high = k + 1, 4 * DEEP - 1 - k
        run_stage(src, base, dst, sponge_ref, wall_ref, vel, wall_vec, h, scale, low, high)
        if k < 3:
            for there, at in ((has_low, DEEP - 1), (has_high, 3 * DEEP)):

                @pl.when(jnp.logical_not(there))
                def _():
                    for f in range(FIELDS):
                        for t in range(4):
                            dst[f, at, pl.ds(ROWS * t, ROWS), :] = zero

        src = dst


def write_pieces(sources, near, far, member):
    for flip, pieces in enumerate((near, far)):
        for e in range(MEMBERS // 2):
            to = member ^ (2 * e + flip)
            row = pl.multiple_of((to % 4) * ROWS, ROWS)
            start = DEEP + DEEP * (to // 4)
            for j, source in enumerate(sources):
                for f in range(FIELDS):
                    for x in range(DEEP):
                        pieces[e, j, f, x] = source[f, start + x, pl.ds(row, ROWS), :]


def merge_kernel(near, far, *targets):
    for e, target in enumerate(targets):
        for b, source in enumerate((near, far)):
            for j in range(2):
                for f in range(FIELDS):
                    for x in range(DEEP):
                        target[b, j, f, x] = source[e + 1, j, f, x]


def block_starts(group):
    even = group % 2 == 0
    return (
        jnp.where(even, 2 * DEEP, DEEP),
        jnp.where(even, DEEP, 2 * DEEP),
        jnp.where(even, 3 * DEEP, 0),
        jnp.where(even, 0, 3 * DEEP),
    )


def forcing_kernel(groups, parts, *walls):
    group, member = position()
    last = groups - 1
    tab = []
    for block in range(4):
        side = jnp.clip(group + (-1, 0, 0, 1)[block], 0, last)
        there = (group > 0, True, True, group < last)[block]
        for half in range(2):
            two = [parts[side * MEMBERS + (4, 0, 4, 0)[block] + 2 * half + n, 1] for n in range(2)]
            tab.append((two, there))
    zero = jnp.zeros((ROWS, LANES), F32)
    low_part, high_part, weights = [], [], []
    for two, there in tab:
        index = jnp.concatenate([two[0][:DEEP], two[1][:DEEP]], axis=0).astype(jnp.int32)
        weight = jnp.concatenate([two[0][DEEP:], two[1][DEEP:]], axis=0)
        weights.append(weight if there is True else jnp.where(there, weight, 0.0))
        low_part.append(index & (LANES - 1))
        high_part.append(index // LANES)
    count = len(weights)

    def body(q, taken):
        taken = [list(taken[j]) for j in range(2)]
        tile = parts[q, 0]
        for s in range(2):
            for j in range(2):
                line = jnp.broadcast_to(tile[2 * s + j : 2 * s + j + 1], (ROWS, LANES))
                for b in range(count):
                    value = jnp.take_along_axis(line, low_part[b], axis=1)
                    taken[j][b] = jnp.where(high_part[b] == 2 * q + s, value, taken[j][b])
        return tuple(tuple(t) for t in taken)

    start = tuple(tuple(zero for _ in range(count)) for _ in range(2))
    taken = lax.fori_loop(0, groups * MEMBERS, body, start)
    sub = lax.broadcasted_iota(jnp.int32, (ROWS, LANES), 0)
    for j in range(2):
        for block in range(4):
            total = sum(taken[j][2 * block + n] * weights[2 * block + n] for n in range(2))
            total = total[:DEEP] + total[DEEP:]
            for x in range(DEEP):
                line = jnp.broadcast_to(total[x : x + 1], (ROWS, LANES))
                walls[j][DEEP * block + x] = jnp.where(sub == 0, line, 0.0)


def first_kernel(groups, mode, vel_ref, vec_ref, wall_ref, *refs):
    blocks, refs = refs[:4], refs[4:]
    if mode == 0:
        a_ref, b_ref, sponge_ref, base, va, vb = refs
    else:
        sponge_ref, a_other, b_other, a_ref, b_ref, near, far, base, va, vb = refs
    group, member = position()
    starts = block_starts(group)
    for source, start in zip(blocks, starts):
        for y in range(4):
            rows = pl.ds(ROWS * y, ROWS)
            for f in range(FIELDS):
                for x in range(DEEP):
                    base[f, start + x, rows, :] = source[y, f * DEEP + x]
            if mode == 0:
                for x in range(DEEP):
                    sponge_ref[start + x, rows, :] = source[y, STATE + x]
    vel = [vel_ref[d] for d in range(3)]
    vec = [vec_ref[f] for f in range(FIELDS)]
    run_step(0, base, va, vb, sponge_ref, wall_ref, vel, vec, group > 0, group < groups - 1)
    for target, start in zip((a_ref, b_ref), starts):
        for f in range(FIELDS):
            for x in range(DEEP):
                target[f, x] = vb[f, start + x]
    if mode == 1:
        for f in range(FIELDS):
            for x in range(DEEP):
                va[f, starts[0] + x] = a_other[f, x]
                va[f, starts[1] + x] = b_other[f, x]
        write_pieces((va, vb), near, far, member)


def second_kernel(groups, mode, vel_ref, vec_ref, wall_ref, *refs):
    blocks, refs = refs[:4], refs[4:]
    if mode == 0:
        sponge_ref, target, base, va, vb = refs
    else:
        sponge_ref, other = refs[:2]
        pieces = refs[2 : 2 + MEMBERS]
        base, va, vb = refs[2 + MEMBERS :]
    group, member = position()
    for source, start in zip(blocks, block_starts(group)):
        for f in range(FIELDS):
            for x in range(DEEP):
                base[f, start + x] = source[f, x]
    vel = [vel_ref[d] for d in range(3)]
    vec = [vec_ref[f] for f in range(FIELDS)]
    run_step(1, base, va, vb, sponge_ref, wall_ref, vel, vec, group > 0, group < groups - 1)
    if mode == 0:
        for f in range(FIELDS):
            for x in range(2 * DEEP):
                target[f, x] = vb[f, DEEP + x]
    else:
        for d in range(MEMBERS):
            to = member ^ TURNS[d]
            row = pl.multiple_of((to % 4) * ROWS, ROWS)
            start = DEEP * (to // 4)
            for f in range(FIELDS):
                for x in range(DEEP):
                    pieces[d][0, f, x] = other[f, start + x, pl.ds(row, ROWS), :]
                    pieces[d][1, f, x] = vb[f, DEEP + start + x, pl.ds(row, ROWS), :]


def three_parts(a):
    high = a.astype(jnp.bfloat16)
    rest = a - high.astype(F32)
    middle = rest.astype(jnp.bfloat16)
    low = (rest - middle.astype(F32)).astype(jnp.bfloat16)
    return jnp.concatenate([high, middle, low], axis=0)


def chunk_of(ref, r):
    stride = FIELDS * DEEP * ROWS
    rows = [ref[pl.ds(CHUNK * r + n, 2 * MEMBERS, stride=stride), :] for n in range(CHUNK)]
    return jnp.concatenate(rows, axis=1)


def split_kernel(near, far, one, two, three, parts_ref, columns):
    _, member = position()
    tiles = FIELDS * DEEP
    for e, got in enumerate((None, one, two, three)):
        for b in range(2):
            other = member ^ (2 * e + b)
            for j in range(2):
                for f in range(FIELDS):
                    for x in range(DEEP):
                        at = ((2 * other + j) * tiles + f * DEEP + x) * ROWS
                        value = got[b, j, f, x] if e else (near, far)[b][0, j, f, x]
                        columns[pl.ds(pl.multiple_of(at, ROWS), ROWS), :] = value

    def body(r, carry):
        parts_ref[r] = three_parts(chunk_of(columns, r))
        return carry

    lax.fori_loop(0, parts_ref.shape[0], body, 0, unroll=4)


def gram_kernel(first_parts, *refs):
    second, (state_ref, gram_ref, columns) = refs[:MEMBERS], refs[MEMBERS:]
    _, member = position()
    tiles = FIELDS * DEEP
    for d in range(MEMBERS):
        other = member ^ TURNS[d]
        for j in range(2):
            start = (2 * other + j) * tiles * ROWS
            for f in range(FIELDS):
                for x in range(DEEP):
                    value = second[d][j, f, x]
                    at = pl.multiple_of(start + (f * DEEP + x) * ROWS, ROWS)
                    columns[pl.ds(at, ROWS), :] = value
                    state_ref[f, 2 * other + j, x] = value
    modes = 2 * MEMBERS

    def body(r, acc):
        parts = jnp.concatenate([first_parts[r], three_parts(chunk_of(columns, r))], axis=0)
        return acc + lax.dot_general(
            parts, parts, (((1,), (1,)), ((), ())), preferred_element_type=F32
        )

    acc = jnp.zeros((6 * modes, 6 * modes), F32)
    acc = lax.fori_loop(0, first_parts.shape[0], body, acc, unroll=4)

    def block(n, m):
        part = [modes * (3 * n + i) for i in range(3)], [modes * (3 * m + i) for i in range(3)]
        return sum(acc[r : r + modes, c : c + modes] for r in part[0] for c in part[1])

    rows = [jnp.concatenate([block(n, m) for m in range(STEPS)], axis=1) for n in range(STEPS)]
    tile = jnp.concatenate([line[ROWS * n : ROWS * n + ROWS] for line in rows for n in range(2)], axis=1)
    for n in range(gram_ref.shape[0]):
        gram_ref[n] = tile


def factor_kernel(total, parts_ref, factor_ref):
    acc = parts_ref[0]
    for n in range(1, parts_ref.shape[0]):
        acc = acc + parts_ref[n]
    acc = acc / total
    size = factor_ref.shape[0]
    a = jnp.concatenate([acc[:, size * n : size * n + size] for n in range(4)], axis=0)
    lines, pivots = [], []
    for k in range(0, size, 2):
        row0, row1 = a[k : k + 1, :], a[k + 1 : k + 2, :]
        pivot0, side, corner = row0[:, k : k + 1], row0[:, k + 1 : k + 2], row1[:, k + 1 : k + 2]
        ratio = side / pivot0
        pivot1 = corner - side * ratio
        row1 = row1 - ratio * row0
        lines += [row0, row1]
        pivots += [pivot0, pivot1]
        if k < size - 2:
            col0, col1 = a[:, k : k + 1], a[:, k + 1 : k + 2]
            a = a - col0 * (row0 / pivot0) - (col1 - ratio * col0) * (row1 / pivot1)
    factor = jnp.concatenate(lines, axis=0) / jnp.sqrt(jnp.concatenate(pivots, axis=0))
    row = lax.broadcasted_iota(jnp.int32, (size, size), 0)
    col = lax.broadcasted_iota(jnp.int32, (size, size), 1)
    factor_ref[...] = jnp.where(col >= row, factor, 0.0)


def local(state_in, sponge, mean_velocity, wall_vector, mode_shapes, wall_nodes, wall_weights, wall_count):
    gx_size, gy_size = lax.axis_size("gx"), lax.axis_size("gy")
    groups = gx_size // 2
    devices = gx_size * gy_size
    cells_x, cells_y, cells_z = state_in.shape[2:]
    def inside(d):
        return [(i, i ^ d) for i in range(devices)]

    def swap(first):
        moves = []
        for i in range(devices):
            g = i // MEMBERS
            target = g + 1 if (g % 2 == 0) == first else g - 1
            if 0 <= target < groups:
                moves.append((i, i + (target - g) * MEMBERS))
        return moves

    def exchange(a, b):
        return a, b, lax.ppermute(a, AXES, swap(True)), lax.ppermute(b, AXES, swap(False))

    def spread(pieces, at=0):
        turns = TURNS[at : at + len(pieces)]
        return [lax.ppermute(p, AXES, inside(d)) if d else p for p, d in zip(pieces, turns)]

    def call(kernel, name, micros, out_shape, inputs, scratch=(), scalars=0):
        return pl.pallas_call(
            kernel,
            out_shape=out_shape,
            in_specs=[SMEM] * scalars + [VMEM] * (len(inputs) - scalars),
            out_specs=[VMEM] * len(out_shape),
            scratch_shapes=scratch,
            compiler_params=PARAMS,
            cost_estimate=cost(micros),
            name=name,
        )(*inputs)

    def shape(*sizes):
        return jax.ShapeDtypeStruct(sizes, F32)

    *pieces, wall = pack(groups, state_in, sponge, wall_nodes, wall_weights, wall_count, mode_shapes)
    pieces = spread(pieces)
    wall, pieces[1] = lax.optimization_barrier((wall, pieces[1]))
    wall = lax.all_to_all(wall, AXES, 0, 0)
    messages = call(
        assemble_kernel,
        "assemble",
        1,
        [shape(4, STATE + DEEP, ROWS, LANES)] * 2 + [shape(4, STATE, ROWS, LANES)] * 2,
        pieces,
    )
    blocks = [exchange(*messages[:2]), exchange(*messages[2:])]
    walls = call(
        functools.partial(forcing_kernel, groups),
        "forcing",
        5.0,
        [shape(4 * DEEP, ROWS, LANES)] * 2,
        [wall],
    )
    field = [pltpu.VMEM((FIELDS, 4 * DEEP, 4 * ROWS, LANES), F32)] * 3
    border = shape(FIELDS, DEEP, 4 * ROWS, LANES)
    piece = shape(2, FIELDS, DEEP, ROWS, LANES)
    quarter = shape(MEMBERS // 2, 2, FIELDS, DEEP, ROWS, LANES)
    constants = (mean_velocity, wall_vector)
    a0, b0, sponge_ext = call(
        functools.partial(first_kernel, groups, 0),
        "first_step_0",
        5.0,
        [border, border, shape(4 * DEEP, 4 * ROWS, LANES)],
        (*constants, walls[0], *blocks[0]),
        field,
        2,
    )
    next_blocks = [exchange(a0, b0)]
    a1, b1, near, far = call(
        functools.partial(first_kernel, groups, 1),
        "first_step_1",
        5.0,
        [border, border, quarter, quarter],
        (*constants, walls[1], *blocks[1], sponge_ext, a0, b0),
        field,
        2,
    )
    next_blocks.append(exchange(a1, b1))
    far, _ = lax.optimization_barrier((far, next_blocks[0]))
    far = lax.ppermute(far, AXES, inside(1))
    merged = call(
        merge_kernel,
        "merge",
        1,
        [shape(2, 2, FIELDS, DEEP, ROWS, LANES)] * 3,
        [near, far],
    )
    first = [lax.ppermute(m, AXES, inside(2 * e + 2)) for e, m in enumerate(merged)]
    (second_0,) = call(
        functools.partial(second_kernel, groups, 0),
        "second_step_0",
        5.0,
        [shape(FIELDS, 2 * DEEP, 4 * ROWS, LANES)],
        (*constants, walls[0], *next_blocks[0], sponge_ext),
        field,
        2,
    )
    second = call(
        functools.partial(second_kernel, groups, 1),
        "second_step_1",
        5.0,
        [piece] * MEMBERS,
        (*constants, walls[1], *next_blocks[1], sponge_ext, second_0),
        field,
        2,
    )
    second = spread(second[:4]) + list(second[4:])
    second[4:], first = lax.optimization_barrier((second[4:], first))
    second[4:] = spread(second[4:], 4)

    row_count = FIELDS * DEEP * ROWS
    (parts,) = call(
        split_kernel,
        "split",
        2,
        [jax.ShapeDtypeStruct((row_count // CHUNK, 6 * MEMBERS, CHUNK * LANES), jnp.bfloat16)],
        [near, far, *first],
        [pltpu.VMEM((2 * MEMBERS * row_count, LANES), F32)],
    )
    rows_total = float(FIELDS * cells_x * gx_size * cells_y * gy_size * cells_z)
    snap_count = STEPS * 2 * MEMBERS
    state_out, grams = pl.pallas_call(
        gram_kernel,
        out_shape=[
            jax.ShapeDtypeStruct(state_in.shape, F32),
            jax.ShapeDtypeStruct((devices, ROWS, LANES), F32),
        ],
        in_specs=[VMEM] * (1 + MEMBERS),
        out_specs=[VMEM, VMEM],
        scratch_shapes=[pltpu.VMEM((2 * MEMBERS * row_count, LANES), F32)],
        compiler_params=PARAMS,
        name="gram",
    )(parts, *second)
    grams = lax.all_to_all(grams, AXES, 0, 0)
    factor = pl.pallas_call(
        functools.partial(factor_kernel, rows_total),
        out_shape=jax.ShapeDtypeStruct((snap_count, snap_count), F32),
        in_specs=[VMEM],
        out_specs=VMEM,
        compiler_params=PARAMS,
        name="factor",
    )(grams)
    return state_out, factor


def solution(mesh):
    placed = (
        P(None, None, "gx", "gy", None),
        P("gx", "gy", None),
        P(),
        P(),
        P(None, ("gx", "gy")),
        P(None, "gx", None),
        P(None, "gx", None),
        P("gx"),
    )
    return jax.shard_map(
        local,
        mesh=mesh,
        in_specs=placed,
        out_specs=(P(None, None, "gx", "gy", None), P()),
        check_vma=False,
    )
```

```python
import functools
import math

import jax
import jax.numpy as jnp
from jax import lax
from jax.experimental import pallas as pl
from jax.experimental.pallas import tpu as pltpu
from jax.sharding import PartitionSpec as P

STEPS = 2
NU_DAMP = 0.25
DT_STEP = 0.4
PULSE_MID = 0.8
PULSE_WIDTH = 0.5

AXES = ("gx", "gy")
FIELDS = 5
DEEP = 4
MEMBERS = 8
ROWS = 8
LANES = 128
STATE = FIELDS * DEEP
SPONGE = 2 * STATE
PIECE = SPONGE + DEEP
CHUNK = 4
F32 = jnp.float32
TURNS = (0, 1, 4, 2, 5, 3, 6, 7)

VMEM = pl.BlockSpec(memory_space=pltpu.VMEM)
SMEM = pl.BlockSpec(memory_space=pltpu.SMEM)
HBM = pl.BlockSpec(memory_space=pltpu.HBM)
PARAMS = pltpu.CompilerParams(vmem_limit_bytes=24 * 1024 * 1024)


def cost(micros):
    return pl.CostEstimate(flops=0, transcendentals=0, bytes_accessed=int(3.0e6 * micros))


def pulse(time_now):
    return math.exp(-(((time_now - PULSE_MID) / PULSE_WIDTH) ** 2))


def step_scales(step):
    start = step * DT_STEP
    p0, ph, p1 = pulse(start), pulse(start + 0.5 * DT_STEP), pulse(start + DT_STEP)
    return (
        (DT_STEP / 4.0, p0),
        (DT_STEP / 3.0, (p0 + ph) / 2.0),
        (DT_STEP / 2.0, (p0 + 2.0 * ph) / 3.0),
        (DT_STEP, (p0 + 4.0 * ph + p1) / 6.0),
    )


def position():
    along_x = lax.axis_index("gx")
    return along_x // 2, (along_x % 2) * 4 + lax.axis_index("gy")


def pack_kernel(groups, state_hbm, sponge_hbm, nodes_hbm, weights_hbm, count_hbm, shapes_hbm, *refs):
    pieces, wall = refs[:MEMBERS], refs[MEMBERS]
    sponge_ref, nodes_ref, weights_ref, count_ref, shapes_ref, sems = refs[MEMBERS + 1 :]
    _, member = position()
    row = member % 4
    small = [
        pltpu.make_async_copy(count_hbm, count_ref, sems.at[0]),
        pltpu.make_async_copy(nodes_hbm.at[row], nodes_ref, sems.at[1]),
        pltpu.make_async_copy(weights_hbm.at[row], weights_ref, sems.at[2]),
        pltpu.make_async_copy(sponge_hbm, sponge_ref, sems.at[3]),
        pltpu.make_async_copy(shapes_hbm, shapes_ref, sems.at[4]),
    ]
    large = []
    for n, piece in enumerate(pieces):
        for f in range(FIELDS):
            large.append(
                pltpu.make_async_copy(
                    state_hbm.at[f, pl.ds(2 * DEEP * (member ^ TURNS[n]), 2 * DEEP)],
                    piece.at[pl.ds(2 * DEEP * f, 2 * DEEP)],
                    sems.at[5 + n * FIELDS + f],
                )
            )
    for copy in small + large:
        copy.start()
    for copy in small:
        copy.wait()
    lane = lax.broadcasted_iota(jnp.int32, (1, LANES), 1)
    table = [nodes_ref[...].astype(F32)]
    for x in range(DEEP):
        kept = jnp.where(lane < count_ref[x], 1.0, 0.0)
        table.append(weights_ref[pl.ds(x, 1), :] * kept)
    table = jnp.concatenate(table, axis=0)
    for piece in pieces:
        for x in range(DEEP):
            piece[SPONGE + x] = sponge_ref[x]
    for m in range(MEMBERS):
        two = shapes_ref[2 * m : 2 * m + 2, :]
        lines = jnp.concatenate([two[:, :LANES], two[:, LANES:]] * 2, axis=0)
        for g in range(groups):
            wall[g * MEMBERS + m, 0] = lines
            wall[g * MEMBERS + m, 1] = table
    for copy in large:
        copy.wait()


def pack(groups, state_in, sponge, nodes, weights, count, shapes):
    inputs = (
        state_in.reshape(FIELDS, 2 * MEMBERS * DEEP, ROWS, LANES),
        sponge, nodes, weights, count, shapes,
    )
    return pl.pallas_call(
        functools.partial(pack_kernel, groups),
        out_shape=[jax.ShapeDtypeStruct((PIECE, ROWS, LANES), F32)] * MEMBERS
        + [jax.ShapeDtypeStruct((groups * MEMBERS, 2, ROWS, LANES), F32)],
        in_specs=[HBM] * 6,
        out_specs=[VMEM] * (MEMBERS + 1),
        scratch_shapes=[
            pltpu.VMEM(sponge.shape, F32),
            pltpu.VMEM(nodes.shape[1:], jnp.int32),
            pltpu.VMEM(weights.shape[1:], F32),
            pltpu.SMEM(count.shape, jnp.int32),
            pltpu.VMEM(shapes.shape, F32),
            pltpu.SemaphoreType.DMA((5 + MEMBERS * FIELDS,)),
        ],
        compiler_params=PARAMS,
        cost_estimate=cost(2),
        name="pack",
    )(*[pltpu.with_memory_space_constraint(x, pltpu.HBM) for x in inputs])


def assemble_kernel(*refs):
    pieces, targets = refs[:MEMBERS], refs[MEMBERS:]
    group, member = position()
    even = group % 2 == 0
    for d, piece in zip(TURNS, pieces):
        other = member ^ d
        is_first = (other >= 4) == even

        def copy(modes):
            for f in range(FIELDS):
                for j in range(2):
                    for x in range(DEEP):
                        modes[j][other % 4, f * DEEP + x] = piece[(f * 2 + j) * DEEP + x]
            for x in range(DEEP):
                modes[0][other % 4, STATE + x] = piece[SPONGE + x]

        @pl.when(is_first)
        def _():
            copy(targets[0::2])

        @pl.when(jnp.logical_not(is_first))
        def _():
            copy(targets[1::2])


def shifted_rows(tiles, sub):
    ahead = [pltpu.roll(t, ROWS - 1, 0) for t in tiles]
    behind = [pltpu.roll(t, 1, 0) for t in tiles]
    zero = jnp.zeros_like(tiles[0])
    last, first = sub == ROWS - 1, sub == 0
    count = len(tiles)
    north = [jnp.where(last, ahead[t + 1] if t + 1 < count else zero, ahead[t]) for t in range(count)]
    south = [jnp.where(first, behind[t - 1] if t > 0 else zero, behind[t]) for t in range(count)]
    return north, south


def run_stage(src, base, dst, sponge_ref, wall_ref, vel, wall_vec, h, scale, low, high):
    lane = lax.broadcasted_iota(jnp.int32, (ROWS, LANES), 1)
    sub = lax.broadcasted_iota(jnp.int32, (ROWS, LANES), 0)
    plus = [h * (NU_DAMP - 0.5 * v) for v in vel]
    minus = [h * (NU_DAMP + 0.5 * v) for v in vel]
    not_top, not_low = lane < LANES - 1, lane > 0
    plus_z = jnp.where(not_top, plus[2], 0.0)
    minus_z = jnp.where(not_low, minus[2], 0.0)
    flux = -0.5 * h
    flux_up = jnp.where(not_top, flux, 0.0)
    flux_low = jnp.where(not_low, flux, 0.0)
    tiles = range(4)

    def plane(i, carry):
        def load(ref, f, at):
            return [ref[f, at, pl.ds(ROWS * t, ROWS), :] for t in tiles]

        damp = [-h * (6.0 * NU_DAMP + sponge_ref[i, pl.ds(ROWS * t, ROWS), :]) for t in tiles]
        new = []
        for f in range(FIELDS):
            center = load(src, f, i)
            east, west = load(src, f, i + 1), load(src, f, i - 1)
            north, south = shifted_rows(center, sub)
            upper = [pltpu.roll(c, LANES - 1, 1) for c in center]
            lower = [pltpu.roll(c, 1, 1) for c in center]
            old = load(base, f, i)
            out = []
            for t in tiles:
                acc = old[t] + damp[t] * center[t]
                acc += plus[0] * east[t] + minus[0] * west[t]
                acc += plus[1] * north[t] + minus[1] * south[t]
                acc += plus_z * upper[t] + minus_z * lower[t]
                if t == 0:
                    acc += (h * scale * wall_vec[f]) * wall_ref[i]
                out.append(acc)
            new.append(out)
            if f == 1:
                d1 = [east[t] - west[t] for t in tiles]
            elif f == 2:
                d2 = [north[t] - south[t] for t in tiles]
            elif f == 3:
                d3 = [flux_up * upper[t] - flux_low * lower[t] for t in tiles]
            elif f == 4:
                for t in tiles:
                    new[1][t] += flux * (east[t] - west[t])
                    new[2][t] += flux * (north[t] - south[t])
                    new[3][t] += flux_up * upper[t] - flux_low * lower[t]
        for t in tiles:
            spread = flux * (d1[t] + d2[t]) + d3[t]
            new[0][t] += spread
            new[4][t] += spread
        for f in range(FIELDS):
            for t in tiles:
                dst[f, i, pl.ds(ROWS * t, ROWS), :] = new[f][t]
        return carry

    count = (high - low) // 2

    def half(n, carry):
        for k in range(count):
            plane(low + count * n + k, carry)
        return carry

    lax.fori_loop(0, 2, half, 0)


def run_step(step, base, va, vb, sponge_ref, wall_ref, vel, wall_vec, has_low, has_high):
    zero = jnp.zeros((ROWS, LANES), F32)
    src = base
    for k, (h, scale) in enumerate(step_scales(step)):
        dst = va if k % 2 == 0 else vb
        low, high = k + 1, 4 * DEEP - 1 - k
        run_stage(src, base, dst, sponge_ref, wall_ref, vel, wall_vec, h, scale, low, high)
        if k < 3:
            for there, at in ((has_low, DEEP - 1), (has_high, 3 * DEEP)):

                @pl.when(jnp.logical_not(there))
                def _():
                    for f in range(FIELDS):
                        for t in range(4):
                            dst[f, at, pl.ds(ROWS * t, ROWS), :] = zero

        src = dst


def write_pieces(sources, near, far, member):
    for flip, pieces in enumerate((near, far)):
        for e in range(MEMBERS // 2):
            to = member ^ (2 * e + flip)
            row = pl.multiple_of((to % 4) * ROWS, ROWS)
            start = DEEP + DEEP * (to // 4)
            for j, source in enumerate(sources):
                for f in range(FIELDS):
                    for x in range(DEEP):
                        pieces[e, j, f, x] = source[f, start + x, pl.ds(row, ROWS), :]


def merge_kernel(near, far, *targets):
    for e, target in enumerate(targets):
        for b, source in enumerate((near, far)):
            for j in range(2):
                for f in range(FIELDS):
                    for x in range(DEEP):
                        target[b, j, f, x] = source[e + 1, j, f, x]


def block_starts(group):
    even = group % 2 == 0
    return (
        jnp.where(even, 2 * DEEP, DEEP),
        jnp.where(even, DEEP, 2 * DEEP),
        jnp.where(even, 3 * DEEP, 0),
        jnp.where(even, 0, 3 * DEEP),
    )


def forcing_kernel(groups, parts, *walls):
    group, member = position()
    last = groups - 1
    tab = []
    for block in range(4):
        side = jnp.clip(group + (-1, 0, 0, 1)[block], 0, last)
        there = (group > 0, True, True, group < last)[block]
        for half in range(2):
            two = [parts[side * MEMBERS + (4, 0, 4, 0)[block] + 2 * half + n, 1] for n in range(2)]
            tab.append((two, there))
    zero = jnp.zeros((ROWS, LANES), F32)
    low_part, high_part, weights = [], [], []
    for two, there in tab:
        index = jnp.concatenate([two[0][:DEEP], two[1][:DEEP]], axis=0).astype(jnp.int32)
        weight = jnp.concatenate([two[0][DEEP:], two[1][DEEP:]], axis=0)
        weights.append(weight if there is True else jnp.where(there, weight, 0.0))
        low_part.append(index & (LANES - 1))
        high_part.append(index // LANES)
    count = len(weights)

    def body(q, taken):
        taken = [list(taken[j]) for j in range(2)]
        tile = parts[q, 0]
        for s in range(2):
            for j in range(2):
                line = jnp.broadcast_to(tile[2 * s + j : 2 * s + j + 1], (ROWS, LANES))
                for b in range(count):
                    value = jnp.take_along_axis(line, low_part[b], axis=1)
                    taken[j][b] = jnp.where(high_part[b] == 2 * q + s, value, taken[j][b])
        return tuple(tuple(t) for t in taken)

    start = tuple(tuple(zero for _ in range(count)) for _ in range(2))
    taken = lax.fori_loop(0, groups * MEMBERS, body, start)
    sub = lax.broadcasted_iota(jnp.int32, (ROWS, LANES), 0)
    for j in range(2):
        for block in range(4):
            total = sum(taken[j][2 * block + n] * weights[2 * block + n] for n in range(2))
            total = total[:DEEP] + total[DEEP:]
            for x in range(DEEP):
                line = jnp.broadcast_to(total[x : x + 1], (ROWS, LANES))
                walls[j][DEEP * block + x] = jnp.where(sub == 0, line, 0.0)


def first_kernel(groups, mode, vel_ref, vec_ref, wall_ref, *refs):
    blocks, refs = refs[:4], refs[4:]
    if mode == 0:
        a_ref, b_ref, sponge_ref, base, va, vb = refs
    else:
        sponge_ref, a_other, b_other, a_ref, b_ref, near, far, base, va, vb = refs
    group, member = position()
    starts = block_starts(group)
    for source, start in zip(blocks, starts):
        for y in range(4):
            rows = pl.ds(ROWS * y, ROWS)
            for f in range(FIELDS):
                for x in range(DEEP):
                    base[f, start + x, rows, :] = source[y, f * DEEP + x]
            if mode == 0:
                for x in range(DEEP):
                    sponge_ref[start + x, rows, :] = source[y, STATE + x]
    vel = [vel_ref[d] for d in range(3)]
    vec = [vec_ref[f] for f in range(FIELDS)]
    run_step(0, base, va, vb, sponge_ref, wall_ref, vel, vec, group > 0, group < groups - 1)
    for target, start in zip((a_ref, b_ref), starts):
        for f in range(FIELDS):
            for x in range(DEEP):
                target[f, x] = vb[f, start + x]
    if mode == 1:
        for f in range(FIELDS):
            for x in range(DEEP):
                va[f, starts[0] + x] = a_other[f, x]
                va[f, starts[1] + x] = b_other[f, x]
        write_pieces((va, vb), near, far, member)


def second_kernel(groups, mode, vel_ref, vec_ref, wall_ref, *refs):
    blocks, refs = refs[:4], refs[4:]
    if mode == 0:
        sponge_ref, target, base, va, vb = refs
    else:
        sponge_ref, other = refs[:2]
        pieces = refs[2 : 2 + MEMBERS]
        base, va, vb = refs[2 + MEMBERS :]
    group, member = position()
    for source, start in zip(blocks, block_starts(group)):
        for f in range(FIELDS):
            for x in range(DEEP):
                base[f, start + x] = source[f, x]
    vel = [vel_ref[d] for d in range(3)]
    vec = [vec_ref[f] for f in range(FIELDS)]
    run_step(1, base, va, vb, sponge_ref, wall_ref, vel, vec, group > 0, group < groups - 1)
    if mode == 0:
        for f in range(FIELDS):
            for x in range(2 * DEEP):
                target[f, x] = vb[f, DEEP + x]
    else:
        for d in range(MEMBERS):
            to = member ^ TURNS[d]
            row = pl.multiple_of((to % 4) * ROWS, ROWS)
            start = DEEP * (to // 4)
            for f in range(FIELDS):
                for x in range(DEEP):
                    pieces[d][0, f, x] = other[f, start + x, pl.ds(row, ROWS), :]
                    pieces[d][1, f, x] = vb[f, DEEP + start + x, pl.ds(row, ROWS), :]


def three_parts(a):
    high = a.astype(jnp.bfloat16)
    rest = a - high.astype(F32)
    middle = rest.astype(jnp.bfloat16)
    low = (rest - middle.astype(F32)).astype(jnp.bfloat16)
    return jnp.concatenate([high, middle, low], axis=0)


def chunk_of(ref, r):
    stride = FIELDS * DEEP * ROWS
    rows = [ref[pl.ds(CHUNK * r + n, 2 * MEMBERS, stride=stride), :] for n in range(CHUNK)]
    return jnp.concatenate(rows, axis=1)


def split_kernel(near, far, one, two, three, parts_ref, columns):
    _, member = position()
    tiles = FIELDS * DEEP
    for e, got in enumerate((None, one, two, three)):
        for b in range(2):
            other = member ^ (2 * e + b)
            for j in range(2):
                for f in range(FIELDS):
                    for x in range(DEEP):
                        at = ((2 * other + j) * tiles + f * DEEP + x) * ROWS
                        value = got[b, j, f, x] if e else (near, far)[b][0, j, f, x]
                        columns[pl.ds(pl.multiple_of(at, ROWS), ROWS), :] = value

    def body(r, carry):
        parts_ref[r] = three_parts(chunk_of(columns, r))
        return carry

    lax.fori_loop(0, parts_ref.shape[0], body, 0, unroll=4)


def gram_kernel(first_parts, *refs):
    second, (state_ref, gram_ref, columns) = refs[:MEMBERS], refs[MEMBERS:]
    _, member = position()
    tiles = FIELDS * DEEP
    for d in range(MEMBERS):
        other = member ^ TURNS[d]
        for j in range(2):
            start = (2 * other + j) * tiles * ROWS
            for f in range(FIELDS):
                for x in range(DEEP):
                    value = second[d][j, f, x]
                    at = pl.multiple_of(start + (f * DEEP + x) * ROWS, ROWS)
                    columns[pl.ds(at, ROWS), :] = value
                    state_ref[f, 2 * other + j, x] = value
    modes = 2 * MEMBERS

    def body(r, acc):
        parts = jnp.concatenate([first_parts[r], three_parts(chunk_of(columns, r))], axis=0)
        return acc + lax.dot_general(
            parts, parts, (((1,), (1,)), ((), ())), preferred_element_type=F32
        )

    acc = jnp.zeros((6 * modes, 6 * modes), F32)
    acc = lax.fori_loop(0, first_parts.shape[0], body, acc, unroll=4)

    def block(n, m):
        part = [modes * (3 * n + i) for i in range(3)], [modes * (3 * m + i) for i in range(3)]
        return sum(acc[r : r + modes, c : c + modes] for r in part[0] for c in part[1])

    rows = [jnp.concatenate([block(n, m) for m in range(STEPS)], axis=1) for n in range(STEPS)]
    tile = jnp.concatenate([line[ROWS * n : ROWS * n + ROWS] for line in rows for n in range(2)], axis=1)
    for n in range(gram_ref.shape[0]):
        gram_ref[n] = tile


def factor_kernel(total, parts_ref, factor_ref):
    acc = parts_ref[0]
    for n in range(1, parts_ref.shape[0]):
        acc = acc + parts_ref[n]
    acc = acc / total
    size = factor_ref.shape[0]
    a = jnp.concatenate([acc[:, size * n : size * n + size] for n in range(4)], axis=0)
    lines, pivots = [], []
    for k in range(0, size, 2):
        row0, row1 = a[k : k + 1, :], a[k + 1 : k + 2, :]
        pivot0, side, corner = row0[:, k : k + 1], row0[:, k + 1 : k + 2], row1[:, k + 1 : k + 2]
        ratio = side / pivot0
        pivot1 = corner - side * ratio
        row1 = row1 - ratio * row0
        lines += [row0, row1]
        pivots += [pivot0, pivot1]
        if k < size - 2:
            col0, col1 = a[:, k : k + 1], a[:, k + 1 : k + 2]
            a = a - col0 * (row0 / pivot0) - (col1 - ratio * col0) * (row1 / pivot1)
    factor = jnp.concatenate(lines, axis=0) / jnp.sqrt(jnp.concatenate(pivots, axis=0))
    row = lax.broadcasted_iota(jnp.int32, (size, size), 0)
    col = lax.broadcasted_iota(jnp.int32, (size, size), 1)
    factor_ref[...] = jnp.where(col >= row, factor, 0.0)


def local(state_in, sponge, mean_velocity, wall_vector, mode_shapes, wall_nodes, wall_weights, wall_count):
    gx_size, gy_size = lax.axis_size("gx"), lax.axis_size("gy")
    groups = gx_size // 2
    devices = gx_size * gy_size
    cells_x, cells_y, cells_z = state_in.shape[2:]
    def inside(d):
        return [(i, i ^ d) for i in range(devices)]

    def swap(first):
        moves = []
        for i in range(devices):
            g = i // MEMBERS
            target = g + 1 if (g % 2 == 0) == first else g - 1
            if 0 <= target < groups:
                moves.append((i, i + (target - g) * MEMBERS))
        return moves

    def exchange(a, b):
        return a, b, lax.ppermute(a, AXES, swap(True)), lax.ppermute(b, AXES, swap(False))

    def spread(pieces, at=0):
        turns = TURNS[at : at + len(pieces)]
        return [lax.ppermute(p, AXES, inside(d)) if d else p for p, d in zip(pieces, turns)]

    def call(kernel, name, micros, out_shape, inputs, scratch=(), scalars=0):
        return pl.pallas_call(
            kernel,
            out_shape=out_shape,
            in_specs=[SMEM] * scalars + [VMEM] * (len(inputs) - scalars),
            out_specs=[VMEM] * len(out_shape),
            scratch_shapes=scratch,
            compiler_params=PARAMS,
            cost_estimate=cost(micros),
            name=name,
        )(*inputs)

    def shape(*sizes):
        return jax.ShapeDtypeStruct(sizes, F32)

    *pieces, wall = pack(groups, state_in, sponge, wall_nodes, wall_weights, wall_count, mode_shapes)
    pieces = spread(pieces)
    wall, pieces[1] = lax.optimization_barrier((wall, pieces[1]))
    wall = lax.all_to_all(wall, AXES, 0, 0)
    messages = call(
        assemble_kernel,
        "assemble",
        1,
        [shape(4, STATE + DEEP, ROWS, LANES)] * 2 + [shape(4, STATE, ROWS, LANES)] * 2,
        pieces,
    )
    blocks = [exchange(*messages[:2]), exchange(*messages[2:])]
    walls = call(
        functools.partial(forcing_kernel, groups),
        "forcing",
        5.0,
        [shape(4 * DEEP, ROWS, LANES)] * 2,
        [wall],
    )
    field = [pltpu.VMEM((FIELDS, 4 * DEEP, 4 * ROWS, LANES), F32)] * 3
    border = shape(FIELDS, DEEP, 4 * ROWS, LANES)
    piece = shape(2, FIELDS, DEEP, ROWS, LANES)
    quarter = shape(MEMBERS // 2, 2, FIELDS, DEEP, ROWS, LANES)
    constants = (mean_velocity, wall_vector)
    a0, b0, sponge_ext = call(
        functools.partial(first_kernel, groups, 0),
        "first_step_0",
        5.0,
        [border, border, shape(4 * DEEP, 4 * ROWS, LANES)],
        (*constants, walls[0], *blocks[0]),
        field,
        2,
    )
    next_blocks = [exchange(a0, b0)]
    a1, b1, near, far = call(
        functools.partial(first_kernel, groups, 1),
        "first_step_1",
        5.0,
        [border, border, quarter, quarter],
        (*constants, walls[1], *blocks[1], sponge_ext, a0, b0),
        field,
        2,
    )
    next_blocks.append(exchange(a1, b1))
    far, _ = lax.optimization_barrier((far, next_blocks[0]))
    far = lax.ppermute(far, AXES, inside(1))
    merged = call(
        merge_kernel,
        "merge",
        1,
        [shape(2, 2, FIELDS, DEEP, ROWS, LANES)] * 3,
        [near, far],
    )
    first = [lax.ppermute(m, AXES, inside(2 * e + 2)) for e, m in enumerate(merged)]
    (second_0,) = call(
        functools.partial(second_kernel, groups, 0),
        "second_step_0",
        5.0,
        [shape(FIELDS, 2 * DEEP, 4 * ROWS, LANES)],
        (*constants, walls[0], *next_blocks[0], sponge_ext),
        field,
        2,
    )
    second = call(
        functools.partial(second_kernel, groups, 1),
        "second_step_1",
        5.0,
        [piece] * MEMBERS,
        (*constants, walls[1], *next_blocks[1], sponge_ext, second_0),
        field,
        2,
    )
    second = spread(second[:4]) + list(second[4:])
    second[4:], first = lax.optimization_barrier((second[4:], first))
    second[4:] = spread(second[4:], 4)

    row_count = FIELDS * DEEP * ROWS
    (parts,) = call(
        split_kernel,
        "split",
        2,
        [jax.ShapeDtypeStruct((row_count // CHUNK, 6 * MEMBERS, CHUNK * LANES), jnp.bfloat16)],
        [near, far, *first],
        [pltpu.VMEM((2 * MEMBERS * row_count, LANES), F32)],
    )
    rows_total = float(FIELDS * cells_x * gx_size * cells_y * gy_size * cells_z)
    snap_count = STEPS * 2 * MEMBERS
    state_out, grams = pl.pallas_call(
        gram_kernel,
        out_shape=[
            jax.ShapeDtypeStruct(state_in.shape, F32),
            jax.ShapeDtypeStruct((devices, ROWS, LANES), F32),
        ],
        in_specs=[VMEM] * (1 + MEMBERS),
        out_specs=[VMEM, VMEM],
        scratch_shapes=[pltpu.VMEM((2 * MEMBERS * row_count, LANES), F32)],
        compiler_params=PARAMS,
        name="gram",
    )(parts, *second)
    grams = lax.all_to_all(grams, AXES, 0, 0)
    factor = pl.pallas_call(
        functools.partial(factor_kernel, rows_total),
        out_shape=jax.ShapeDtypeStruct((snap_count, snap_count), F32),
        in_specs=[VMEM],
        out_specs=VMEM,
        compiler_params=PARAMS,
        name="factor",
    )(grams)
    return state_out, factor


def solution(mesh):
    placed = (
        P(None, None, "gx", "gy", None),
        P("gx", "gy", None),
        P(),
        P(),
        P(None, ("gx", "gy")),
        P(None, "gx", None),
        P(None, "gx", None),
        P("gx"),
    )
    return jax.shard_map(
        local,
        mesh=mesh,
        in_specs=placed,
        out_specs=(P(None, None, "gx", "gy", None), P()),
        check_vma=False,
    )
```

```python
import functools
import math

import jax
import jax.numpy as jnp
from jax import lax
from jax.experimental import pallas as pl
from jax.experimental.pallas import tpu as pltpu
from jax.sharding import PartitionSpec as P

STEPS = 2
NU_DAMP = 0.25
DT_STEP = 0.4
PULSE_MID = 0.8
PULSE_WIDTH = 0.5

AXES = ("gx", "gy")
FIELDS = 5
DEEP = 4
MEMBERS = 8
ROWS = 8
LANES = 128
STATE = FIELDS * DEEP
SPONGE = 2 * STATE
PIECE = SPONGE + DEEP
CHUNK = 4
F32 = jnp.float32
TURNS = (0, 1, 4, 2, 5, 3, 6, 7)

VMEM = pl.BlockSpec(memory_space=pltpu.VMEM)
SMEM = pl.BlockSpec(memory_space=pltpu.SMEM)
HBM = pl.BlockSpec(memory_space=pltpu.HBM)
PARAMS = pltpu.CompilerParams(vmem_limit_bytes=24 * 1024 * 1024)


def cost(micros):
    return pl.CostEstimate(flops=0, transcendentals=0, bytes_accessed=int(3.0e6 * micros))


def pulse(time_now):
    return math.exp(-(((time_now - PULSE_MID) / PULSE_WIDTH) ** 2))


def step_scales(step):
    start = step * DT_STEP
    p0, ph, p1 = pulse(start), pulse(start + 0.5 * DT_STEP), pulse(start + DT_STEP)
    return (
        (DT_STEP / 4.0, p0),
        (DT_STEP / 3.0, (p0 + ph) / 2.0),
        (DT_STEP / 2.0, (p0 + 2.0 * ph) / 3.0),
        (DT_STEP, (p0 + 4.0 * ph + p1) / 6.0),
    )


def position():
    along_x = lax.axis_index("gx")
    return along_x // 2, (along_x % 2) * 4 + lax.axis_index("gy")


def pack_kernel(groups, state_hbm, sponge_hbm, nodes_hbm, weights_hbm, count_hbm, shapes_hbm, *refs):
    pieces, wall = refs[:MEMBERS], refs[MEMBERS]
    sponge_ref, nodes_ref, weights_ref, count_ref, shapes_ref, sems = refs[MEMBERS + 1 :]
    _, member = position()
    row = member % 4
    small = [
        pltpu.make_async_copy(count_hbm, count_ref, sems.at[0]),
        pltpu.make_async_copy(nodes_hbm.at[row], nodes_ref, sems.at[1]),
        pltpu.make_async_copy(weights_hbm.at[row], weights_ref, sems.at[2]),
        pltpu.make_async_copy(sponge_hbm, sponge_ref, sems.at[3]),
        pltpu.make_async_copy(shapes_hbm, shapes_ref, sems.at[4]),
    ]
    large = []
    for n, piece in enumerate(pieces):
        for f in range(FIELDS):
            large.append(
                pltpu.make_async_copy(
                    state_hbm.at[f, pl.ds(2 * DEEP * (member ^ TURNS[n]), 2 * DEEP)],
                    piece.at[pl.ds(2 * DEEP * f, 2 * DEEP)],
                    sems.at[5 + n * FIELDS + f],
                )
            )
    for copy in small + large:
        copy.start()
    for copy in small:
        copy.wait()
    lane = lax.broadcasted_iota(jnp.int32, (1, LANES), 1)
    table = [nodes_ref[...].astype(F32)]
    for x in range(DEEP):
        kept = jnp.where(lane < count_ref[x], 1.0, 0.0)
        table.append(weights_ref[pl.ds(x, 1), :] * kept)
    table = jnp.concatenate(table, axis=0)
    for piece in pieces:
        for x in range(DEEP):
            piece[SPONGE + x] = sponge_ref[x]
    for m in range(MEMBERS):
        two = shapes_ref[2 * m : 2 * m + 2, :]
        lines = jnp.concatenate([two[:, :LANES], two[:, LANES:]] * 2, axis=0)
        for g in range(groups):
            wall[g * MEMBERS + m, 0] = lines
            wall[g * MEMBERS + m, 1] = table
    for copy in large:
        copy.wait()


def pack(groups, state_in, sponge, nodes, weights, count, shapes):
    inputs = (
        state_in.reshape(FIELDS, 2 * MEMBERS * DEEP, ROWS, LANES),
        sponge, nodes, weights, count, shapes,
    )
    return pl.pallas_call(
        functools.partial(pack_kernel, groups),
        out_shape=[jax.ShapeDtypeStruct((PIECE, ROWS, LANES), F32)] * MEMBERS
        + [jax.ShapeDtypeStruct((groups * MEMBERS, 2, ROWS, LANES), F32)],
        in_specs=[HBM] * 6,
        out_specs=[VMEM] * (MEMBERS + 1),
        scratch_shapes=[
            pltpu.VMEM(sponge.shape, F32),
            pltpu.VMEM(nodes.shape[1:], jnp.int32),
            pltpu.VMEM(weights.shape[1:], F32),
            pltpu.SMEM(count.shape, jnp.int32),
            pltpu.VMEM(shapes.shape, F32),
            pltpu.SemaphoreType.DMA((5 + MEMBERS * FIELDS,)),
        ],
        compiler_params=PARAMS,
        cost_estimate=cost(2),
        name="pack",
    )(*[pltpu.with_memory_space_constraint(x, pltpu.HBM) for x in inputs])


def assemble_kernel(*refs):
    pieces, targets = refs[:MEMBERS], refs[MEMBERS:]
    group, member = position()
    even = group % 2 == 0
    for d, piece in zip(TURNS, pieces):
        other = member ^ d
        is_first = (other >= 4) == even

        def copy(modes):
            for f in range(FIELDS):
                for j in range(2):
                    for x in range(DEEP):
                        modes[j][other % 4, f * DEEP + x] = piece[(f * 2 + j) * DEEP + x]
            for x in range(DEEP):
                modes[0][other % 4, STATE + x] = piece[SPONGE + x]

        @pl.when(is_first)
        def _():
            copy(targets[0::2])

        @pl.when(jnp.logical_not(is_first))
        def _():
            copy(targets[1::2])


def shifted_rows(tiles, sub):
    ahead = [pltpu.roll(t, ROWS - 1, 0) for t in tiles]
    behind = [pltpu.roll(t, 1, 0) for t in tiles]
    zero = jnp.zeros_like(tiles[0])
    last, first = sub == ROWS - 1, sub == 0
    count = len(tiles)
    north = [jnp.where(last, ahead[t + 1] if t + 1 < count else zero, ahead[t]) for t in range(count)]
    south = [jnp.where(first, behind[t - 1] if t > 0 else zero, behind[t]) for t in range(count)]
    return north, south


def run_stage(src, base, dst, sponge_ref, wall_ref, vel, wall_vec, h, scale, low, high):
    lane = lax.broadcasted_iota(jnp.int32, (ROWS, LANES), 1)
    sub = lax.broadcasted_iota(jnp.int32, (ROWS, LANES), 0)
    plus = [h * (NU_DAMP - 0.5 * v) for v in vel]
    minus = [h * (NU_DAMP + 0.5 * v) for v in vel]
    not_top, not_low = lane < LANES - 1, lane > 0
    plus_z = jnp.where(not_top, plus[2], 0.0)
    minus_z = jnp.where(not_low, minus[2], 0.0)
    flux = -0.5 * h
    flux_up = jnp.where(not_top, flux, 0.0)
    flux_low = jnp.where(not_low, flux, 0.0)
    tiles = range(4)

    def plane(i):
        def load(ref, f, at):
            return [ref[f, at, pl.ds(ROWS * t, ROWS), :] for t in tiles]

        damp = [-h * (6.0 * NU_DAMP + sponge_ref[i, pl.ds(ROWS * t, ROWS), :]) for t in tiles]
        new = []
        for f in range(FIELDS):
            center = load(src, f, i)
            east, west = load(src, f, i + 1), load(src, f, i - 1)
            north, south = shifted_rows(center, sub)
            upper = [pltpu.roll(c, LANES - 1, 1) for c in center]
            lower = [pltpu.roll(c, 1, 1) for c in center]
            old = load(base, f, i)
            out = []
            for t in tiles:
                acc = old[t] + damp[t] * center[t]
                acc += plus[0] * east[t] + minus[0] * west[t]
                acc += plus[1] * north[t] + minus[1] * south[t]
                acc += plus_z * upper[t] + minus_z * lower[t]
                if t == 0:
                    acc += (h * scale * wall_vec[f]) * wall_ref[i]
                out.append(acc)
            new.append(out)
            if f == 1:
                d1 = [east[t] - west[t] for t in tiles]
            elif f == 2:
                d2 = [north[t] - south[t] for t in tiles]
            elif f == 3:
                d3 = [flux_up * upper[t] - flux_low * lower[t] for t in tiles]
            elif f == 4:
                for t in tiles:
                    new[1][t] += flux * (east[t] - west[t])
                    new[2][t] += flux * (north[t] - south[t])
                    new[3][t] += flux_up * upper[t] - flux_low * lower[t]
        for t in tiles:
            spread = flux * (d1[t] + d2[t]) + d3[t]
            new[0][t] += spread
            new[4][t] += spread
        for f in range(FIELDS):
            for t in tiles:
                dst[f, i, pl.ds(ROWS * t, ROWS), :] = new[f][t]

    for i in range(low, high):
        plane(i)


def run_step(step, base, va, vb, sponge_ref, wall_ref, vel, wall_vec, has_low, has_high):
    zero = jnp.zeros((ROWS, LANES), F32)
    src = base
    for k, (h, scale) in enumerate(step_scales(step)):
        dst = va if k % 2 == 0 else vb
        low, high = k + 1, 4 * DEEP - 1 - k
        run_stage(src, base, dst, sponge_ref, wall_ref, vel, wall_vec, h, scale, low, high)
        if k < 3:
            for there, at in ((has_low, DEEP - 1), (has_high, 3 * DEEP)):

                @pl.when(jnp.logical_not(there))
                def _():
                    for f in range(FIELDS):
                        for t in range(4):
                            dst[f, at, pl.ds(ROWS * t, ROWS), :] = zero

        src = dst


def write_pieces(sources, near, far, member):
    for flip, pieces in enumerate((near, far)):
        for e in range(MEMBERS // 2):
            to = member ^ (2 * e + flip)
            row = pl.multiple_of((to % 4) * ROWS, ROWS)
            start = DEEP + DEEP * (to // 4)
            for j, source in enumerate(sources):
                for f in range(FIELDS):
                    for x in range(DEEP):
                        pieces[e, j, f, x] = source[f, start + x, pl.ds(row, ROWS), :]


def merge_kernel(near, far, *targets):
    for e, target in enumerate(targets):
        for b, source in enumerate((near, far)):
            for j in range(2):
                for f in range(FIELDS):
                    for x in range(DEEP):
                        target[b, j, f, x] = source[e + 1, j, f, x]


def block_starts(group):
    even = group % 2 == 0
    return (
        jnp.where(even, 2 * DEEP, DEEP),
        jnp.where(even, DEEP, 2 * DEEP),
        jnp.where(even, 3 * DEEP, 0),
        jnp.where(even, 0, 3 * DEEP),
    )


def forcing_kernel(groups, parts, *walls):
    group, member = position()
    last = groups - 1
    tab = []
    for block in range(4):
        side = jnp.clip(group + (-1, 0, 0, 1)[block], 0, last)
        there = (group > 0, True, True, group < last)[block]
        for half in range(2):
            two = [parts[side * MEMBERS + (4, 0, 4, 0)[block] + 2 * half + n, 1] for n in range(2)]
            tab.append((two, there))
    zero = jnp.zeros((ROWS, LANES), F32)
    low_part, high_part, weights = [], [], []
    for two, there in tab:
        index = jnp.concatenate([two[0][:DEEP], two[1][:DEEP]], axis=0).astype(jnp.int32)
        weight = jnp.concatenate([two[0][DEEP:], two[1][DEEP:]], axis=0)
        weights.append(weight if there is True else jnp.where(there, weight, 0.0))
        low_part.append(index & (LANES - 1))
        high_part.append(index // LANES)
    count = len(weights)

    def body(q, taken):
        taken = [list(taken[j]) for j in range(2)]
        tile = parts[q, 0]
        for s in range(2):
            for j in range(2):
                line = jnp.broadcast_to(tile[2 * s + j : 2 * s + j + 1], (ROWS, LANES))
                for b in range(count):
                    value = jnp.take_along_axis(line, low_part[b], axis=1)
                    taken[j][b] = jnp.where(high_part[b] == 2 * q + s, value, taken[j][b])
        return tuple(tuple(t) for t in taken)

    start = tuple(tuple(zero for _ in range(count)) for _ in range(2))
    taken = lax.fori_loop(0, groups * MEMBERS, body, start)
    sub = lax.broadcasted_iota(jnp.int32, (ROWS, LANES), 0)
    for j in range(2):
        for block in range(4):
            total = sum(taken[j][2 * block + n] * weights[2 * block + n] for n in range(2))
            total = total[:DEEP] + total[DEEP:]
            for x in range(DEEP):
                line = jnp.broadcast_to(total[x : x + 1], (ROWS, LANES))
                walls[j][DEEP * block + x] = jnp.where(sub == 0, line, 0.0)


def first_kernel(groups, mode, vel_ref, vec_ref, wall_ref, *refs):
    blocks, refs = refs[:4], refs[4:]
    if mode == 0:
        a_ref, b_ref, sponge_ref, base, va, vb = refs
    else:
        sponge_ref, a_other, b_other, a_ref, b_ref, near, far, base, va, vb = refs
    group, member = position()
    starts = block_starts(group)
    for source, start in zip(blocks, starts):
        for y in range(4):
            rows = pl.ds(ROWS * y, ROWS)
            for f in range(FIELDS):
                for x in range(DEEP):
                    base[f, start + x, rows, :] = source[y, f * DEEP + x]
            if mode == 0:
                for x in range(DEEP):
                    sponge_ref[start + x, rows, :] = source[y, STATE + x]
    vel = [vel_ref[d] for d in range(3)]
    vec = [vec_ref[f] for f in range(FIELDS)]
    run_step(0, base, va, vb, sponge_ref, wall_ref, vel, vec, group > 0, group < groups - 1)
    for target, start in zip((a_ref, b_ref), starts):
        for f in range(FIELDS):
            for x in range(DEEP):
                target[f, x] = vb[f, start + x]
    if mode == 1:
        for f in range(FIELDS):
            for x in range(DEEP):
                va[f, starts[0] + x] = a_other[f, x]
                va[f, starts[1] + x] = b_other[f, x]
        write_pieces((va, vb), near, far, member)


def second_kernel(groups, mode, vel_ref, vec_ref, wall_ref, *refs):
    blocks, refs = refs[:4], refs[4:]
    if mode == 0:
        sponge_ref, target, base, va, vb = refs
    else:
        sponge_ref, other = refs[:2]
        pieces = refs[2 : 2 + MEMBERS]
        base, va, vb = refs[2 + MEMBERS :]
    group, member = position()
    for source, start in zip(blocks, block_starts(group)):
        for f in range(FIELDS):
            for x in range(DEEP):
                base[f, start + x] = source[f, x]
    vel = [vel_ref[d] for d in range(3)]
    vec = [vec_ref[f] for f in range(FIELDS)]
    run_step(1, base, va, vb, sponge_ref, wall_ref, vel, vec, group > 0, group < groups - 1)
    if mode == 0:
        for f in range(FIELDS):
            for x in range(2 * DEEP):
                target[f, x] = vb[f, DEEP + x]
    else:
        for d in range(MEMBERS):
            to = member ^ TURNS[d]
            row = pl.multiple_of((to % 4) * ROWS, ROWS)
            start = DEEP * (to // 4)
            for f in range(FIELDS):
                for x in range(DEEP):
                    pieces[d][0, f, x] = other[f, start + x, pl.ds(row, ROWS), :]
                    pieces[d][1, f, x] = vb[f, DEEP + start + x, pl.ds(row, ROWS), :]


def three_parts(a):
    high = a.astype(jnp.bfloat16)
    rest = a - high.astype(F32)
    middle = rest.astype(jnp.bfloat16)
    low = (rest - middle.astype(F32)).astype(jnp.bfloat16)
    return jnp.concatenate([high, middle, low], axis=0)


def chunk_of(ref, r):
    stride = FIELDS * DEEP * ROWS
    rows = [ref[pl.ds(CHUNK * r + n, 2 * MEMBERS, stride=stride), :] for n in range(CHUNK)]
    return jnp.concatenate(rows, axis=1)


def split_kernel(near, far, one, two, three, parts_ref, columns):
    _, member = position()
    tiles = FIELDS * DEEP
    for e, got in enumerate((None, one, two, three)):
        for b in range(2):
            other = member ^ (2 * e + b)
            for j in range(2):
                for f in range(FIELDS):
                    for x in range(DEEP):
                        at = ((2 * other + j) * tiles + f * DEEP + x) * ROWS
                        value = got[b, j, f, x] if e else (near, far)[b][0, j, f, x]
                        columns[pl.ds(pl.multiple_of(at, ROWS), ROWS), :] = value

    def body(r, carry):
        parts_ref[r] = three_parts(chunk_of(columns, r))
        return carry

    lax.fori_loop(0, parts_ref.shape[0], body, 0, unroll=4)


def gram_kernel(first_parts, *refs):
    second, (state_ref, gram_ref, columns) = refs[:MEMBERS], refs[MEMBERS:]
    _, member = position()
    tiles = FIELDS * DEEP
    for d in range(MEMBERS):
        other = member ^ TURNS[d]
        for j in range(2):
            start = (2 * other + j) * tiles * ROWS
            for f in range(FIELDS):
                for x in range(DEEP):
                    value = second[d][j, f, x]
                    at = pl.multiple_of(start + (f * DEEP + x) * ROWS, ROWS)
                    columns[pl.ds(at, ROWS), :] = value
                    state_ref[f, 2 * other + j, x] = value
    modes = 2 * MEMBERS

    def body(r, acc):
        parts = jnp.concatenate([first_parts[r], three_parts(chunk_of(columns, r))], axis=0)
        return acc + lax.dot_general(
            parts, parts, (((1,), (1,)), ((), ())), preferred_element_type=F32
        )

    acc = jnp.zeros((6 * modes, 6 * modes), F32)
    acc = lax.fori_loop(0, first_parts.shape[0], body, acc, unroll=4)

    def block(n, m):
        part = [modes * (3 * n + i) for i in range(3)], [modes * (3 * m + i) for i in range(3)]
        return sum(acc[r : r + modes, c : c + modes] for r in part[0] for c in part[1])

    rows = [jnp.concatenate([block(n, m) for m in range(STEPS)], axis=1) for n in range(STEPS)]
    tile = jnp.concatenate([line[ROWS * n : ROWS * n + ROWS] for line in rows for n in range(2)], axis=1)
    for n in range(gram_ref.shape[0]):
        gram_ref[n] = tile


def factor_kernel(total, parts_ref, factor_ref):
    acc = parts_ref[0]
    for n in range(1, parts_ref.shape[0]):
        acc = acc + parts_ref[n]
    acc = acc / total
    size = factor_ref.shape[0]
    a = jnp.concatenate([acc[:, size * n : size * n + size] for n in range(4)], axis=0)
    lines, pivots = [], []
    for k in range(0, size, 2):
        row0, row1 = a[k : k + 1, :], a[k + 1 : k + 2, :]
        pivot0, side, corner = row0[:, k : k + 1], row0[:, k + 1 : k + 2], row1[:, k + 1 : k + 2]
        ratio = side / pivot0
        pivot1 = corner - side * ratio
        row1 = row1 - ratio * row0
        lines += [row0, row1]
        pivots += [pivot0, pivot1]
        if k < size - 2:
            col0, col1 = a[:, k : k + 1], a[:, k + 1 : k + 2]
            a = a - col0 * (row0 / pivot0) - (col1 - ratio * col0) * (row1 / pivot1)
    factor = jnp.concatenate(lines, axis=0) / jnp.sqrt(jnp.concatenate(pivots, axis=0))
    row = lax.broadcasted_iota(jnp.int32, (size, size), 0)
    col = lax.broadcasted_iota(jnp.int32, (size, size), 1)
    factor_ref[...] = jnp.where(col >= row, factor, 0.0)


def local(state_in, sponge, mean_velocity, wall_vector, mode_shapes, wall_nodes, wall_weights, wall_count):
    gx_size, gy_size = lax.axis_size("gx"), lax.axis_size("gy")
    groups = gx_size // 2
    devices = gx_size * gy_size
    cells_x, cells_y, cells_z = state_in.shape[2:]
    def inside(d):
        return [(i, i ^ d) for i in range(devices)]

    def swap(first):
        moves = []
        for i in range(devices):
            g = i // MEMBERS
            target = g + 1 if (g % 2 == 0) == first else g - 1
            if 0 <= target < groups:
                moves.append((i, i + (target - g) * MEMBERS))
        return moves

    def exchange(a, b):
        return a, b, lax.ppermute(a, AXES, swap(True)), lax.ppermute(b, AXES, swap(False))

    def spread(pieces, at=0):
        turns = TURNS[at : at + len(pieces)]
        return [lax.ppermute(p, AXES, inside(d)) if d else p for p, d in zip(pieces, turns)]

    def call(kernel, name, micros, out_shape, inputs, scratch=(), scalars=0):
        return pl.pallas_call(
            kernel,
            out_shape=out_shape,
            in_specs=[SMEM] * scalars + [VMEM] * (len(inputs) - scalars),
            out_specs=[VMEM] * len(out_shape),
            scratch_shapes=scratch,
            compiler_params=PARAMS,
            cost_estimate=cost(micros),
            name=name,
        )(*inputs)

    def shape(*sizes):
        return jax.ShapeDtypeStruct(sizes, F32)

    *pieces, wall = pack(groups, state_in, sponge, wall_nodes, wall_weights, wall_count, mode_shapes)
    pieces = spread(pieces)
    wall, pieces[1] = lax.optimization_barrier((wall, pieces[1]))
    wall = lax.all_to_all(wall, AXES, 0, 0)
    messages = call(
        assemble_kernel,
        "assemble",
        1,
        [shape(4, STATE + DEEP, ROWS, LANES)] * 2 + [shape(4, STATE, ROWS, LANES)] * 2,
        pieces,
    )
    blocks = [exchange(*messages[:2]), exchange(*messages[2:])]
    walls = call(
        functools.partial(forcing_kernel, groups),
        "forcing",
        5.0,
        [shape(4 * DEEP, ROWS, LANES)] * 2,
        [wall],
    )
    field = [pltpu.VMEM((FIELDS, 4 * DEEP, 4 * ROWS, LANES), F32)] * 3
    border = shape(FIELDS, DEEP, 4 * ROWS, LANES)
    piece = shape(2, FIELDS, DEEP, ROWS, LANES)
    quarter = shape(MEMBERS // 2, 2, FIELDS, DEEP, ROWS, LANES)
    constants = (mean_velocity, wall_vector)
    a0, b0, sponge_ext = call(
        functools.partial(first_kernel, groups, 0),
        "first_step_0",
        5.0,
        [border, border, shape(4 * DEEP, 4 * ROWS, LANES)],
        (*constants, walls[0], *blocks[0]),
        field,
        2,
    )
    next_blocks = [exchange(a0, b0)]
    a1, b1, near, far = call(
        functools.partial(first_kernel, groups, 1),
        "first_step_1",
        5.0,
        [border, border, quarter, quarter],
        (*constants, walls[1], *blocks[1], sponge_ext, a0, b0),
        field,
        2,
    )
    next_blocks.append(exchange(a1, b1))
    far, _ = lax.optimization_barrier((far, next_blocks[0]))
    far = lax.ppermute(far, AXES, inside(1))
    merged = call(
        merge_kernel,
        "merge",
        1,
        [shape(2, 2, FIELDS, DEEP, ROWS, LANES)] * 3,
        [near, far],
    )
    first = [lax.ppermute(m, AXES, inside(2 * e + 2)) for e, m in enumerate(merged)]
    (second_0,) = call(
        functools.partial(second_kernel, groups, 0),
        "second_step_0",
        5.0,
        [shape(FIELDS, 2 * DEEP, 4 * ROWS, LANES)],
        (*constants, walls[0], *next_blocks[0], sponge_ext),
        field,
        2,
    )
    second = call(
        functools.partial(second_kernel, groups, 1),
        "second_step_1",
        5.0,
        [piece] * MEMBERS,
        (*constants, walls[1], *next_blocks[1], sponge_ext, second_0),
        field,
        2,
    )
    second = spread(second[:5]) + list(second[5:])
    second[5:], first = lax.optimization_barrier((second[5:], first))
    second[5:] = spread(second[5:], 5)

    row_count = FIELDS * DEEP * ROWS
    (parts,) = call(
        split_kernel,
        "split",
        2,
        [jax.ShapeDtypeStruct((row_count // CHUNK, 6 * MEMBERS, CHUNK * LANES), jnp.bfloat16)],
        [near, far, *first],
        [pltpu.VMEM((2 * MEMBERS * row_count, LANES), F32)],
    )
    rows_total = float(FIELDS * cells_x * gx_size * cells_y * gy_size * cells_z)
    snap_count = STEPS * 2 * MEMBERS
    state_out, grams = pl.pallas_call(
        gram_kernel,
        out_shape=[
            jax.ShapeDtypeStruct(state_in.shape, F32),
            jax.ShapeDtypeStruct((devices, ROWS, LANES), F32),
        ],
        in_specs=[VMEM] * (1 + MEMBERS),
        out_specs=[VMEM, VMEM],
        scratch_shapes=[pltpu.VMEM((2 * MEMBERS * row_count, LANES), F32)],
        compiler_params=PARAMS,
        name="gram",
    )(parts, *second)
    grams = lax.all_to_all(grams, AXES, 0, 0)
    factor = pl.pallas_call(
        functools.partial(factor_kernel, rows_total),
        out_shape=jax.ShapeDtypeStruct((snap_count, snap_count), F32),
        in_specs=[VMEM],
        out_specs=VMEM,
        compiler_params=PARAMS,
        name="factor",
    )(grams)
    return state_out, factor


def solution(mesh):
    placed = (
        P(None, None, "gx", "gy", None),
        P("gx", "gy", None),
        P(),
        P(),
        P(None, ("gx", "gy")),
        P(None, "gx", None),
        P(None, "gx", None),
        P("gx"),
    )
    return jax.shard_map(
        local,
        mesh=mesh,
        in_specs=placed,
        out_specs=(P(None, None, "gx", "gy", None), P()),
        check_vma=False,
    )
```

```python
import functools
import math

import jax
import jax.numpy as jnp
from jax import lax
from jax.experimental import pallas as pl
from jax.experimental.pallas import tpu as pltpu
from jax.sharding import PartitionSpec as P

STEPS = 2
NU_DAMP = 0.25
DT_STEP = 0.4
PULSE_MID = 0.8
PULSE_WIDTH = 0.5

AXES = ("gx", "gy")
FIELDS = 5
DEEP = 4
MEMBERS = 8
ROWS = 8
LANES = 128
STATE = FIELDS * DEEP
SPONGE = 2 * STATE
PIECE = SPONGE + DEEP
CHUNK = 4
F32 = jnp.float32
TURNS = (0, 1, 4, 2, 5, 3, 6, 7)

VMEM = pl.BlockSpec(memory_space=pltpu.VMEM)
SMEM = pl.BlockSpec(memory_space=pltpu.SMEM)
HBM = pl.BlockSpec(memory_space=pltpu.HBM)
PARAMS = pltpu.CompilerParams(vmem_limit_bytes=24 * 1024 * 1024)


def cost(micros):
    return pl.CostEstimate(flops=0, transcendentals=0, bytes_accessed=int(3.0e6 * micros))


def pulse(time_now):
    return math.exp(-(((time_now - PULSE_MID) / PULSE_WIDTH) ** 2))


def step_scales(step):
    start = step * DT_STEP
    p0, ph, p1 = pulse(start), pulse(start + 0.5 * DT_STEP), pulse(start + DT_STEP)
    return (
        (DT_STEP / 4.0, p0),
        (DT_STEP / 3.0, (p0 + ph) / 2.0),
        (DT_STEP / 2.0, (p0 + 2.0 * ph) / 3.0),
        (DT_STEP, (p0 + 4.0 * ph + p1) / 6.0),
    )


def position():
    along_x = lax.axis_index("gx")
    return along_x // 2, (along_x % 2) * 4 + lax.axis_index("gy")


def pack_kernel(groups, state_hbm, sponge_hbm, nodes_hbm, weights_hbm, count_hbm, shapes_hbm, *refs):
    pieces, wall = refs[:MEMBERS], refs[MEMBERS]
    sponge_ref, nodes_ref, weights_ref, count_ref, shapes_ref, sems = refs[MEMBERS + 1 :]
    _, member = position()
    row = member % 4
    small = [
        pltpu.make_async_copy(count_hbm, count_ref, sems.at[0]),
        pltpu.make_async_copy(nodes_hbm.at[row], nodes_ref, sems.at[1]),
        pltpu.make_async_copy(weights_hbm.at[row], weights_ref, sems.at[2]),
        pltpu.make_async_copy(sponge_hbm, sponge_ref, sems.at[3]),
        pltpu.make_async_copy(shapes_hbm, shapes_ref, sems.at[4]),
    ]
    large = []
    for n, piece in enumerate(pieces):
        for f in range(FIELDS):
            large.append(
                pltpu.make_async_copy(
                    state_hbm.at[f, pl.ds(2 * DEEP * (member ^ TURNS[n]), 2 * DEEP)],
                    piece.at[pl.ds(2 * DEEP * f, 2 * DEEP)],
                    sems.at[5 + n * FIELDS + f],
                )
            )
    for copy in small + large:
        copy.start()
    for copy in small:
        copy.wait()
    lane = lax.broadcasted_iota(jnp.int32, (1, LANES), 1)
    table = [nodes_ref[...].astype(F32)]
    for x in range(DEEP):
        kept = jnp.where(lane < count_ref[x], 1.0, 0.0)
        table.append(weights_ref[pl.ds(x, 1), :] * kept)
    table = jnp.concatenate(table, axis=0)
    for piece in pieces:
        for x in range(DEEP):
            piece[SPONGE + x] = sponge_ref[x]
    for m in range(MEMBERS):
        two = shapes_ref[2 * m : 2 * m + 2, :]
        lines = jnp.concatenate([two[:, :LANES], two[:, LANES:]] * 2, axis=0)
        for g in range(groups):
            wall[g * MEMBERS + m, 0] = lines
            wall[g * MEMBERS + m, 1] = table
    for copy in large:
        copy.wait()


def pack(groups, state_in, sponge, nodes, weights, count, shapes):
    inputs = (
        state_in.reshape(FIELDS, 2 * MEMBERS * DEEP, ROWS, LANES),
        sponge, nodes, weights, count, shapes,
    )
    return pl.pallas_call(
        functools.partial(pack_kernel, groups),
        out_shape=[jax.ShapeDtypeStruct((PIECE, ROWS, LANES), F32)] * MEMBERS
        + [jax.ShapeDtypeStruct((groups * MEMBERS, 2, ROWS, LANES), F32)],
        in_specs=[HBM] * 6,
        out_specs=[VMEM] * (MEMBERS + 1),
        scratch_shapes=[
            pltpu.VMEM(sponge.shape, F32),
            pltpu.VMEM(nodes.shape[1:], jnp.int32),
            pltpu.VMEM(weights.shape[1:], F32),
            pltpu.SMEM(count.shape, jnp.int32),
            pltpu.VMEM(shapes.shape, F32),
            pltpu.SemaphoreType.DMA((5 + MEMBERS * FIELDS,)),
        ],
        compiler_params=PARAMS,
        cost_estimate=cost(2),
        name="pack",
    )(*[pltpu.with_memory_space_constraint(x, pltpu.HBM) for x in inputs])


def assemble_kernel(*refs):
    pieces, targets = refs[:MEMBERS], refs[MEMBERS:]
    group, member = position()
    even = group % 2 == 0
    for d, piece in zip(TURNS, pieces):
        other = member ^ d
        is_first = (other >= 4) == even

        def copy(modes):
            for f in range(FIELDS):
                for j in range(2):
                    for x in range(DEEP):
                        modes[j][other % 4, f * DEEP + x] = piece[(f * 2 + j) * DEEP + x]
            for x in range(DEEP):
                modes[0][other % 4, STATE + x] = piece[SPONGE + x]

        @pl.when(is_first)
        def _():
            copy(targets[0::2])

        @pl.when(jnp.logical_not(is_first))
        def _():
            copy(targets[1::2])


def shifted_rows(tiles, sub):
    ahead = [pltpu.roll(t, ROWS - 1, 0) for t in tiles]
    behind = [pltpu.roll(t, 1, 0) for t in tiles]
    zero = jnp.zeros_like(tiles[0])
    last, first = sub == ROWS - 1, sub == 0
    count = len(tiles)
    north = [jnp.where(last, ahead[t + 1] if t + 1 < count else zero, ahead[t]) for t in range(count)]
    south = [jnp.where(first, behind[t - 1] if t > 0 else zero, behind[t]) for t in range(count)]
    return north, south


def run_stage(src, base, dst, sponge_ref, wall_ref, vel, wall_vec, h, scale, low, high):
    lane = lax.broadcasted_iota(jnp.int32, (ROWS, LANES), 1)
    sub = lax.broadcasted_iota(jnp.int32, (ROWS, LANES), 0)
    plus = [h * (NU_DAMP - 0.5 * v) for v in vel]
    minus = [h * (NU_DAMP + 0.5 * v) for v in vel]
    not_top, not_low = lane < LANES - 1, lane > 0
    plus_z = jnp.where(not_top, plus[2], 0.0)
    minus_z = jnp.where(not_low, minus[2], 0.0)
    flux = -0.5 * h
    flux_up = jnp.where(not_top, flux, 0.0)
    flux_low = jnp.where(not_low, flux, 0.0)
    tiles = range(4)

    def plane(i, carry):
        def load(ref, f, at):
            return [ref[f, at, pl.ds(ROWS * t, ROWS), :] for t in tiles]

        damp = [-h * (6.0 * NU_DAMP + sponge_ref[i, pl.ds(ROWS * t, ROWS), :]) for t in tiles]
        new = []
        for f in range(FIELDS):
            center = load(src, f, i)
            east, west = load(src, f, i + 1), load(src, f, i - 1)
            north, south = shifted_rows(center, sub)
            upper = [pltpu.roll(c, LANES - 1, 1) for c in center]
            lower = [pltpu.roll(c, 1, 1) for c in center]
            old = load(base, f, i)
            out = []
            for t in tiles:
                acc = old[t] + damp[t] * center[t]
                acc += plus[0] * east[t] + minus[0] * west[t]
                acc += plus[1] * north[t] + minus[1] * south[t]
                acc += plus_z * upper[t] + minus_z * lower[t]
                if t == 0:
                    acc += (h * scale * wall_vec[f]) * wall_ref[i]
                out.append(acc)
            new.append(out)
            if f == 1:
                d1 = [east[t] - west[t] for t in tiles]
            elif f == 2:
                d2 = [north[t] - south[t] for t in tiles]
            elif f == 3:
                d3 = [flux_up * upper[t] - flux_low * lower[t] for t in tiles]
            elif f == 4:
                for t in tiles:
                    new[1][t] += flux * (east[t] - west[t])
                    new[2][t] += flux * (north[t] - south[t])
                    new[3][t] += flux_up * upper[t] - flux_low * lower[t]
        for t in tiles:
            spread = flux * (d1[t] + d2[t]) + d3[t]
            new[0][t] += spread
            new[4][t] += spread
        for f in range(FIELDS):
            for t in tiles:
                dst[f, i, pl.ds(ROWS * t, ROWS), :] = new[f][t]
        return carry

    count = (high - low) // 2

    def half(n, carry):
        for k in range(count):
            plane(low + count * n + k, carry)
        return carry

    lax.fori_loop(0, 2, half, 0)


def run_step(step, base, va, vb, sponge_ref, wall_ref, vel, wall_vec, has_low, has_high):
    zero = jnp.zeros((ROWS, LANES), F32)
    src = base
    for k, (h, scale) in enumerate(step_scales(step)):
        dst = va if k % 2 == 0 else vb
        low, high = k + 1, 4 * DEEP - 1 - k
        run_stage(src, base, dst, sponge_ref, wall_ref, vel, wall_vec, h, scale, low, high)
        if k < 3:
            for there, at in ((has_low, DEEP - 1), (has_high, 3 * DEEP)):

                @pl.when(jnp.logical_not(there))
                def _():
                    for f in range(FIELDS):
                        for t in range(4):
                            dst[f, at, pl.ds(ROWS * t, ROWS), :] = zero

        src = dst


def write_pieces(sources, near, far, member):
    for flip, pieces in enumerate((near, far)):
        for e in range(MEMBERS // 2):
            to = member ^ (2 * e + flip)
            row = pl.multiple_of((to % 4) * ROWS, ROWS)
            start = DEEP + DEEP * (to // 4)
            for j, source in enumerate(sources):
                for f in range(FIELDS):
                    for x in range(DEEP):
                        pieces[e, j, f, x] = source[f, start + x, pl.ds(row, ROWS), :]


def merge_kernel(near, far, *targets):
    for e, target in enumerate(targets):
        for b, source in enumerate((near, far)):
            for j in range(2):
                for f in range(FIELDS):
                    for x in range(DEEP):
                        target[b, j, f, x] = source[MEMBERS // 2 - 1 - e, j, f, x]


def block_starts(group):
    even = group % 2 == 0
    return (
        jnp.where(even, 2 * DEEP, DEEP),
        jnp.where(even, DEEP, 2 * DEEP),
        jnp.where(even, 3 * DEEP, 0),
        jnp.where(even, 0, 3 * DEEP),
    )


def forcing_kernel(groups, parts, *walls):
    group, member = position()
    last = groups - 1
    tab = []
    for block in range(4):
        side = jnp.clip(group + (-1, 0, 0, 1)[block], 0, last)
        there = (group > 0, True, True, group < last)[block]
        for half in range(2):
            two = [parts[side * MEMBERS + (4, 0, 4, 0)[block] + 2 * half + n, 1] for n in range(2)]
            tab.append((two, there))
    zero = jnp.zeros((ROWS, LANES), F32)
    low_part, high_part, weights = [], [], []
    for two, there in tab:
        index = jnp.concatenate([two[0][:DEEP], two[1][:DEEP]], axis=0).astype(jnp.int32)
        weight = jnp.concatenate([two[0][DEEP:], two[1][DEEP:]], axis=0)
        weights.append(weight if there is True else jnp.where(there, weight, 0.0))
        low_part.append(index & (LANES - 1))
        high_part.append(index // LANES)
    count = len(weights)

    def body(q, taken):
        taken = [list(taken[j]) for j in range(2)]
        tile = parts[q, 0]
        for s in range(2):
            for j in range(2):
                line = jnp.broadcast_to(tile[2 * s + j : 2 * s + j + 1], (ROWS, LANES))
                for b in range(count):
                    value = jnp.take_along_axis(line, low_part[b], axis=1)
                    taken[j][b] = jnp.where(high_part[b] == 2 * q + s, value, taken[j][b])
        return tuple(tuple(t) for t in taken)

    start = tuple(tuple(zero for _ in range(count)) for _ in range(2))
    taken = lax.fori_loop(0, groups * MEMBERS, body, start)
    sub = lax.broadcasted_iota(jnp.int32, (ROWS, LANES), 0)
    for j in range(2):
        for block in range(4):
            total = sum(taken[j][2 * block + n] * weights[2 * block + n] for n in range(2))
            total = total[:DEEP] + total[DEEP:]
            for x in range(DEEP):
                line = jnp.broadcast_to(total[x : x + 1], (ROWS, LANES))
                walls[j][DEEP * block + x] = jnp.where(sub == 0, line, 0.0)


def first_kernel(groups, mode, vel_ref, vec_ref, wall_ref, *refs):
    blocks, refs = refs[:4], refs[4:]
    if mode == 0:
        a_ref, b_ref, sponge_ref, base, va, vb = refs
    else:
        sponge_ref, a_other, b_other, a_ref, b_ref, near, far, base, va, vb = refs
    group, member = position()
    starts = block_starts(group)
    for source, start in zip(blocks, starts):
        for y in range(4):
            rows = pl.ds(ROWS * y, ROWS)
            for f in range(FIELDS):
                for x in range(DEEP):
                    base[f, start + x, rows, :] = source[y, f * DEEP + x]
            if mode == 0:
                for x in range(DEEP):
                    sponge_ref[start + x, rows, :] = source[y, STATE + x]
    vel = [vel_ref[d] for d in range(3)]
    vec = [vec_ref[f] for f in range(FIELDS)]
    run_step(0, base, va, vb, sponge_ref, wall_ref, vel, vec, group > 0, group < groups - 1)
    for target, start in zip((a_ref, b_ref), starts):
        for f in range(FIELDS):
            for x in range(DEEP):
                target[f, x] = vb[f, start + x]
    if mode == 1:
        for f in range(FIELDS):
            for x in range(DEEP):
                va[f, starts[0] + x] = a_other[f, x]
                va[f, starts[1] + x] = b_other[f, x]
        write_pieces((va, vb), near, far, member)


def second_kernel(groups, mode, vel_ref, vec_ref, wall_ref, *refs):
    blocks, refs = refs[:4], refs[4:]
    if mode == 0:
        sponge_ref, target, base, va, vb = refs
    else:
        sponge_ref, other = refs[:2]
        pieces = refs[2 : 2 + MEMBERS]
        base, va, vb = refs[2 + MEMBERS :]
    group, member = position()
    for source, start in zip(blocks, block_starts(group)):
        for f in range(FIELDS):
            for x in range(DEEP):
                base[f, start + x] = source[f, x]
    vel = [vel_ref[d] for d in range(3)]
    vec = [vec_ref[f] for f in range(FIELDS)]
    run_step(1, base, va, vb, sponge_ref, wall_ref, vel, vec, group > 0, group < groups - 1)
    if mode == 0:
        for f in range(FIELDS):
            for x in range(2 * DEEP):
                target[f, x] = vb[f, DEEP + x]
    else:
        for d in range(MEMBERS):
            to = member ^ TURNS[d]
            row = pl.multiple_of((to % 4) * ROWS, ROWS)
            start = DEEP * (to // 4)
            for f in range(FIELDS):
                for x in range(DEEP):
                    pieces[d][0, f, x] = other[f, start + x, pl.ds(row, ROWS), :]
                    pieces[d][1, f, x] = vb[f, DEEP + start + x, pl.ds(row, ROWS), :]


def three_parts(a):
    high = a.astype(jnp.bfloat16)
    rest = a - high.astype(F32)
    middle = rest.astype(jnp.bfloat16)
    low = (rest - middle.astype(F32)).astype(jnp.bfloat16)
    return jnp.concatenate([high, middle, low], axis=0)


def chunk_of(ref, r):
    stride = FIELDS * DEEP * ROWS
    rows = [ref[pl.ds(CHUNK * r + n, 2 * MEMBERS, stride=stride), :] for n in range(CHUNK)]
    return jnp.concatenate(rows, axis=1)


def split_kernel(near, far, one, two, three, parts_ref, columns):
    _, member = position()
    tiles = FIELDS * DEEP
    for e, got in ((0, None), (3, one), (2, two), (1, three)):
        for b in range(2):
            other = member ^ (2 * e + b)
            for j in range(2):
                for f in range(FIELDS):
                    for x in range(DEEP):
                        at = ((2 * other + j) * tiles + f * DEEP + x) * ROWS
                        value = got[b, j, f, x] if e else (near, far)[b][0, j, f, x]
                        columns[pl.ds(pl.multiple_of(at, ROWS), ROWS), :] = value

    def body(r, carry):
        parts_ref[r] = three_parts(chunk_of(columns, r))
        return carry

    lax.fori_loop(0, parts_ref.shape[0], body, 0, unroll=4)


def gram_kernel(first_parts, *refs):
    second, (state_ref, gram_ref, columns) = refs[:MEMBERS], refs[MEMBERS:]
    _, member = position()
    tiles = FIELDS * DEEP
    for d in range(MEMBERS):
        other = member ^ TURNS[d]
        for j in range(2):
            start = (2 * other + j) * tiles * ROWS
            for f in range(FIELDS):
                for x in range(DEEP):
                    value = second[d][j, f, x]
                    at = pl.multiple_of(start + (f * DEEP + x) * ROWS, ROWS)
                    columns[pl.ds(at, ROWS), :] = value
                    state_ref[f, 2 * other + j, x] = value
    modes = 2 * MEMBERS

    def body(r, acc):
        parts = jnp.concatenate([first_parts[r], three_parts(chunk_of(columns, r))], axis=0)
        return acc + lax.dot_general(
            parts, parts, (((1,), (1,)), ((), ())), preferred_element_type=F32
        )

    acc = jnp.zeros((6 * modes, 6 * modes), F32)
    acc = lax.fori_loop(0, first_parts.shape[0], body, acc, unroll=4)

    def block(n, m):
        part = [modes * (3 * n + i) for i in range(3)], [modes * (3 * m + i) for i in range(3)]
        return sum(acc[r : r + modes, c : c + modes] for r in part[0] for c in part[1])

    rows = [jnp.concatenate([block(n, m) for m in range(STEPS)], axis=1) for n in range(STEPS)]
    tile = jnp.concatenate([line[ROWS * n : ROWS * n + ROWS] for line in rows for n in range(2)], axis=1)
    for n in range(gram_ref.shape[0]):
        gram_ref[n] = tile


def factor_kernel(total, parts_ref, factor_ref):
    acc = parts_ref[0]
    for n in range(1, parts_ref.shape[0]):
        acc = acc + parts_ref[n]
    acc = acc / total
    size = factor_ref.shape[0]
    a = jnp.concatenate([acc[:, size * n : size * n + size] for n in range(4)], axis=0)
    lines, pivots = [], []
    for k in range(0, size, 2):
        row0, row1 = a[k : k + 1, :], a[k + 1 : k + 2, :]
        pivot0, side, corner = row0[:, k : k + 1], row0[:, k + 1 : k + 2], row1[:, k + 1 : k + 2]
        ratio = side / pivot0
        pivot1 = corner - side * ratio
        row1 = row1 - ratio * row0
        lines += [row0, row1]
        pivots += [pivot0, pivot1]
        if k < size - 2:
            col0, col1 = a[:, k : k + 1], a[:, k + 1 : k + 2]
            a = a - col0 * (row0 / pivot0) - (col1 - ratio * col0) * (row1 / pivot1)
    factor = jnp.concatenate(lines, axis=0) / jnp.sqrt(jnp.concatenate(pivots, axis=0))
    row = lax.broadcasted_iota(jnp.int32, (size, size), 0)
    col = lax.broadcasted_iota(jnp.int32, (size, size), 1)
    factor_ref[...] = jnp.where(col >= row, factor, 0.0)


def local(state_in, sponge, mean_velocity, wall_vector, mode_shapes, wall_nodes, wall_weights, wall_count):
    gx_size, gy_size = lax.axis_size("gx"), lax.axis_size("gy")
    groups = gx_size // 2
    devices = gx_size * gy_size
    cells_x, cells_y, cells_z = state_in.shape[2:]
    def inside(d):
        return [(i, i ^ d) for i in range(devices)]

    def swap(first):
        moves = []
        for i in range(devices):
            g = i // MEMBERS
            target = g + 1 if (g % 2 == 0) == first else g - 1
            if 0 <= target < groups:
                moves.append((i, i + (target - g) * MEMBERS))
        return moves

    def exchange(a, b):
        return a, b, lax.ppermute(a, AXES, swap(True)), lax.ppermute(b, AXES, swap(False))

    def spread(pieces, at=0):
        turns = TURNS[at : at + len(pieces)]
        return [lax.ppermute(p, AXES, inside(d)) if d else p for p, d in zip(pieces, turns)]

    def call(kernel, name, micros, out_shape, inputs, scratch=(), scalars=0):
        return pl.pallas_call(
            kernel,
            out_shape=out_shape,
            in_specs=[SMEM] * scalars + [VMEM] * (len(inputs) - scalars),
            out_specs=[VMEM] * len(out_shape),
            scratch_shapes=scratch,
            compiler_params=PARAMS,
            cost_estimate=cost(micros),
            name=name,
        )(*inputs)

    def shape(*sizes):
        return jax.ShapeDtypeStruct(sizes, F32)

    *pieces, wall = pack(groups, state_in, sponge, wall_nodes, wall_weights, wall_count, mode_shapes)
    pieces = spread(pieces)
    wall, pieces[1] = lax.optimization_barrier((wall, pieces[1]))
    wall = lax.all_to_all(wall, AXES, 0, 0)
    messages = call(
        assemble_kernel,
        "assemble",
        1,
        [shape(4, STATE + DEEP, ROWS, LANES)] * 2 + [shape(4, STATE, ROWS, LANES)] * 2,
        pieces,
    )
    blocks = [exchange(*messages[:2]), exchange(*messages[2:])]
    walls = call(
        functools.partial(forcing_kernel, groups),
        "forcing",
        5.0,
        [shape(4 * DEEP, ROWS, LANES)] * 2,
        [wall],
    )
    field = [pltpu.VMEM((FIELDS, 4 * DEEP, 4 * ROWS, LANES), F32)] * 3
    border = shape(FIELDS, DEEP, 4 * ROWS, LANES)
    piece = shape(2, FIELDS, DEEP, ROWS, LANES)
    quarter = shape(MEMBERS // 2, 2, FIELDS, DEEP, ROWS, LANES)
    constants = (mean_velocity, wall_vector)
    a0, b0, sponge_ext = call(
        functools.partial(first_kernel, groups, 0),
        "first_step_0",
        5.0,
        [border, border, shape(4 * DEEP, 4 * ROWS, LANES)],
        (*constants, walls[0], *blocks[0]),
        field,
        2,
    )
    next_blocks = [exchange(a0, b0)]
    a1, b1, near, far = call(
        functools.partial(first_kernel, groups, 1),
        "first_step_1",
        5.0,
        [border, border, quarter, quarter],
        (*constants, walls[1], *blocks[1], sponge_ext, a0, b0),
        field,
        2,
    )
    next_blocks.append(exchange(a1, b1))
    far, _ = lax.optimization_barrier((far, next_blocks[0]))
    far = lax.ppermute(far, AXES, inside(1))
    merged = call(
        merge_kernel,
        "merge",
        1,
        [shape(2, 2, FIELDS, DEEP, ROWS, LANES)] * 3,
        [near, far],
    )
    first = [lax.ppermute(m, AXES, inside(2 * (MEMBERS // 2 - 1 - e))) for e, m in enumerate(merged)]
    (second_0,) = call(
        functools.partial(second_kernel, groups, 0),
        "second_step_0",
        5.0,
        [shape(FIELDS, 2 * DEEP, 4 * ROWS, LANES)],
        (*constants, walls[0], *next_blocks[0], sponge_ext),
        field,
        2,
    )
    second = call(
        functools.partial(second_kernel, groups, 1),
        "second_step_1",
        5.0,
        [piece] * MEMBERS,
        (*constants, walls[1], *next_blocks[1], sponge_ext, second_0),
        field,
        2,
    )
    second = spread(second[:5]) + list(second[5:])
    second[5:], first = lax.optimization_barrier((second[5:], first))
    second[5:] = spread(second[5:], 5)

    row_count = FIELDS * DEEP * ROWS
    (parts,) = call(
        split_kernel,
        "split",
        2,
        [jax.ShapeDtypeStruct((row_count // CHUNK, 6 * MEMBERS, CHUNK * LANES), jnp.bfloat16)],
        [near, far, *first],
        [pltpu.VMEM((2 * MEMBERS * row_count, LANES), F32)],
    )
    rows_total = float(FIELDS * cells_x * gx_size * cells_y * gy_size * cells_z)
    snap_count = STEPS * 2 * MEMBERS
    state_out, grams = pl.pallas_call(
        gram_kernel,
        out_shape=[
            jax.ShapeDtypeStruct(state_in.shape, F32),
            jax.ShapeDtypeStruct((devices, ROWS, LANES), F32),
        ],
        in_specs=[VMEM] * (1 + MEMBERS),
        out_specs=[VMEM, VMEM],
        scratch_shapes=[pltpu.VMEM((2 * MEMBERS * row_count, LANES), F32)],
        compiler_params=PARAMS,
        name="gram",
    )(parts, *second)
    grams = lax.all_to_all(grams, AXES, 0, 0)
    factor = pl.pallas_call(
        functools.partial(factor_kernel, rows_total),
        out_shape=jax.ShapeDtypeStruct((snap_count, snap_count), F32),
        in_specs=[VMEM],
        out_specs=VMEM,
        compiler_params=PARAMS,
        name="factor",
    )(grams)
    return state_out, factor


def solution(mesh):
    placed = (
        P(None, None, "gx", "gy", None),
        P("gx", "gy", None),
        P(),
        P(),
        P(None, ("gx", "gy")),
        P(None, "gx", None),
        P(None, "gx", None),
        P("gx"),
    )
    return jax.shard_map(
        local,
        mesh=mesh,
        in_specs=placed,
        out_specs=(P(None, None, "gx", "gy", None), P()),
        check_vma=False,
    )
```
